32 devices in a mesh: gx: 8 (over z, y), gy: 4 (over x, core).
Axes of the slice: x: 2, y: 2, z: 4, core: 2. Of those that a mesh axis runs over, the one named last changes fastest.
Arguments:
- positions: float32 [3, 131072], P(None, ('gx', 'gy')), may hold values from 0 to 128, as said below
- mass: float32 [131072], P(('gx', 'gy')), may hold values from 0.5 to 2
- smoothing: float32 [131072], P(('gx', 'gy')), may hold values from 1.5 to 3
- energy: float32 [131072], P(('gx', 'gy')), may hold values from 0.5 to 4
- destination: int32 [131072, 1], P(('gx', 'gy')), may hold values from 0 to 31, as said below
- pairs: int32 [2, 27648], P(None, ('gx', 'gy')), may hold values from 0 to 63, as said below
- pair_count: int32 [32], P(('gx', 'gy')), may hold values from 432 to 864, as said below
Outputs:
- density: float32 [131072], P(('gx', 'gy'))
- accel: float32 [3, 131072], P(None, ('gx', 'gy'))
The draws below stay inside these ranges and needn't reach their ends.
Inputs may be any that keep to these rules, and one draw needn't show every extreme that they name: `destination`: the 4096 particles of every domain name each domain exactly 128 times. `positions`: each particle lies in the box of its new domain (i, j): first coordinate in [16 i, 16 (i + 1)], second in [16 j, 16 (j + 1)], third in [0, 16]. `pairs`: row 0 holds target tiles below 32, row 1 source tiles below 32 + 4 * 8 (tiles from 32 on are ghost tiles); domain d's list is columns d * 864 to (d + 1) * 864 - 1, and slots from pair_count[d] on are unused. `pair_count`: some domain uses all 864 slots.
All inputs are finite; a program needn't handle non-finite values.
Results may differ from the reference program's by a relative error of at most 0.0005.
Values sent between devices are 32-bit elements; how exact they have to be, the bound alone decides.
A program may use at most 64 MiB of HBM per device.

```python
import math
import jax
import jax.numpy as jnp
from jax import lax

P_DEV = 4096
TILE = 128
GT = 8
BOX = 16
NPART = 131072
CAP = 128
NT = 32
MAXP = 864
DEPTH = 16
N_GX = 8
N_GY = 4
DEVICES = 32


def route_plan(key):
    keys = jax.random.split(jax.random.fold_in(key, 31), DEVICES)
    base = jnp.repeat(jnp.arange(DEVICES, dtype=jnp.int32), CAP)
    return jax.vmap(lambda one: jax.random.permutation(one, base))(keys).astype(jnp.int32)


def draw_destination(key, part):
    return route_plan(key).reshape(-1, 1)


def draw_positions(key, part):
    plan = route_plan(key)
    order = jnp.argsort(plan, axis=1, stable=True).astype(jnp.int32)
    placed = jnp.argsort(order, axis=1, stable=True).astype(jnp.int32)
    source = jnp.arange(DEVICES, dtype=jnp.int32)[:, None]
    column = source * CAP + placed - plan * CAP
    edge = column < GT * TILE
    first = (plan // N_GY).astype(jnp.float32)
    second = (plan % N_GY).astype(jnp.float32)
    spread = jax.random.uniform(jax.random.fold_in(key, 41), (3, DEVICES, P_DEV), jnp.float32)
    coord_x = (first + spread[0]) * BOX
    coord_y = (second + spread[1]) * BOX
    coord_z = spread[2] * DEPTH
    face = jax.random.randint(jax.random.fold_in(key, 42), (DEVICES, P_DEV), 0, 4)
    near = jax.random.uniform(jax.random.fold_in(key, 43), (DEVICES, P_DEV), jnp.float32) * 3.0
    coord_x = jnp.where(edge & (face == 0), first * BOX + near, coord_x)
    coord_x = jnp.where(edge & (face == 1), (first + 1.0) * BOX - near, coord_x)
    coord_y = jnp.where(edge & (face == 2), second * BOX + near, coord_y)
    coord_y = jnp.where(edge & (face == 3), (second + 1.0) * BOX - near, coord_y)
    return jnp.stack([coord_x, coord_y, coord_z]).reshape(3, -1).astype(jnp.float32)


def draw_pairs(key, part):
    total = DEVICES * MAXP
    target = jax.random.randint(jax.random.fold_in(key, 11), (total,), 0, NT)
    source = jax.random.randint(jax.random.fold_in(key, 12), (total,), 0, NT + 4 * GT)
    return jnp.stack([target, source]).astype(jnp.int32)


def draw_pair_count(key, part):
    counts = jax.random.randint(jax.random.fold_in(key, 21), (DEVICES,), MAXP // 2, MAXP + 1)
    fullest = jax.random.randint(jax.random.fold_in(key, 22), (), 0, DEVICES)
    return jnp.where(jnp.arange(DEVICES) == fullest, MAXP, counts).astype(jnp.int32)


def shard_levels(own_key, shape, pieces, low, top_value):
    factor_of = 1.0
    for position, blocks in pieces:
        steps = jax.random.uniform(jax.random.fold_in(jax.random.fold_in(own_key, 6), position), (blocks,), jnp.float32, low / len(pieces), top_value / len(pieces))
        factor_of = factor_of * jnp.repeat(jnp.exp(steps), shape[position] // blocks).reshape((-1,) + (1,) * (len(shape) - 1 - position))
    return factor_of


def setup_inputs(seed: int = 0) -> dict:
    streams_of = jax.random.split(jax.random.key(seed), 8)
    positions = draw_positions(jax.random.fold_in(streams_of[7], 71), 0)
    mass = jnp.clip(jnp.exp(math.log(2.0) - 1.3862944 * jax.random.uniform(streams_of[1], (NPART,), jnp.float32) ** shard_levels(streams_of[1], (NPART,), ((0, 32),), -0.2, 0.2)), 0.5, 2.0)
    smoothing = jnp.clip(1.5 + 1.5 * jax.random.uniform(streams_of[2], (NPART,), jnp.float32) ** shard_levels(streams_of[2], (NPART,), ((0, 32),), -0.2, 0.2), 1.5, 3.0)
    energy = jnp.clip(jnp.exp(math.log(4.0) - 2.0794415 * jax.random.uniform(streams_of[3], (NPART,), jnp.float32) ** shard_levels(streams_of[3], (NPART,), ((0, 32),), -0.2, 0.2)), 0.5, 4.0)
    destination = draw_destination(jax.random.fold_in(streams_of[7], 71), 0)
    pairs = draw_pairs(jax.random.fold_in(streams_of[7], 71), 0)
    pair_count = draw_pair_count(jax.random.fold_in(streams_of[7], 71), 0)
    return {"positions": positions, "mass": mass, "smoothing": smoothing, "energy": energy, "destination": destination, "pairs": pairs, "pair_count": pair_count}


KERNEL_NORM = 21.0 / (2.0 * math.pi)
GAMMA_LESS = 2.0 / 3.0

def neighbour_rows(boundary):
    padded = jnp.pad(boundary, ((0, 0), (1, 1), (1, 1), (0, 0)))
    return jnp.concatenate([padded[:, :-2, 1:-1], padded[:, 2:, 1:-1], padded[:, 1:-1, :-2], padded[:, 1:-1, 2:]], axis=3)

def density_domain(pool, pair_list, count, own_tiles):
    slots = pair_list.shape[1]
    group_size = slots // own_tiles
    tile_rows = pool.shape[2]

    def advance(totals, block):
        start = block * group_size
        target = lax.dynamic_slice_in_dim(pair_list[0], start, group_size)
        source = lax.dynamic_slice_in_dim(pair_list[1], start, group_size)
        active = start + jnp.arange(group_size, dtype=jnp.int32) < count
        nearer = pool[target]
        farther = pool[source]
        dist_sq = jnp.zeros((group_size, tile_rows, tile_rows), jnp.float32)
        for component in range(3):
            offset = nearer[:, component, :, None] - farther[:, component, None, :]
            dist_sq = dist_sq + offset * offset
        radius = nearer[:, 4, :, None]
        ratio = jnp.sqrt(dist_sq) / radius
        falloff = jnp.maximum(1.0 - ratio, 0.0)
        kernel = KERNEL_NORM / (radius * radius * radius) * falloff ** 4 * (1.0 + 4.0 * ratio)
        summed = lax.optimization_barrier(jnp.sum(kernel * farther[:, 3, None, :], axis=2))
        summed = jnp.where(active[:, None], summed, 0.0)
        return (totals.at[target].add(summed), None)
    start_totals = jnp.zeros((own_tiles, tile_rows), jnp.float32)
    totals, unused = lax.scan(advance, start_totals, jnp.arange(slots // group_size, dtype=jnp.int32))
    own = pool[:own_tiles]
    radius = own[:, 4, :]
    self_term = own[:, 3, :] * KERNEL_NORM / (radius * radius * radius)
    return (totals + self_term).reshape(-1)

def accel_domain(pool, press_pool, pair_list, count, own_tiles):
    slots = pair_list.shape[1]
    group_size = slots // own_tiles
    tile_rows = pool.shape[2]

    def advance(totals, block):
        start = block * group_size
        target = lax.dynamic_slice_in_dim(pair_list[0], start, group_size)
        source = lax.dynamic_slice_in_dim(pair_list[1], start, group_size)
        active = start + jnp.arange(group_size, dtype=jnp.int32) < count
        nearer = pool[target]
        farther = pool[source]
        press_own = press_pool[target]
        press_far = press_pool[source]
        dist_sq = jnp.zeros((group_size, tile_rows, tile_rows), jnp.float32)
        for component in range(3):
            offset = nearer[:, component, :, None] - farther[:, component, None, :]
            dist_sq = dist_sq + offset * offset
        mean_radius = 0.5 * (nearer[:, 4, :, None] + farther[:, 4, None, :])
        ratio = jnp.sqrt(dist_sq) / mean_radius
        falloff = jnp.maximum(1.0 - ratio, 0.0)
        slope = -20.0 * KERNEL_NORM * falloff ** 3 / mean_radius ** 5
        coupling = farther[:, 3, None, :] * (press_own[:, :, None] + press_far[:, None, :]) * slope
        summed = lax.optimization_barrier(jnp.sum(coupling, axis=2))
        parts_list = []
        for component in range(3):
            pulled = lax.optimization_barrier(jnp.sum(coupling * farther[:, component, None, :], axis=2))
            parts_list.append(-(nearer[:, component, :] * summed - pulled))
        result = jnp.stack(parts_list, axis=1)
        result = jnp.where(active[:, None, None], result, 0.0)
        return (totals.at[target].add(result), None)
    start_totals = jnp.zeros((own_tiles, 3, tile_rows), jnp.float32)
    totals, unused = lax.scan(advance, start_totals, jnp.arange(slots // group_size, dtype=jnp.int32))
    return jnp.transpose(totals, (1, 0, 2)).reshape(3, -1)

def reference(positions, mass, smoothing, energy, destination, pairs, pair_count):
    domains = N_GX * N_GY
    edge_rows = GT * TILE
    fields = jnp.concatenate([positions, mass[None], smoothing[None], energy[None]], 0).reshape(6, domains, P_DEV)
    ranking = jnp.argsort(destination[:, 0].reshape(domains, P_DEV), axis=1, stable=True).astype(jnp.int32)
    outgoing = jnp.take_along_axis(fields, ranking[None], axis=2).reshape(6, domains, domains, CAP)
    settled = jnp.transpose(outgoing, (0, 2, 1, 3)).reshape(6, domains, P_DEV)
    boundary = settled[:, :, :edge_rows].reshape(6, N_GX, N_GY, edge_rows)
    extra = neighbour_rows(boundary).reshape(6, domains, 4 * edge_rows)
    pool = jnp.concatenate([settled, extra], 2).reshape(6, domains, NT + 4 * GT, TILE)
    pool = jnp.transpose(pool, (1, 2, 0, 3))
    pair_lists = jnp.transpose(pairs.reshape(2, domains, MAXP), (1, 0, 2))
    density = lax.map(lambda items: density_domain(items[0], items[1], items[2], NT), (pool, pair_lists, pair_count))
    press = GAMMA_LESS * settled[5] / density
    press_edge = press[:, :edge_rows].reshape(1, N_GX, N_GY, edge_rows)
    press_extra = neighbour_rows(press_edge).reshape(domains, 4 * edge_rows)
    press_pool = jnp.concatenate([press, press_extra], 1).reshape(domains, NT + 4 * GT, TILE)
    accel = lax.map(lambda items: accel_domain(items[0], items[1], items[2], items[3], NT), (pool, press_pool, pair_lists, pair_count))
    accel = jnp.transpose(accel, (1, 0, 2)).reshape(3, -1)
    return (density.reshape(-1), accel)
```

```python
import functools
import math

import jax
import jax.numpy as jnp
from jax import lax
from jax.experimental import pallas as pl
from jax.experimental.pallas import tpu as pltpu
from jax.sharding import PartitionSpec as P

GT = 8
LANES = 128
FEATS = 32
TINY = 1e-12

KERNEL_NORM = 21.0 / (2.0 * math.pi)
GAMMA_LESS = 2.0 / 3.0


def extended(block, sides, width):
    for axis, dim in sides:
        count = lax.axis_size(axis)
        forward = [(i, i + 1) for i in range(count - 1)]
        backward = [(target, source) for source, target in forward]
        low = lax.ppermute(
            lax.slice_in_dim(block, block.shape[dim] - width, None, axis=dim), axis, forward
        )
        high = lax.ppermute(lax.slice_in_dim(block, 0, width, axis=dim), axis, backward)
        block = jnp.concatenate([low, block, high], axis=dim)
    return block


def neighbour_rows(ghosts):
    return jnp.concatenate(
        [ghosts[..., 0, 1, :], ghosts[..., 2, 1, :], ghosts[..., 1, 0, :], ghosts[..., 1, 2, :]],
        axis=-1,
    )


def three(x):
    one = x.astype(jnp.bfloat16).astype(jnp.float32)
    rest = x - one
    two = rest.astype(jnp.bfloat16).astype(jnp.float32)
    return one, two, (rest - two).astype(jnp.bfloat16).astype(jnp.float32)


def source_terms(x):
    one, two, low = three(x)
    return [one, two, one, two, low, one]


def target_terms(x):
    one, two, low = three(x)
    return [one, one, two, two, one, low]


def put_rows(stage, rows, width, tiles):
    for k, row in enumerate(rows):
        stage[pl.ds(k, tiles, stride=width), :] = row


def plan_kernel(count_ref, pairs_ref, sizes_ref, own_ref, ghost_ref, times_ref, own_tiles, tiles):
    step = 16

    def clear(block, carry):
        for u in range(step):
            times_ref[block * step + u] = 0
        return carry

    lax.fori_loop(0, times_ref.shape[0] // step, clear, 0)

    count = count_ref[0]
    spare = own_tiles * tiles
    last = pairs_ref.shape[1] - 1
    ahead = 8

    def add(block, carry):
        own, ghost = carry
        picked = []
        for u in range(ahead):
            k = block * ahead + u
            live = k < count
            at = jnp.minimum(k, last)
            source = jnp.where(live, pairs_ref[1, at], 0)
            key = jnp.where(live, pairs_ref[0, at] * tiles + source, spare)
            near = (source < own_tiles).astype(jnp.int32)
            alive = live.astype(jnp.int32)
            picked.append((key, near * alive, (1 - near) * alive))
        for key, near, beyond in picked:
            seen = times_ref[key]
            times_ref[key] = seen + 1
            own_ref[own] = key
            ghost_ref[ghost] = key
            fresh = (seen == 0).astype(jnp.int32)
            own = own + fresh * near
            ghost = ghost + fresh * beyond
        return own, ghost

    own, ghost = lax.fori_loop(0, (count + ahead - 1) // ahead, add, (0, 0))
    sizes_ref[0] = own
    sizes_ref[1] = ghost


def one_hot_rows(dest):
    rows = lax.broadcasted_iota(jnp.int32, (LANES, LANES), 0)
    wide = jnp.broadcast_to(dest, (LANES, LANES))
    return jnp.where(wide == rows, 1.0, 0.0).astype(jnp.bfloat16)


def by_last(a, b):
    return lax.dot_general(a, b, (((1,), (1,)), ((), ())), preferred_element_type=jnp.float32)


def sweep(list_ref, size, times_ref, tiles, dump, unroll, body):
    last = list_ref.shape[0] - 1

    def advance(block, carry):
        for u in range(unroll):
            k = block * unroll + u
            live = k < size
            key = jnp.where(live, list_ref[jnp.minimum(k, last)], 0)
            target = key // tiles
            source = key - target * tiles
            weight = times_ref[key].astype(jnp.float32)
            body(target, source, jnp.where(live, target, dump), weight)
        return carry

    lax.fori_loop(0, (size + unroll - 1) // unroll, advance, 0)


def sweep_two(list_ref, size, times_ref, tiles, dump, unroll, body):
    last = list_ref.shape[0] - 1

    def advance(block, carry):
        for u in range(0, unroll, 2):
            both = []
            for v in range(2):
                k = block * unroll + u + v
                live = k < size
                key = jnp.where(live, list_ref[jnp.minimum(k, last)], 0)
                target = key // tiles
                source = key - target * tiles
                weight = times_ref[key].astype(jnp.float32)
                both.append((target, source, jnp.where(live, target, dump), weight))
            body(both)
        return carry

    lax.fori_loop(0, (size + unroll - 1) // unroll, advance, 0)


def recip(x):
    return pl.reciprocal(x, approx=True)


def keep_rows(stage, near, tiles):
    group = 4

    def keep(block, carry):
        for u in range(group):
            t = block * group + u
            near[t] = stage[pl.ds(t * FEATS, FEATS), :].astype(jnp.bfloat16)
        return carry

    lax.fori_loop(0, tiles // group, keep, 0)


def target_rows(coords, scale, stage, near, tiles):
    norm = sum(c * c for c in coords)
    zero = jnp.zeros_like(norm)
    rows = []
    for c in coords:
        rows += target_terms(-2.0 * c * scale)
    rows += target_terms(scale)
    rows += list(three(norm * scale))
    rows += [zero] * (FEATS - len(rows))
    put_rows(stage, rows, FEATS, tiles)
    keep_rows(stage, near, tiles)


def spread_column(far, first, last, wide):
    row = lax.broadcasted_iota(jnp.int32, (FEATS, LANES), 0)
    pick = jnp.where((row >= first) & (row < last), 1.0, 0.0).astype(jnp.bfloat16)
    group = 4

    def one(block, carry):
        for u in range(group):
            t = block * group + u
            wide[t] = jnp.dot(far[t], pick, preferred_element_type=jnp.float32)
        return carry

    lax.fori_loop(0, wide.shape[0] // group, one, 0)


def density_kernel(sizes_ref, own_ref, ghost_ref, times_ref, pool_ref,
                   dens_ref, press_ref, far, packed_ref, dest_ref, more_ref,
                   stage, near, mass_b, totals):
    own_tiles = dens_ref.shape[0]
    tiles = pool_ref.shape[1]
    ghosts = tiles - own_tiles
    own, out_of_reach = [], 0.0
    ghost = []
    reach = jnp.max(pool_ref[4]) + 0.01
    for k in range(3):
        x = pool_ref[k, :own_tiles]
        low, high = jnp.min(x), jnp.max(x)
        centre = 0.5 * (low + high)
        far_x = pool_ref[k, own_tiles:]
        gap = jnp.maximum(jnp.maximum(low - far_x, far_x - high), 0.0)
        out_of_reach = out_of_reach + gap * gap
        own.append(x - centre)
        ghost.append(far_x - centre)
    ghost_mass = pool_ref[3, own_tiles:]
    active = (out_of_reach < reach * reach) & (ghost_mass != 0.0)
    upto = lax.broadcasted_iota(jnp.int32, (LANES, LANES), 0) <= lax.broadcasted_iota(
        jnp.int32, (LANES, LANES), 1)
    upto = jnp.where(upto, 1.0, 0.0).astype(jnp.bfloat16)
    flags = jnp.where(active, 1.0, 0.0).astype(jnp.bfloat16)
    rank = jnp.dot(flags, upto, preferred_element_type=jnp.float32)
    dest = jnp.where(active, rank - 1.0, -1.0).astype(jnp.int32)
    dest_ref[...] = dest
    most = jnp.max(rank)
    more = (most > LANES // 2 + 0.5).astype(jnp.int32)
    more_ref[0] = more
    split = [three(x) for x in ghost + [ghost_mass, pool_ref[4, own_tiles:]]]
    zero = jnp.zeros_like(ghost_mass)
    rows = []
    for term in range(3):
        rows += [s[term] for s in split] + [zero] * 3
    put_rows(stage, rows + [zero] * 8, FEATS, ghosts)

    def squeeze(block, carry):
        for u in range(4):
            g = block * 4 + u
            part = stage[pl.ds(g * FEATS, FEATS), :].astype(jnp.bfloat16)
            moved = by_last(part, one_hot_rows(dest_ref[pl.ds(g, 1), :]))
            totals[g] = moved[:8] + moved[8:16] + moved[16:24]
        return carry

    lax.fori_loop(0, ghosts // 4, squeeze, 0)
    fields = []
    for k, x in enumerate(own + [pool_ref[3, :own_tiles], pool_ref[4, :own_tiles]]):
        packed_ref[k, :own_tiles] = x
        packed_ref[k, own_tiles:] = totals[:ghosts, k, :]
        fields.append(packed_ref[k])
    norm = sum(c * c for c in fields[:3])
    ones = jnp.ones_like(norm)
    rows = []
    for c in fields[:3] + [norm]:
        rows += source_terms(c)
    rows += [ones, ones, ones] + list(three(0.5 * fields[4])) + list(three(fields[3])[:2])
    put_rows(stage, rows, FEATS, tiles)

    def turn(g, carry):
        for v in range(2):
            at = g * 2 + v
            cols = jnp.transpose(stage[pl.ds(at * LANES, LANES), :]).astype(jnp.bfloat16)
            for u in range(LANES // FEATS):
                far[at * (LANES // FEATS) + u] = cols[:, u * FEATS:(u + 1) * FEATS]
        return carry

    lax.fori_loop(0, tiles * FEATS // LANES // 2, turn, 0)
    radius = fields[4][:own_tiles]
    target_rows(own, 1.0 / (radius * radius), stage, near, own_tiles)
    spread_column(far, 30, 32, mass_b)
    totals[...] = jnp.zeros_like(totals)

    def add(first, height):
        def body(target, source, place, weight):
            sq = jnp.dot(far[source, first:first + height], near[target],
                         preferred_element_type=jnp.float32)
            sq = jnp.maximum(sq, TINY)
            ratio = sq * lax.rsqrt(sq)
            falloff = jnp.maximum(1.0 - ratio, 0.0)
            falloff = falloff * falloff
            term = falloff * falloff * ((ratio + 0.25) * mass_b[source, first:first + height])
            totals[place] += weight * jnp.sum(term.reshape(height // 8, 8, LANES), axis=0)
        return body

    half = LANES // 2
    sweep(own_ref, sizes_ref[0], times_ref, tiles, own_tiles, 16, add(0, LANES))
    sweep(ghost_ref, sizes_ref[1], times_ref, tiles, own_tiles, 32, add(0, half))

    @pl.when(more > 0)
    def _():
        sweep(ghost_ref, sizes_ref[1], times_ref, tiles, own_tiles, 4, add(half, half))

    summed = jnp.sum(totals[:own_tiles], axis=1)
    norm = KERNEL_NORM / (radius * radius * radius)
    density = norm * (4.0 * summed + pool_ref[3, :own_tiles])
    dens_ref[...] = density
    press_ref[...] = GAMMA_LESS * pool_ref[5, :own_tiles] / density


def accel_kernel(sizes_ref, own_ref, ghost_ref, times_ref, more_ref, far, packed_ref, dest_ref,
                 press_ref, press_far_ref, out_ref, stage, near, half_a, half_b, press_all, left, left_half,
                 totals):
    own_tiles = out_ref.shape[1]
    tiles = packed_ref.shape[1]
    ghosts = tiles - own_tiles
    half = LANES // 2
    zero = jnp.zeros((ghosts, LANES), jnp.float32)
    put_rows(stage, list(three(press_far_ref[...])) + [zero] * 13, 16, ghosts)

    def squeeze(block, carry):
        for u in range(4):
            g = block * 4 + u
            part = stage[pl.ds(g * 16, 16), :].astype(jnp.bfloat16)
            moved = by_last(part, one_hot_rows(dest_ref[pl.ds(g, 1), :]))
            press_all[pl.ds(own_tiles + g, 1), :] = moved[0:1] + moved[1:2] + moved[2:3]
        return carry

    lax.fori_loop(0, ghosts // 4, squeeze, 0)
    press_all[:own_tiles] = press_ref[...]
    own = [packed_ref[k, :own_tiles] for k in range(3)]
    target_rows(own, jnp.ones_like(own[0]), stage, near, own_tiles)
    spread_column(far, 27, 30, half_b)
    half_a[...] = 0.5 * packed_ref[4, :own_tiles]
    mass = packed_ref[3]
    load = mass * press_all[...]
    coords = [packed_ref[k] for k in range(3)]
    rows = [mass] + [mass * c for c in coords] + [load] + [load * c for c in coords]
    split = [three(row) for row in rows]
    put_rows(stage, [s[0] for s in split] + [s[1] for s in split], 16, tiles)

    def pack(block, carry):
        for u in range(4):
            t = block * 4 + u
            part = stage[pl.ds(t * 16, 16), :].astype(jnp.bfloat16)
            left[t] = jnp.concatenate([part, part], axis=1)
        return carry

    def pack_half(block, carry):
        for u in range(4):
            t = block * 4 + u
            part = stage[pl.ds((t + own_tiles) * 16, 16), :].astype(jnp.bfloat16)
            for v in range(2):
                piece = part[:, v * half:(v + 1) * half]
                two = jnp.concatenate([piece, piece], axis=1)
                none = jnp.zeros_like(two)
                left_half[v, 0, t] = jnp.concatenate([two, none], axis=1)
                left_half[v, 1, t] = jnp.concatenate([none, two], axis=1)
        return carry

    lax.fori_loop(0, own_tiles // 4, pack, 0)
    lax.fori_loop(0, ghosts // 4, pack_half, 0)
    totals[...] = jnp.zeros_like(totals)

    def slopes(source, target, first, height):
        sq = jnp.dot(far[source, first:first + height], near[target],
                     preferred_element_type=jnp.float32)
        sq = jnp.maximum(sq, TINY)
        radius = half_b[source, first:first + height] + half_a[pl.ds(target, 1), :]
        dist = sq * lax.rsqrt(sq)
        inv = recip(radius)
        wide = inv * inv
        fall = jnp.maximum(inv - dist * wide, 0.0)
        slope = fall * fall * (fall * wide)
        high = slope.astype(jnp.bfloat16)
        low = (slope - high.astype(jnp.float32)).astype(jnp.bfloat16)
        return [high, low]

    def add_one(target, source, place, weight):
        terms = jnp.concatenate(slopes(source, target, 0, LANES), axis=0)
        totals[place] += weight * jnp.dot(left[source], terms, preferred_element_type=jnp.float32)

    def add_two(v):
        def body(both):
            terms, lhs = [], []
            for side, (target, source, place, weight) in enumerate(both):
                terms += slopes(source, target, v * half, half)
                lhs.append(left_half[v, side, jnp.maximum(source - own_tiles, 0)])
            moved = jnp.dot(jnp.concatenate(lhs, axis=0), jnp.concatenate(terms, axis=0),
                            preferred_element_type=jnp.float32)
            for side, (target, source, place, weight) in enumerate(both):
                totals[place] += weight * moved[side * 16:(side + 1) * 16]
        return body

    sweep(own_ref, sizes_ref[0], times_ref, tiles, own_tiles, 16, add_one)
    sweep_two(ghost_ref, sizes_ref[1], times_ref, tiles, own_tiles, 32, add_two(0))

    @pl.when(more_ref[0] > 0)
    def _():
        sweep_two(ghost_ref, sizes_ref[1], times_ref, tiles, own_tiles, 4, add_two(1))

    folded = totals[:own_tiles, :8] + totals[:own_tiles, 8:]
    mixed = [press_ref[...] * folded[:, k] + folded[:, k + 4] for k in range(4)]
    for k in range(3):
        out_ref[k] = 20.0 * KERNEL_NORM * (own[k] * mixed[0] - mixed[k + 1])


SMEM = pl.BlockSpec(memory_space=pltpu.SMEM)
VMEM = pl.BlockSpec(memory_space=pltpu.VMEM)


def plan_call(count, pairs, own_tiles, tiles):
    slots = pairs.shape[1]
    shapes = [(2,), (slots + 1,), (slots + 1,), (own_tiles * tiles + LANES,)]
    return pl.pallas_call(
        functools.partial(plan_kernel, own_tiles=own_tiles, tiles=tiles),
        out_shape=[jax.ShapeDtypeStruct(shape, jnp.int32) for shape in shapes],
        in_specs=[SMEM, SMEM],
        out_specs=[SMEM] * 4,
        cost_estimate=pl.CostEstimate(flops=10 ** 7, bytes_accessed=10 ** 7, transcendentals=0),
        name="plan",
    )(count, pairs)


def density_call(plan, pool, own_tiles):
    tiles = pool.shape[1]
    flat = jax.ShapeDtypeStruct((own_tiles, LANES), jnp.float32)
    return pl.pallas_call(
        density_kernel,
        out_shape=(
            flat,
            flat,
            jax.ShapeDtypeStruct((tiles, LANES, FEATS), jnp.bfloat16),
            jax.ShapeDtypeStruct((5, tiles, LANES), jnp.float32),
            jax.ShapeDtypeStruct((tiles - own_tiles, LANES), jnp.int32),
            jax.ShapeDtypeStruct((1,), jnp.int32),
        ),
        in_specs=[SMEM] * 4 + [VMEM],
        out_specs=(VMEM, VMEM, VMEM, VMEM, VMEM, SMEM),
        scratch_shapes=[
            pltpu.VMEM((tiles * FEATS, LANES), jnp.float32),
            pltpu.VMEM((own_tiles, FEATS, LANES), jnp.bfloat16),
            pltpu.VMEM((tiles, LANES, LANES), jnp.float32),
            pltpu.VMEM((max(own_tiles, tiles - own_tiles) + 1, 8, LANES), jnp.float32),
        ],
        name="density",
    )(*plan, pool)


def accel_call(plan, more, far, packed, dest, press, press_far):
    own_tiles = press.shape[0]
    tiles = packed.shape[1]
    return pl.pallas_call(
        accel_kernel,
        out_shape=jax.ShapeDtypeStruct((3, own_tiles, LANES), jnp.float32),
        in_specs=[SMEM] * 5 + [VMEM] * 5,
        out_specs=VMEM,
        scratch_shapes=[
            pltpu.VMEM((tiles * FEATS, LANES), jnp.float32),
            pltpu.VMEM((own_tiles, FEATS, LANES), jnp.bfloat16),
            pltpu.VMEM((own_tiles, LANES), jnp.float32),
            pltpu.VMEM((tiles, LANES, LANES), jnp.float32),
            pltpu.VMEM((tiles, LANES), jnp.float32),
            pltpu.VMEM((own_tiles, 16, 2 * LANES), jnp.bfloat16),
            pltpu.VMEM((2, 2, tiles - own_tiles, 16, 2 * LANES), jnp.bfloat16),
            pltpu.VMEM((own_tiles + 1, 16, LANES), jnp.float32),
        ],
        name="accel",
    )(*plan, more, far, packed, dest, press, press_far)


def local(positions, mass, smoothing, energy, destination, pairs, pair_count):
    across = lax.axis_size("gx")
    beside = lax.axis_size("gy")
    domains = across * beside
    dev_rows = mass.shape[0]
    slot_count = dev_rows // domains
    own_tiles = dev_rows // LANES
    edge_rows = GT * LANES
    plan = plan_call(pair_count, pairs, own_tiles, own_tiles + 4 * GT)
    fields = jnp.concatenate([positions, mass[None], smoothing[None], energy[None]], 0)
    ordered = lax.sort(
        (destination[:, 0],) + tuple(fields[k] for k in range(6)), num_keys=1, is_stable=True
    )
    outgoing = jnp.stack([row.reshape(domains, slot_count) for row in ordered[1:]], 1)
    outgoing = outgoing.reshape(across, beside, 6 * slot_count)
    halfway = lax.all_to_all(outgoing, "gy", split_axis=1, concat_axis=1, tiled=True)
    moved = lax.all_to_all(halfway, "gx", split_axis=0, concat_axis=0, tiled=True)
    settled = jnp.transpose(moved.reshape(domains, 6, slot_count), (1, 0, 2)).reshape(6, dev_rows)
    boundary = settled[:, :edge_rows].reshape(6, 1, 1, edge_rows)
    ghosts = extended(boundary, (("gx", 1), ("gy", 2)), 1)
    extra = neighbour_rows(ghosts)
    pool = jnp.concatenate([settled, extra], 1).reshape(6, own_tiles + 4 * GT, LANES)
    density, press, far, packed, dest, more = density_call(plan, pool, own_tiles)
    press_edge = press.reshape(-1)[:edge_rows].reshape(1, 1, edge_rows)
    press_ghosts = extended(press_edge, (("gx", 0), ("gy", 1)), 1)
    press_far = neighbour_rows(press_ghosts).reshape(4 * GT, LANES)
    accel = accel_call(plan, more, far, packed, dest, press, press_far)
    return (density.reshape(-1), accel.reshape(3, -1))


def solution(mesh):
    placed = (
        P(None, ("gx", "gy")),
        P(("gx", "gy")),
        P(("gx", "gy")),
        P(("gx", "gy")),
        P(("gx", "gy"), None),
        P(None, ("gx", "gy")),
        P(("gx", "gy")),
    )
    return jax.shard_map(
        local,
        mesh=mesh,
        in_specs=placed,
        out_specs=(P(("gx", "gy")), P(None, ("gx", "gy"))),
        check_vma=False,
    )
```

```python
import functools
import math

import jax
import jax.numpy as jnp
from jax import lax
from jax.experimental import pallas as pl
from jax.experimental.pallas import tpu as pltpu
from jax.sharding import PartitionSpec as P

GT = 8
LANES = 128
FEATS = 32
TINY = 1e-12
MESH = pl.DeviceIdType.MESH

KERNEL_NORM = 21.0 / (2.0 * math.pi)
GAMMA_LESS = 2.0 / 3.0


def three(x):
    one = x.astype(jnp.bfloat16).astype(jnp.float32)
    rest = x - one
    two = rest.astype(jnp.bfloat16).astype(jnp.float32)
    return one, two, (rest - two).astype(jnp.bfloat16).astype(jnp.float32)


def source_terms(x):
    one, two, low = three(x)
    return [one, two, one, two, low, one]


def target_terms(x):
    one, two, low = three(x)
    return [one, one, two, two, one, low]


def put_rows(stage, rows, width, tiles):
    for k, row in enumerate(rows):
        stage[pl.ds(k, tiles, stride=width), :] = row


def equal_rows(row, height, base=0):
    at = lax.broadcasted_iota(jnp.int32, (height, row.shape[-1]), 0) + base
    return jnp.broadcast_to(row, at.shape) == at


def ones_where(mask):
    return jnp.where(mask, 1.0, 0.0).astype(jnp.bfloat16)


def earlier(size, width):
    row = lax.broadcasted_iota(jnp.int32, (size, width), 0)
    col = lax.broadcasted_iota(jnp.int32, (size, width), 1)
    return row, col


def route_kernel(pos_ref, mass_ref, smooth_ref, energy_ref, dest_ref, out_ref,
                 flags, prefix, rank_ref, rows_ref, domains):
    tiles = mass_ref.shape[0]
    slots = tiles * LANES // domains
    row, col = earlier(LANES, 2 * LANES)
    before = ones_where((row < col) | (col >= LANES))
    for t in range(tiles):
        flags[t * domains:(t + 1) * domains] = ones_where(
            equal_rows(dest_ref[t:t + 1, :], domains))
    prefix[...] = jnp.dot(flags[...], before, preferred_element_type=jnp.float32)
    seen = jnp.zeros((domains, LANES), jnp.float32)
    for t in range(tiles):
        part = slice(t * domains, (t + 1) * domains)
        mine = flags[part].astype(jnp.float32)
        rank = jnp.sum(mine * (prefix[part, :LANES] + seen), axis=0, keepdims=True)
        rank_ref[t:t + 1, :] = rank.astype(jnp.int32)
        seen = seen + prefix[part, LANES:]
    place = dest_ref[...] * slots + rank_ref[...]
    block = place // LANES
    rank_ref[...] = place - block * LANES
    lane = lax.broadcasted_iota(jnp.int32, (tiles, LANES), 1).astype(jnp.float32)
    from_lane = jnp.zeros((tiles, LANES), jnp.float32)
    from_tile = jnp.zeros((tiles, LANES), jnp.float32)
    for t in range(tiles):
        picked = equal_rows(block[t:t + 1, :], tiles)
        both = jnp.concatenate([jnp.where(picked, lane, 0.0), jnp.where(picked, 1.0, 0.0)], axis=0)
        found = by_last(both.astype(jnp.bfloat16),
                        ones_where(equal_rows(rank_ref[t:t + 1, :], LANES)))
        from_lane = from_lane + found[:tiles]
        from_tile = from_tile + float(t) * found[tiles:]
    fields = [pos_ref[0], pos_ref[1], pos_ref[2], mass_ref[...], smooth_ref[...], energy_ref[...]]
    put_rows(rows_ref, fields + [jnp.zeros_like(lane)] * 2, 8, tiles)
    from_lane = from_lane.astype(jnp.int32)
    from_tile = from_tile.astype(jnp.int32)
    for q in range(tiles):
        at = jnp.broadcast_to(from_lane[q:q + 1, :], (8, LANES))
        tile = jnp.broadcast_to(from_tile[q:q + 1, :], (8, LANES))
        out = jnp.zeros((8, LANES), jnp.float32)
        for t in range(tiles):
            moved = jnp.take_along_axis(rows_ref[t * 8:(t + 1) * 8, :], at, axis=1)
            out = jnp.where(tile == t, moved, out)
        out_ref[q] = out


def beside(i, j, rows, cols):
    return [(i > 0, (i - 1, j), 1), (i < rows - 1, (i + 1, j), 0),
            (j > 0, (i, j - 1), 3), (j < cols - 1, (i, j + 1), 2)]


def exchange_kernel(out_ref, own_ref, ghost_ref, near_sem, send_sem, recv_sem, edge_send, edge_recv,
                    rows, cols):
    domains = rows * cols
    edge = ghost_ref.shape[1]
    i, j = lax.axis_index("gx"), lax.axis_index("gy")
    me = i * cols + j
    barrier = pltpu.get_barrier_semaphore()

    def greet(k, carry):
        peer = lax.rem(me + k, domains)
        pl.semaphore_signal(barrier, inc=1, device_id=(peer // cols, lax.rem(peer, cols)),
                            device_id_type=MESH)
        return carry

    lax.fori_loop(1, domains, greet, 0)
    stay = pltpu.make_async_copy(out_ref.at[me], own_ref.at[me], near_sem)
    stay.start()
    pl.semaphore_wait(barrier, domains - 1)

    def outgoing(peer):
        return pltpu.make_async_remote_copy(
            src_ref=out_ref.at[peer], dst_ref=own_ref.at[me],
            send_sem=send_sem.at[peer], recv_sem=recv_sem.at[me],
            device_id=(peer // cols, lax.rem(peer, cols)), device_id_type=MESH)

    def incoming(source):
        return pltpu.make_async_remote_copy(
            src_ref=out_ref.at[source], dst_ref=own_ref.at[source],
            send_sem=send_sem.at[source], recv_sem=recv_sem.at[source],
            device_id=(source // cols, lax.rem(source, cols)), device_id_type=MESH)

    def send(k, carry):
        outgoing(lax.rem(me + k, domains)).start()
        return carry

    lax.fori_loop(1, domains, send, 0)
    stay.wait()

    def arrive(source, carry):
        @pl.when(source != me)
        def _():
            incoming(source).wait_recv()
        return carry

    lax.fori_loop(0, edge, arrive, 0)
    sides = beside(i, j, rows, cols)

    def across(side):
        there, peer, slot = sides[side]
        return pltpu.make_async_remote_copy(
            src_ref=own_ref.at[pl.ds(0, edge)], dst_ref=ghost_ref.at[slot],
            send_sem=edge_send.at[side], recv_sem=edge_recv.at[slot],
            device_id=peer, device_id_type=MESH)

    def back(side):
        there, peer, slot = sides[side]
        return pltpu.make_async_remote_copy(
            src_ref=own_ref.at[pl.ds(0, edge)], dst_ref=ghost_ref.at[side],
            send_sem=edge_send.at[side], recv_sem=edge_recv.at[side],
            device_id=peer, device_id_type=MESH)

    for side in range(4):
        @pl.when(sides[side][0])
        def _():
            across(side).start()

        @pl.when(jnp.logical_not(sides[side][0]))
        def _():
            ghost_ref[side] = jnp.zeros_like(ghost_ref[side])

    lax.fori_loop(edge, domains, arrive, 0)

    def left(k, carry):
        outgoing(lax.rem(me + k, domains)).wait_send()
        return carry

    lax.fori_loop(1, domains, left, 0)
    for side in range(4):
        @pl.when(sides[side][0])
        def _():
            across(side).wait_send()
            back(side).wait_recv()


def press_kernel(press_ref, ghost_ref, send_sem, recv_sem, rows, cols):
    i, j = lax.axis_index("gx"), lax.axis_index("gy")
    sides = beside(i, j, rows, cols)
    barrier = pltpu.get_barrier_semaphore()
    for there, peer, slot in sides:
        @pl.when(there)
        def _():
            pl.semaphore_signal(barrier, inc=1, device_id=peer, device_id_type=MESH)

    pl.semaphore_wait(barrier, sum(there.astype(jnp.int32) for there, peer, slot in sides))

    def across(side, slot):
        return pltpu.make_async_remote_copy(
            src_ref=press_ref, dst_ref=ghost_ref.at[slot],
            send_sem=send_sem.at[side], recv_sem=recv_sem.at[slot],
            device_id=sides[side][1], device_id_type=MESH)

    for side in range(4):
        @pl.when(sides[side][0])
        def _():
            across(side, sides[side][2]).start()

        @pl.when(jnp.logical_not(sides[side][0]))
        def _():
            ghost_ref[side] = jnp.zeros_like(ghost_ref[side])

    for side in range(4):
        @pl.when(sides[side][0])
        def _():
            across(side, sides[side][2]).wait_send()
            across(side, side).wait_recv()


def plan_kernel(count_ref, pairs_ref, sizes_ref, own_ref, ghost_ref, times_ref, own_tiles, tiles):
    step = 16

    def clear(block, carry):
        for u in range(step):
            times_ref[block * step + u] = 0
        return carry

    lax.fori_loop(0, times_ref.shape[0] // step, clear, 0)

    count = count_ref[0]
    spare = own_tiles * tiles
    last = pairs_ref.shape[1] - 1
    ahead = 8

    def add(block, carry):
        own, ghost = carry
        picked = []
        for u in range(ahead):
            k = block * ahead + u
            live = k < count
            at = jnp.minimum(k, last)
            source = jnp.where(live, pairs_ref[1, at], 0)
            key = jnp.where(live, pairs_ref[0, at] * tiles + source, spare)
            near = (source < own_tiles).astype(jnp.int32)
            alive = live.astype(jnp.int32)
            picked.append((key, near * alive, (1 - near) * alive))
        for key, near, beyond in picked:
            seen = times_ref[key]
            times_ref[key] = seen + 1
            own_ref[own] = key
            ghost_ref[ghost] = key
            fresh = (seen == 0).astype(jnp.int32)
            own = own + fresh * near
            ghost = ghost + fresh * beyond
        return own, ghost

    own, ghost = lax.fori_loop(0, (count + ahead - 1) // ahead, add, (0, 0))
    sizes_ref[0] = own
    sizes_ref[1] = ghost


def one_hot_rows(dest):
    rows = lax.broadcasted_iota(jnp.int32, (LANES, LANES), 0)
    wide = jnp.broadcast_to(dest, (LANES, LANES))
    return jnp.where(wide == rows, 1.0, 0.0).astype(jnp.bfloat16)


def by_last(a, b):
    return lax.dot_general(a, b, (((1,), (1,)), ((), ())), preferred_element_type=jnp.float32)


def sweep(list_ref, size, times_ref, tiles, dump, unroll, body):
    last = list_ref.shape[0] - 1

    def advance(block, carry):
        for u in range(unroll):
            k = block * unroll + u
            live = k < size
            key = jnp.where(live, list_ref[jnp.minimum(k, last)], 0)
            target = key // tiles
            source = key - target * tiles
            weight = times_ref[key].astype(jnp.float32)
            body(target, source, jnp.where(live, target, dump), weight)
        return carry

    lax.fori_loop(0, (size + unroll - 1) // unroll, advance, 0)


def sweep_two(list_ref, size, times_ref, tiles, dump, unroll, body):
    last = list_ref.shape[0] - 1

    def advance(block, carry):
        for u in range(0, unroll, 2):
            both = []
            for v in range(2):
                k = block * unroll + u + v
                live = k < size
                key = jnp.where(live, list_ref[jnp.minimum(k, last)], 0)
                target = key // tiles
                source = key - target * tiles
                weight = times_ref[key].astype(jnp.float32)
                both.append((target, source, jnp.where(live, target, dump), weight))
            body(both)
        return carry

    lax.fori_loop(0, (size + unroll - 1) // unroll, advance, 0)


def recip(x):
    return pl.reciprocal(x, approx=True)


def keep_rows(stage, near, tiles):
    group = 4

    def keep(block, carry):
        for u in range(group):
            t = block * group + u
            near[t] = stage[pl.ds(t * FEATS, FEATS), :].astype(jnp.bfloat16)
        return carry

    lax.fori_loop(0, tiles // group, keep, 0)


def target_rows(coords, scale, stage, near, tiles):
    norm = sum(c * c for c in coords)
    zero = jnp.zeros_like(norm)
    rows = []
    for c in coords:
        rows += target_terms(-2.0 * c * scale)
    rows += target_terms(scale)
    rows += list(three(norm * scale))
    rows += [zero] * (FEATS - len(rows))
    put_rows(stage, rows, FEATS, tiles)
    keep_rows(stage, near, tiles)


def spread_column(far, first, last, wide):
    row = lax.broadcasted_iota(jnp.int32, (FEATS, LANES), 0)
    pick = jnp.where((row >= first) & (row < last), 1.0, 0.0).astype(jnp.bfloat16)
    group = 4

    def one(block, carry):
        for u in range(group):
            t = block * group + u
            wide[t] = jnp.dot(far[t], pick, preferred_element_type=jnp.float32)
        return carry

    lax.fori_loop(0, wide.shape[0] // group, one, 0)


def density_kernel(sizes_ref, own_ref, ghost_ref, times_ref, here_ref, there_ref,
                   dens_ref, press_ref, far, packed_ref, dest_ref, more_ref,
                   stage, near, mass_b, totals):
    own_tiles = dens_ref.shape[0]
    ghosts = there_ref.shape[0] // 8
    tiles = own_tiles + ghosts

    def field(k):
        return here_ref[pl.ds(k, own_tiles, stride=8), :]

    def far_field(k):
        return there_ref[pl.ds(k, ghosts, stride=8), :]

    own, out_of_reach = [], 0.0
    ghost = []
    reach = jnp.maximum(jnp.max(field(4)), jnp.max(far_field(4))) + 0.01
    for k in range(3):
        x = field(k)
        low, high = jnp.min(x), jnp.max(x)
        centre = 0.5 * (low + high)
        far_x = far_field(k)
        gap = jnp.maximum(jnp.maximum(low - far_x, far_x - high), 0.0)
        out_of_reach = out_of_reach + gap * gap
        own.append(x - centre)
        ghost.append(far_x - centre)
    ghost_mass = far_field(3)
    active = (out_of_reach < reach * reach) & (ghost_mass != 0.0)
    upto = lax.broadcasted_iota(jnp.int32, (LANES, LANES), 0) <= lax.broadcasted_iota(
        jnp.int32, (LANES, LANES), 1)
    upto = jnp.where(upto, 1.0, 0.0).astype(jnp.bfloat16)
    flags = jnp.where(active, 1.0, 0.0).astype(jnp.bfloat16)
    rank = jnp.dot(flags, upto, preferred_element_type=jnp.float32)
    dest = jnp.where(active, rank - 1.0, -1.0).astype(jnp.int32)
    dest_ref[...] = dest
    most = jnp.max(rank)
    more = (most > LANES // 2 + 0.5).astype(jnp.int32)
    more_ref[0] = more
    split = [three(x) for x in ghost + [ghost_mass, far_field(4)]]
    zero = jnp.zeros_like(ghost_mass)
    rows = []
    for term in range(3):
        rows += [s[term] for s in split] + [zero] * 3
    put_rows(stage, rows + [zero] * 8, FEATS, ghosts)

    def squeeze(block, carry):
        for u in range(4):
            g = block * 4 + u
            part = stage[pl.ds(g * FEATS, FEATS), :].astype(jnp.bfloat16)
            moved = by_last(part, one_hot_rows(dest_ref[pl.ds(g, 1), :]))
            totals[g] = moved[:8] + moved[8:16] + moved[16:24]
        return carry

    lax.fori_loop(0, ghosts // 4, squeeze, 0)
    fields = []
    for k, x in enumerate(own + [field(3), field(4)]):
        packed_ref[k, :own_tiles] = x
        packed_ref[k, own_tiles:] = totals[:ghosts, k, :]
        fields.append(packed_ref[k])
    norm = sum(c * c for c in fields[:3])
    ones = jnp.ones_like(norm)
    rows = []
    for c in fields[:3] + [norm]:
        rows += source_terms(c)
    rows += [ones, ones, ones] + list(three(0.5 * fields[4])) + list(three(fields[3])[:2])
    put_rows(stage, rows, FEATS, tiles)

    def turn(g, carry):
        for v in range(2):
            at = g * 2 + v
            cols = jnp.transpose(stage[pl.ds(at * LANES, LANES), :]).astype(jnp.bfloat16)
            for u in range(LANES // FEATS):
                far[at * (LANES // FEATS) + u] = cols[:, u * FEATS:(u + 1) * FEATS]
        return carry

    lax.fori_loop(0, tiles * FEATS // LANES // 2, turn, 0)
    radius = fields[4][:own_tiles]
    target_rows(own, 1.0 / (radius * radius), stage, near, own_tiles)
    spread_column(far, 30, 32, mass_b)
    totals[...] = jnp.zeros_like(totals)

    def add(first, height):
        def body(target, source, place, weight):
            sq = jnp.dot(far[source, first:first + height], near[target],
                         preferred_element_type=jnp.float32)
            sq = jnp.maximum(sq, TINY)
            ratio = sq * lax.rsqrt(sq)
            falloff = jnp.maximum(1.0 - ratio, 0.0)
            falloff = falloff * falloff
            term = falloff * falloff * ((ratio + 0.25) * mass_b[source, first:first + height])
            totals[place] += weight * jnp.sum(term.reshape(height // 8, 8, LANES), axis=0)
        return body

    half = LANES // 2
    sweep(own_ref, sizes_ref[0], times_ref, tiles, own_tiles, 16, add(0, LANES))
    sweep(ghost_ref, sizes_ref[1], times_ref, tiles, own_tiles, 32, add(0, half))

    @pl.when(more > 0)
    def _():
        sweep(ghost_ref, sizes_ref[1], times_ref, tiles, own_tiles, 4, add(half, half))

    summed = jnp.sum(totals[:own_tiles], axis=1)
    norm = KERNEL_NORM / (radius * radius * radius)
    density = norm * (4.0 * summed + field(3))
    dens_ref[...] = density
    press_ref[...] = GAMMA_LESS * field(5) / density


def accel_kernel(sizes_ref, own_ref, ghost_ref, times_ref, more_ref, far, packed_ref, dest_ref,
                 press_ref, press_far_ref, out_ref, stage, near, half_a, half_b, press_all, left, left_half,
                 totals):
    own_tiles = out_ref.shape[1]
    tiles = packed_ref.shape[1]
    ghosts = tiles - own_tiles
    half = LANES // 2
    zero = jnp.zeros((ghosts, LANES), jnp.float32)
    put_rows(stage, list(three(press_far_ref[...])) + [zero] * 13, 16, ghosts)

    def squeeze(block, carry):
        for u in range(4):
            g = block * 4 + u
            part = stage[pl.ds(g * 16, 16), :].astype(jnp.bfloat16)
            moved = by_last(part, one_hot_rows(dest_ref[pl.ds(g, 1), :]))
            press_all[pl.ds(own_tiles + g, 1), :] = moved[0:1] + moved[1:2] + moved[2:3]
        return carry

    lax.fori_loop(0, ghosts // 4, squeeze, 0)
    press_all[:own_tiles] = press_ref[...]
    own = [packed_ref[k, :own_tiles] for k in range(3)]
    target_rows(own, jnp.ones_like(own[0]), stage, near, own_tiles)
    spread_column(far, 27, 30, half_b)
    half_a[...] = 0.5 * packed_ref[4, :own_tiles]
    mass = packed_ref[3]
    load = mass * press_all[...]
    coords = [packed_ref[k] for k in range(3)]
    rows = [mass] + [mass * c for c in coords] + [load] + [load * c for c in coords]
    split = [three(row) for row in rows]
    put_rows(stage, [s[0] for s in split] + [s[1] for s in split], 16, tiles)

    def pack(block, carry):
        for u in range(4):
            t = block * 4 + u
            part = stage[pl.ds(t * 16, 16), :].astype(jnp.bfloat16)
            left[t] = jnp.concatenate([part, part], axis=1)
        return carry

    def pack_half(block, carry):
        for u in range(4):
            t = block * 4 + u
            part = stage[pl.ds((t + own_tiles) * 16, 16), :].astype(jnp.bfloat16)
            for v in range(2):
                piece = part[:, v * half:(v + 1) * half]
                two = jnp.concatenate([piece, piece], axis=1)
                none = jnp.zeros_like(two)
                left_half[v, 0, t] = jnp.concatenate([two, none], axis=1)
                left_half[v, 1, t] = jnp.concatenate([none, two], axis=1)
        return carry

    lax.fori_loop(0, own_tiles // 4, pack, 0)
    lax.fori_loop(0, ghosts // 4, pack_half, 0)
    totals[...] = jnp.zeros_like(totals)

    def slopes(source, target, first, height):
        sq = jnp.dot(far[source, first:first + height], near[target],
                     preferred_element_type=jnp.float32)
        sq = jnp.maximum(sq, TINY)
        radius = half_b[source, first:first + height] + half_a[pl.ds(target, 1), :]
        dist = sq * lax.rsqrt(sq)
        inv = recip(radius)
        wide = inv * inv
        fall = jnp.maximum(inv - dist * wide, 0.0)
        slope = fall * fall * (fall * wide)
        high = slope.astype(jnp.bfloat16)
        low = (slope - high.astype(jnp.float32)).astype(jnp.bfloat16)
        return [high, low]

    def add_one(target, source, place, weight):
        terms = jnp.concatenate(slopes(source, target, 0, LANES), axis=0)
        totals[place] += weight * jnp.dot(left[source], terms, preferred_element_type=jnp.float32)

    def add_two(v):
        def body(both):
            terms, lhs = [], []
            for side, (target, source, place, weight) in enumerate(both):
                terms += slopes(source, target, v * half, half)
                lhs.append(left_half[v, side, jnp.maximum(source - own_tiles, 0)])
            moved = jnp.dot(jnp.concatenate(lhs, axis=0), jnp.concatenate(terms, axis=0),
                            preferred_element_type=jnp.float32)
            for side, (target, source, place, weight) in enumerate(both):
                totals[place] += weight * moved[side * 16:(side + 1) * 16]
        return body

    sweep(own_ref, sizes_ref[0], times_ref, tiles, own_tiles, 16, add_one)
    sweep_two(ghost_ref, sizes_ref[1], times_ref, tiles, own_tiles, 32, add_two(0))

    @pl.when(more_ref[0] > 0)
    def _():
        sweep_two(ghost_ref, sizes_ref[1], times_ref, tiles, own_tiles, 4, add_two(1))

    folded = totals[:own_tiles, :8] + totals[:own_tiles, 8:]
    mixed = [press_ref[...] * folded[:, k] + folded[:, k + 4] for k in range(4)]
    for k in range(3):
        out_ref[k] = 20.0 * KERNEL_NORM * (own[k] * mixed[0] - mixed[k + 1])


SMEM = pl.BlockSpec(memory_space=pltpu.SMEM)
VMEM = pl.BlockSpec(memory_space=pltpu.VMEM)


def plan_call(count, pairs, own_tiles, tiles):
    slots = pairs.shape[1]
    shapes = [(2,), (slots + 1,), (slots + 1,), (own_tiles * tiles + LANES,)]
    return pl.pallas_call(
        functools.partial(plan_kernel, own_tiles=own_tiles, tiles=tiles),
        out_shape=[jax.ShapeDtypeStruct(shape, jnp.int32) for shape in shapes],
        in_specs=[SMEM, SMEM],
        out_specs=[SMEM] * 4,
        cost_estimate=pl.CostEstimate(flops=10 ** 7, bytes_accessed=10 ** 7, transcendentals=0),
        name="plan",
    )(count, pairs)


def route_call(positions, mass, smoothing, energy, destination, domains):
    tiles = mass.shape[0]
    return pl.pallas_call(
        functools.partial(route_kernel, domains=domains),
        out_shape=jax.ShapeDtypeStruct((tiles, 8, LANES), jnp.float32),
        in_specs=[VMEM] * 5,
        out_specs=VMEM,
        scratch_shapes=[
            pltpu.VMEM((tiles * domains, LANES), jnp.bfloat16),
            pltpu.VMEM((tiles * domains, 2 * LANES), jnp.float32),
            pltpu.VMEM((tiles, LANES), jnp.int32),
            pltpu.VMEM((tiles * 8, LANES), jnp.float32),
        ],
        compiler_params=pltpu.CompilerParams(vmem_limit_bytes=48 * 2 ** 20),
        name="route",
    )(positions, mass, smoothing, energy, destination)


def exchange_call(outgoing, rows, cols):
    domains, fields, slots = outgoing.shape
    edge = GT * LANES // slots
    dma = pltpu.SemaphoreType.DMA
    return pl.pallas_call(
        functools.partial(exchange_kernel, rows=rows, cols=cols),
        out_shape=(
            jax.ShapeDtypeStruct(outgoing.shape, jnp.float32),
            jax.ShapeDtypeStruct((4, edge, fields, slots), jnp.float32),
        ),
        in_specs=[VMEM],
        out_specs=(VMEM, VMEM),
        scratch_shapes=[dma, dma((domains,)), dma((domains,)), dma((4,)), dma((4,))],
        compiler_params=pltpu.CompilerParams(collective_id=0, has_side_effects=True),
        name="exchange",
    )(outgoing)


def press_call(press, rows, cols):
    dma = pltpu.SemaphoreType.DMA
    return pl.pallas_call(
        functools.partial(press_kernel, rows=rows, cols=cols),
        out_shape=jax.ShapeDtypeStruct((4,) + press.shape, jnp.float32),
        in_specs=[VMEM],
        out_specs=VMEM,
        scratch_shapes=[dma((4,)), dma((4,))],
        compiler_params=pltpu.CompilerParams(collective_id=1, has_side_effects=True),
        name="press",
    )(press)


def density_call(plan, here, there):
    own_tiles = here.shape[0] // 8
    tiles = own_tiles + there.shape[0] // 8
    flat = jax.ShapeDtypeStruct((own_tiles, LANES), jnp.float32)
    return pl.pallas_call(
        density_kernel,
        out_shape=(
            flat,
            flat,
            jax.ShapeDtypeStruct((tiles, LANES, FEATS), jnp.bfloat16),
            jax.ShapeDtypeStruct((5, tiles, LANES), jnp.float32),
            jax.ShapeDtypeStruct((tiles - own_tiles, LANES), jnp.int32),
            jax.ShapeDtypeStruct((1,), jnp.int32),
        ),
        in_specs=[SMEM] * 4 + [VMEM] * 2,
        out_specs=(VMEM, VMEM, VMEM, VMEM, VMEM, SMEM),
        scratch_shapes=[
            pltpu.VMEM((tiles * FEATS, LANES), jnp.float32),
            pltpu.VMEM((own_tiles, FEATS, LANES), jnp.bfloat16),
            pltpu.VMEM((tiles, LANES, LANES), jnp.float32),
            pltpu.VMEM((max(own_tiles, tiles - own_tiles) + 1, 8, LANES), jnp.float32),
        ],
        name="density",
    )(*plan, here, there)


def accel_call(plan, more, far, packed, dest, press, press_far):
    own_tiles = press.shape[0]
    tiles = packed.shape[1]
    return pl.pallas_call(
        accel_kernel,
        out_shape=jax.ShapeDtypeStruct((3, own_tiles, LANES), jnp.float32),
        in_specs=[SMEM] * 5 + [VMEM] * 5,
        out_specs=VMEM,
        scratch_shapes=[
            pltpu.VMEM((tiles * FEATS, LANES), jnp.float32),
            pltpu.VMEM((own_tiles, FEATS, LANES), jnp.bfloat16),
            pltpu.VMEM((own_tiles, LANES), jnp.float32),
            pltpu.VMEM((tiles, LANES, LANES), jnp.float32),
            pltpu.VMEM((tiles, LANES), jnp.float32),
            pltpu.VMEM((own_tiles, 16, 2 * LANES), jnp.bfloat16),
            pltpu.VMEM((2, 2, tiles - own_tiles, 16, 2 * LANES), jnp.bfloat16),
            pltpu.VMEM((own_tiles + 1, 16, LANES), jnp.float32),
        ],
        name="accel",
    )(*plan, more, far, packed, dest, press, press_far)


def as_tiles(blocks):
    count, fields, slots = blocks.shape
    per = LANES // slots
    joined = blocks.reshape(count // per, per, fields, slots).transpose(0, 2, 1, 3)
    return joined.reshape(count // per * fields, LANES)


def as_blocks(tiles, slots):
    count, fields, lanes = tiles.shape
    per = lanes // slots
    split = tiles.reshape(count, fields, per, slots).transpose(0, 2, 1, 3)
    return split.reshape(count * per, fields, slots)


def local(positions, mass, smoothing, energy, destination, pairs, pair_count):
    rows = lax.axis_size("gx")
    cols = lax.axis_size("gy")
    domains = rows * cols
    own_tiles = mass.shape[0] // LANES
    slots = mass.shape[0] // domains
    flat = (own_tiles, LANES)
    plan = plan_call(pair_count, pairs, own_tiles, own_tiles + 4 * GT)
    sent = route_call(positions.reshape((3,) + flat), mass.reshape(flat), smoothing.reshape(flat),
                      energy.reshape(flat), destination.reshape(flat), domains)
    own, ghost = exchange_call(as_blocks(sent, slots), rows, cols)
    here = as_tiles(own)
    there = as_tiles(ghost.reshape((-1,) + ghost.shape[2:]))
    density, press, far, packed, dest, more = density_call(plan, here, there)
    press_far = press_call(press[:GT], rows, cols).reshape(4 * GT, LANES)
    accel = accel_call(plan, more, far, packed, dest, press, press_far)
    return (density.reshape(-1), accel.reshape(3, -1))


def solution(mesh):
    placed = (
        P(None, ("gx", "gy")),
        P(("gx", "gy")),
        P(("gx", "gy")),
        P(("gx", "gy")),
        P(("gx", "gy"), None),
        P(None, ("gx", "gy")),
        P(("gx", "gy")),
    )
    return jax.shard_map(
        local,
        mesh=mesh,
        in_specs=placed,
        out_specs=(P(("gx", "gy")), P(None, ("gx", "gy"))),
        check_vma=False,
    )
```

```python
import functools
import math

import jax
import jax.numpy as jnp
from jax import lax
from jax.experimental import pallas as pl
from jax.experimental.pallas import tpu as pltpu
from jax.sharding import PartitionSpec as P

GT = 8
LANES = 128
FEATS = 32
TINY = 1e-12
MESH = pl.DeviceIdType.MESH

KERNEL_NORM = 21.0 / (2.0 * math.pi)
GAMMA_LESS = 2.0 / 3.0


def three(x):
    one = x.astype(jnp.bfloat16).astype(jnp.float32)
    rest = x - one
    two = rest.astype(jnp.bfloat16).astype(jnp.float32)
    return one, two, (rest - two).astype(jnp.bfloat16).astype(jnp.float32)


def source_terms(x):
    one, two, low = three(x)
    return [one, two, one, two, low, one]


def target_terms(x):
    one, two, low = three(x)
    return [one, one, two, two, one, low]


def put_rows(stage, rows, width, tiles):
    for k, row in enumerate(rows):
        stage[pl.ds(k, tiles, stride=width), :] = row


def equal_rows(row, height, base=0):
    at = lax.broadcasted_iota(jnp.int32, (height, row.shape[-1]), 0) + base
    return jnp.broadcast_to(row, at.shape) == at


def ones_where(mask):
    return jnp.where(mask, 1.0, 0.0).astype(jnp.bfloat16)


def earlier(size, width):
    row = lax.broadcasted_iota(jnp.int32, (size, width), 0)
    col = lax.broadcasted_iota(jnp.int32, (size, width), 1)
    return row, col


def list_pairs(count_ref, pairs_ref, sizes_ref, key_ref, times_ref, rank_ref, hits_ref, own_tiles,
               tiles):
    slots = pairs_ref.shape[1]
    live = lax.broadcasted_iota(jnp.int32, (1, slots), 1) < count_ref[0]
    target = jnp.where(live, pairs_ref[0:1, :], -1)
    hits = by_last(ones_where(equal_rows(target, own_tiles)),
                   ones_where(equal_rows(pairs_ref[1:2, :], tiles)))
    fresh = jnp.where(hits > 0.0, 1.0, 0.0)
    row, col = earlier(tiles, tiles)
    far_row, far_col = row >= own_tiles, col >= own_tiles
    inside = jnp.dot(fresh.astype(jnp.bfloat16), ones_where((row < col) & (far_row == far_col)),
                     preferred_element_type=jnp.float32)
    total = jnp.dot(fresh.astype(jnp.bfloat16), ones_where(far_row == far_col),
                    preferred_element_type=jnp.float32)
    row, col = earlier(own_tiles, own_tiles)
    above = jnp.dot(ones_where(col < row), total.astype(jnp.bfloat16),
                    preferred_element_type=jnp.float32)
    all_rows = jnp.sum(total, axis=0, keepdims=True).astype(jnp.int32)
    sizes_ref[0:1, :] = all_rows[:, :own_tiles]
    sizes_ref[1:2, :] = all_rows[:, own_tiles:2 * own_tiles]
    column = lax.broadcasted_iota(jnp.int32, (own_tiles, tiles), 1)
    place = jnp.where(hits > 0.0, (inside + above).astype(jnp.int32), -1)
    lists = key_ref.shape[0] // 2
    place = jnp.where((column >= own_tiles) & (place >= 0), place + lists * LANES, place)
    rank_ref[...] = place
    hits_ref[...] = hits.astype(jnp.int32)
    source = lax.broadcasted_iota(jnp.int32, (1, tiles), 1).astype(jnp.float32)
    keys = jnp.zeros((2 * lists, LANES), jnp.float32)
    times = jnp.zeros((2 * lists, LANES), jnp.float32)
    for t in range(own_tiles):
        at = rank_ref[t:t + 1, :]
        high = at // LANES
        many = hits_ref[t:t + 1, :]
        upper = many // LANES
        mine = jnp.where(equal_rows(jnp.where(at < 0, -1, high), 2 * lists), 1.0, 0.0)
        parts = [mine * source, mine, mine * upper.astype(jnp.float32),
                 mine * (many - upper * LANES).astype(jnp.float32)]
        found = by_last(jnp.concatenate(parts, axis=0).astype(jnp.bfloat16),
                        ones_where(equal_rows(jnp.where(at < 0, -1, at - high * LANES), LANES)))
        size = 2 * lists
        keys = keys + found[:size] + float(t * tiles) * found[size:2 * size]
        times = times + float(LANES) * found[2 * size:3 * size] + found[3 * size:]
    key_ref[...] = keys.astype(jnp.int32)
    times_ref[...] = times.astype(jnp.int32)


def route_kernel(count_ref, pairs_ref, pos_ref, mass_ref, smooth_ref, energy_ref, dest_ref, out_ref,
                 sizes_ref, key_ref, times_ref, flags, prefix, rank_ref, rows_ref, place_ref,
                 hits_ref, domains):
    tiles = mass_ref.shape[0]
    list_pairs(count_ref, pairs_ref, sizes_ref, key_ref, times_ref, place_ref, hits_ref, tiles,
               tiles + 4 * GT)
    slots = tiles * LANES // domains
    row, col = earlier(LANES, 2 * LANES)
    before = ones_where((row < col) | (col >= LANES))
    for t in range(tiles):
        flags[t * domains:(t + 1) * domains] = ones_where(
            equal_rows(dest_ref[t:t + 1, :], domains))
    prefix[...] = jnp.dot(flags[...], before, preferred_element_type=jnp.float32)
    seen = jnp.zeros((domains, LANES), jnp.float32)
    for t in range(tiles):
        part = slice(t * domains, (t + 1) * domains)
        mine = flags[part].astype(jnp.float32)
        rank = jnp.sum(mine * (prefix[part, :LANES] + seen), axis=0, keepdims=True)
        rank_ref[t:t + 1, :] = rank.astype(jnp.int32)
        seen = seen + prefix[part, LANES:]
    place = dest_ref[...] * slots + rank_ref[...]
    block = place // LANES
    rank_ref[...] = place - block * LANES
    lane = lax.broadcasted_iota(jnp.int32, (tiles, LANES), 1).astype(jnp.float32)
    from_lane = jnp.zeros((tiles, LANES), jnp.float32)
    from_tile = jnp.zeros((tiles, LANES), jnp.float32)
    for t in range(tiles):
        picked = equal_rows(block[t:t + 1, :], tiles)
        both = jnp.concatenate([jnp.where(picked, lane, 0.0), jnp.where(picked, 1.0, 0.0)], axis=0)
        found = by_last(both.astype(jnp.bfloat16),
                        ones_where(equal_rows(rank_ref[t:t + 1, :], LANES)))
        from_lane = from_lane + found[:tiles]
        from_tile = from_tile + float(t) * found[tiles:]
    fields = [pos_ref[0], pos_ref[1], pos_ref[2], mass_ref[...], smooth_ref[...], energy_ref[...]]
    put_rows(rows_ref, fields + [jnp.zeros_like(lane)] * 2, 8, tiles)
    from_lane = from_lane.astype(jnp.int32)
    from_tile = from_tile.astype(jnp.int32)
    for q in range(tiles):
        at = jnp.broadcast_to(from_lane[q:q + 1, :], (8, LANES))
        tile = jnp.broadcast_to(from_tile[q:q + 1, :], (8, LANES))
        out = jnp.zeros((8, LANES), jnp.float32)
        for t in range(tiles):
            moved = jnp.take_along_axis(rows_ref[t * 8:(t + 1) * 8, :], at, axis=1)
            out = jnp.where(tile == t, moved, out)
        out_ref[q] = out


def beside(i, j, rows, cols):
    return [(i > 0, (i - 1, j), 1), (i < rows - 1, (i + 1, j), 0),
            (j > 0, (i, j - 1), 3), (j < cols - 1, (i, j + 1), 2)]


def exchange_kernel(out_ref, own_ref, ghost_ref, near_sem, send_sem, recv_sem, edge_send, edge_recv,
                    rows, cols):
    domains = rows * cols
    edge = ghost_ref.shape[1]
    i, j = lax.axis_index("gx"), lax.axis_index("gy")
    me = i * cols + j
    barrier = pltpu.get_barrier_semaphore()

    def greet(k, carry):
        peer = lax.rem(me + k, domains)
        pl.semaphore_signal(barrier, inc=1, device_id=(peer // cols, lax.rem(peer, cols)),
                            device_id_type=MESH)
        return carry

    lax.fori_loop(1, domains, greet, 0)
    stay = pltpu.make_async_copy(out_ref.at[me], own_ref.at[me], near_sem)
    stay.start()
    pl.semaphore_wait(barrier, domains - 1)

    def outgoing(peer):
        return pltpu.make_async_remote_copy(
            src_ref=out_ref.at[peer], dst_ref=own_ref.at[me],
            send_sem=send_sem.at[peer], recv_sem=recv_sem.at[me],
            device_id=(peer // cols, lax.rem(peer, cols)), device_id_type=MESH)

    def incoming(source):
        return pltpu.make_async_remote_copy(
            src_ref=out_ref.at[source], dst_ref=own_ref.at[source],
            send_sem=send_sem.at[source], recv_sem=recv_sem.at[source],
            device_id=(source // cols, lax.rem(source, cols)), device_id_type=MESH)

    def send(k, carry):
        outgoing(lax.rem(me + k, domains)).start()
        return carry

    lax.fori_loop(1, domains, send, 0)
    stay.wait()

    def arrive(source, carry):
        @pl.when(source != me)
        def _():
            incoming(source).wait_recv()
        return carry

    lax.fori_loop(0, edge, arrive, 0)
    sides = beside(i, j, rows, cols)

    def across(side):
        there, peer, slot = sides[side]
        return pltpu.make_async_remote_copy(
            src_ref=own_ref.at[pl.ds(0, edge)], dst_ref=ghost_ref.at[slot],
            send_sem=edge_send.at[side], recv_sem=edge_recv.at[slot],
            device_id=peer, device_id_type=MESH)

    def back(side):
        there, peer, slot = sides[side]
        return pltpu.make_async_remote_copy(
            src_ref=own_ref.at[pl.ds(0, edge)], dst_ref=ghost_ref.at[side],
            send_sem=edge_send.at[side], recv_sem=edge_recv.at[side],
            device_id=peer, device_id_type=MESH)

    for side in range(4):
        @pl.when(sides[side][0])
        def _():
            across(side).start()

        @pl.when(jnp.logical_not(sides[side][0]))
        def _():
            ghost_ref[side] = jnp.zeros_like(ghost_ref[side])

    lax.fori_loop(edge, domains, arrive, 0)

    def left(k, carry):
        outgoing(lax.rem(me + k, domains)).wait_send()
        return carry

    lax.fori_loop(1, domains, left, 0)
    for side in range(4):
        @pl.when(sides[side][0])
        def _():
            across(side).wait_send()
            back(side).wait_recv()


def press_kernel(press_ref, ghost_ref, send_sem, recv_sem, rows, cols):
    i, j = lax.axis_index("gx"), lax.axis_index("gy")
    sides = beside(i, j, rows, cols)
    barrier = pltpu.get_barrier_semaphore()
    for there, peer, slot in sides:
        @pl.when(there)
        def _():
            pl.semaphore_signal(barrier, inc=1, device_id=peer, device_id_type=MESH)

    pl.semaphore_wait(barrier, sum(there.astype(jnp.int32) for there, peer, slot in sides))

    def across(side, slot):
        return pltpu.make_async_remote_copy(
            src_ref=press_ref, dst_ref=ghost_ref.at[slot],
            send_sem=send_sem.at[side], recv_sem=recv_sem.at[slot],
            device_id=sides[side][1], device_id_type=MESH)

    for side in range(4):
        @pl.when(sides[side][0])
        def _():
            across(side, sides[side][2]).start()

        @pl.when(jnp.logical_not(sides[side][0]))
        def _():
            ghost_ref[side] = jnp.zeros_like(ghost_ref[side])

    for side in range(4):
        @pl.when(sides[side][0])
        def _():
            across(side, sides[side][2]).wait_send()
            across(side, side).wait_recv()


def one_hot_rows(dest):
    rows = lax.broadcasted_iota(jnp.int32, (LANES, LANES), 0)
    wide = jnp.broadcast_to(dest, (LANES, LANES))
    return jnp.where(wide == rows, 1.0, 0.0).astype(jnp.bfloat16)


def by_last(a, b):
    return lax.dot_general(a, b, (((1,), (1,)), ((), ())), preferred_element_type=jnp.float32)


def sweep(key_ref, times_ref, first, size, tiles, dump, unroll, together, body):
    last = key_ref.shape[0] - 1

    def advance(block, carry):
        for u in range(0, unroll, together):
            picked = []
            for v in range(together):
                k = block * unroll + u + v
                live = k < size
                at = jnp.minimum(first + k, last)
                key = jnp.where(live, key_ref[at], 0)
                target = key // tiles
                source = key - target * tiles
                weight = times_ref[at].astype(jnp.float32)
                picked.append((target, source, jnp.where(live, target, dump), weight))
            body(picked)
        return carry

    lax.fori_loop(0, (size + unroll - 1) // unroll, advance, 0)


def keep_rows(stage, near, tiles):
    group = 4

    def keep(block, carry):
        for u in range(group):
            t = block * group + u
            near[t] = stage[pl.ds(t * FEATS, FEATS), :].astype(jnp.bfloat16)
        return carry

    lax.fori_loop(0, tiles // group, keep, 0)


def target_rows(coords, scale, stage, near, tiles):
    norm = sum(c * c for c in coords)
    zero = jnp.zeros_like(norm)
    rows = []
    for c in coords:
        rows += target_terms(-2.0 * c * scale)
    rows += target_terms(scale)
    rows += list(three(norm * scale))
    rows += [zero] * (FEATS - len(rows))
    put_rows(stage, rows, FEATS, tiles)
    keep_rows(stage, near, tiles)


def spread_column(far, first, last, wide):
    row = lax.broadcasted_iota(jnp.int32, (FEATS, LANES), 0)
    pick = jnp.where((row >= first) & (row < last), 1.0, 0.0).astype(jnp.bfloat16)
    group = 4

    def one(block, carry):
        for u in range(group):
            t = block * group + u
            wide[t] = jnp.dot(far[t], pick, preferred_element_type=jnp.float32)
        return carry

    lax.fori_loop(0, wide.shape[0] // group, one, 0)


def density_kernel(sizes_ref, key_ref, times_ref, here_ref, there_ref,
                   dens_ref, press_ref, far, packed_ref, dest_ref, more_ref,
                   stage, near, mass_b, totals):
    own_tiles = dens_ref.shape[0]
    ghosts = there_ref.shape[0] // 8
    tiles = own_tiles + ghosts

    def field(k):
        return here_ref[pl.ds(k, own_tiles, stride=8), :]

    def far_field(k):
        return there_ref[pl.ds(k, ghosts, stride=8), :]

    own, out_of_reach = [], 0.0
    ghost = []
    reach = jnp.maximum(jnp.max(field(4)), jnp.max(far_field(4))) + 0.01
    for k in range(3):
        x = field(k)
        low, high = jnp.min(x), jnp.max(x)
        centre = 0.5 * (low + high)
        far_x = far_field(k)
        gap = jnp.maximum(jnp.maximum(low - far_x, far_x - high), 0.0)
        out_of_reach = out_of_reach + gap * gap
        own.append(x - centre)
        ghost.append(far_x - centre)
    ghost_mass = far_field(3)
    active = (out_of_reach < reach * reach) & (ghost_mass != 0.0)
    upto = lax.broadcasted_iota(jnp.int32, (LANES, LANES), 0) <= lax.broadcasted_iota(
        jnp.int32, (LANES, LANES), 1)
    upto = jnp.where(upto, 1.0, 0.0).astype(jnp.bfloat16)
    flags = jnp.where(active, 1.0, 0.0).astype(jnp.bfloat16)
    rank = jnp.dot(flags, upto, preferred_element_type=jnp.float32)
    dest = jnp.where(active, rank - 1.0, -1.0).astype(jnp.int32)
    dest_ref[...] = dest
    most = jnp.max(rank)
    more = (most > LANES // 2 + 0.5).astype(jnp.int32)
    more_ref[0] = more
    split = [three(x) for x in ghost + [ghost_mass, far_field(4)]]
    zero = jnp.zeros_like(ghost_mass)
    rows = []
    for term in range(3):
        rows += [s[term] for s in split] + [zero] * 3
    put_rows(stage, rows + [zero] * 8, FEATS, ghosts)

    def squeeze(block, carry):
        for u in range(4):
            g = block * 4 + u
            part = stage[pl.ds(g * FEATS, FEATS), :].astype(jnp.bfloat16)
            moved = by_last(part, one_hot_rows(dest_ref[pl.ds(g, 1), :]))
            totals[g] = moved[:8] + moved[8:16] + moved[16:24]
        return carry

    lax.fori_loop(0, ghosts // 4, squeeze, 0)
    fields = []
    for k, x in enumerate(own + [field(3), field(4)]):
        packed_ref[k, :own_tiles] = x
        packed_ref[k, own_tiles:] = totals[:ghosts, k, :]
        fields.append(packed_ref[k])
    norm = sum(c * c for c in fields[:3])
    ones = jnp.ones_like(norm)
    rows = []
    for c in fields[:3] + [norm]:
        rows += source_terms(c)
    rows += [ones, ones, ones] + list(three(0.5 * fields[4])) + list(three(fields[3])[:2])
    put_rows(stage, rows, FEATS, tiles)

    def turn(g, carry):
        for v in range(2):
            at = g * 2 + v
            cols = jnp.transpose(stage[pl.ds(at * LANES, LANES), :]).astype(jnp.bfloat16)
            for u in range(LANES // FEATS):
                far[at * (LANES // FEATS) + u] = cols[:, u * FEATS:(u + 1) * FEATS]
        return carry

    lax.fori_loop(0, tiles * FEATS // LANES // 2, turn, 0)
    radius = fields[4][:own_tiles]
    target_rows(own, 1.0 / (radius * radius), stage, near, own_tiles)
    spread_column(far, 30, 32, mass_b)
    totals[...] = jnp.zeros_like(totals)

    def add(first, height):
        def body(picked):
            (target, source, place, weight), = picked
            sq = jnp.dot(far[source, first:first + height], near[target],
                         preferred_element_type=jnp.float32)
            sq = jnp.maximum(sq, TINY)
            ratio = sq * lax.rsqrt(sq)
            falloff = jnp.maximum(1.0 - ratio, 0.0)
            falloff = falloff * falloff
            term = falloff * falloff * ((ratio + 0.25) * mass_b[source, first:first + height])
            totals[place] += weight * jnp.sum(term.reshape(height // 8, 8, LANES), axis=0)
        return body

    half = LANES // 2
    own_size, ghost_size, start = sizes_ref[0, 0], sizes_ref[1, 0], key_ref.shape[0] // 2
    sweep(key_ref, times_ref, 0, own_size, tiles, own_tiles, 16, 1, add(0, LANES))
    sweep(key_ref, times_ref, start, ghost_size, tiles, own_tiles, 32, 1, add(0, half))

    @pl.when(more > 0)
    def _():
        sweep(key_ref, times_ref, start, ghost_size, tiles, own_tiles, 4, 1, add(half, half))

    summed = jnp.sum(totals[:own_tiles], axis=1)
    norm = KERNEL_NORM / (radius * radius * radius)
    density = norm * (4.0 * summed + field(3))
    dens_ref[...] = density
    press_ref[...] = GAMMA_LESS * field(5) / density


def accel_kernel(sizes_ref, key_ref, times_ref, more_ref, far, packed_ref, dest_ref,
                 press_ref, press_far_ref, out_ref, stage, near, half_a, half_b, press_all, left, left_half,
                 totals):
    own_tiles = out_ref.shape[1]
    tiles = packed_ref.shape[1]
    ghosts = tiles - own_tiles
    half = LANES // 2
    zero = jnp.zeros((ghosts, LANES), jnp.float32)
    put_rows(stage, list(three(press_far_ref[...])) + [zero] * 13, 16, ghosts)

    def squeeze(block, carry):
        for u in range(4):
            g = block * 4 + u
            part = stage[pl.ds(g * 16, 16), :].astype(jnp.bfloat16)
            moved = by_last(part, one_hot_rows(dest_ref[pl.ds(g, 1), :]))
            press_all[pl.ds(own_tiles + g, 1), :] = moved[0:1] + moved[1:2] + moved[2:3]
        return carry

    lax.fori_loop(0, ghosts // 4, squeeze, 0)
    press_all[:own_tiles] = press_ref[...]
    own = [packed_ref[k, :own_tiles] for k in range(3)]
    target_rows(own, jnp.ones_like(own[0]), stage, near, own_tiles)
    spread_column(far, 27, 30, half_b)
    half_a[...] = 0.5 * packed_ref[4, :own_tiles]
    mass = packed_ref[3]
    load = mass * press_all[...]
    coords = [packed_ref[k] for k in range(3)]
    rows = [mass] + [mass * c for c in coords] + [load] + [load * c for c in coords]
    split = [three(row) for row in rows]
    put_rows(stage, [s[0] for s in split] + [s[1] for s in split], 16, tiles)

    def pack(block, carry):
        for u in range(4):
            t = block * 4 + u
            part = stage[pl.ds(t * 16, 16), :].astype(jnp.bfloat16)
            left[t] = jnp.concatenate([part, part], axis=1)
        return carry

    def pack_half(block, carry):
        for u in range(4):
            t = block * 4 + u
            part = stage[pl.ds((t + own_tiles) * 16, 16), :].astype(jnp.bfloat16)
            for v in range(2):
                piece = part[:, v * half:(v + 1) * half]
                two = jnp.concatenate([piece, piece], axis=1)
                none = jnp.zeros_like(two)
                left_half[v, 0, t] = jnp.concatenate([two, none], axis=1)
                left_half[v, 1, t] = jnp.concatenate([none, two], axis=1)
        return carry

    lax.fori_loop(0, own_tiles // 4, pack, 0)
    lax.fori_loop(0, ghosts // 4, pack_half, 0)
    totals[...] = jnp.zeros_like(totals)

    def slopes(source, target, first, height):
        sq = jnp.dot(far[source, first:first + height], near[target],
                     preferred_element_type=jnp.float32)
        sq = jnp.maximum(sq, TINY)
        radius = half_b[source, first:first + height] + half_a[pl.ds(target, 1), :]
        dist = sq * lax.rsqrt(sq)
        inv = pl.reciprocal(radius, approx=True)
        wide = inv * inv
        fall = jnp.maximum(inv - dist * wide, 0.0)
        slope = fall * fall * (fall * wide)
        high = slope.astype(jnp.bfloat16)
        low = (slope - high.astype(jnp.float32)).astype(jnp.bfloat16)
        return [high, low]

    def add_one(picked):
        (target, source, place, weight), = picked
        terms = jnp.concatenate(slopes(source, target, 0, LANES), axis=0)
        totals[place] += weight * jnp.dot(left[source], terms, preferred_element_type=jnp.float32)

    def add_two(v):
        def body(both):
            terms, lhs = [], []
            for side, (target, source, place, weight) in enumerate(both):
                terms += slopes(source, target, v * half, half)
                lhs.append(left_half[v, side, jnp.maximum(source - own_tiles, 0)])
            moved = jnp.dot(jnp.concatenate(lhs, axis=0), jnp.concatenate(terms, axis=0),
                            preferred_element_type=jnp.float32)
            for side, (target, source, place, weight) in enumerate(both):
                totals[place] += weight * moved[side * 16:(side + 1) * 16]
        return body

    own_size, ghost_size, start = sizes_ref[0, 0], sizes_ref[1, 0], key_ref.shape[0] // 2
    sweep(key_ref, times_ref, 0, own_size, tiles, own_tiles, 16, 1, add_one)
    sweep(key_ref, times_ref, start, ghost_size, tiles, own_tiles, 32, 2, add_two(0))

    @pl.when(more_ref[0] > 0)
    def _():
        sweep(key_ref, times_ref, start, ghost_size, tiles, own_tiles, 4, 2, add_two(1))

    folded = totals[:own_tiles, :8] + totals[:own_tiles, 8:]
    mixed = [press_ref[...] * folded[:, k] + folded[:, k + 4] for k in range(4)]
    for k in range(3):
        out_ref[k] = 20.0 * KERNEL_NORM * (own[k] * mixed[0] - mixed[k + 1])


SMEM = pl.BlockSpec(memory_space=pltpu.SMEM)
VMEM = pl.BlockSpec(memory_space=pltpu.VMEM)


def route_call(count, pairs, positions, mass, smoothing, energy, destination, domains):
    tiles = mass.shape[0]
    pool_tiles = tiles + 4 * GT
    lists = 2 * pl.cdiv(tiles * max(tiles, 4 * GT), LANES)
    return pl.pallas_call(
        functools.partial(route_kernel, domains=domains),
        out_shape=(
            jax.ShapeDtypeStruct((tiles, 8, LANES), jnp.float32),
            jax.ShapeDtypeStruct((2, tiles), jnp.int32),
            jax.ShapeDtypeStruct((lists, LANES), jnp.int32),
            jax.ShapeDtypeStruct((lists, LANES), jnp.int32),
        ),
        in_specs=[SMEM] + [VMEM] * 6,
        out_specs=[VMEM] * 4,
        scratch_shapes=[
            pltpu.VMEM((tiles * domains, LANES), jnp.bfloat16),
            pltpu.VMEM((tiles * domains, 2 * LANES), jnp.float32),
            pltpu.VMEM((tiles, LANES), jnp.int32),
            pltpu.VMEM((tiles * 8, LANES), jnp.float32),
            pltpu.VMEM((tiles, pool_tiles), jnp.int32),
            pltpu.VMEM((tiles, pool_tiles), jnp.int32),
        ],
        compiler_params=pltpu.CompilerParams(vmem_limit_bytes=48 * 2 ** 20),
        name="route",
    )(count, pairs, positions, mass, smoothing, energy, destination)


def exchange_call(outgoing, rows, cols):
    domains, fields, slots = outgoing.shape
    edge = GT * LANES // slots
    dma = pltpu.SemaphoreType.DMA
    return pl.pallas_call(
        functools.partial(exchange_kernel, rows=rows, cols=cols),
        out_shape=(
            jax.ShapeDtypeStruct(outgoing.shape, jnp.float32),
            jax.ShapeDtypeStruct((4, edge, fields, slots), jnp.float32),
        ),
        in_specs=[VMEM],
        out_specs=(VMEM, VMEM),
        scratch_shapes=[dma, dma((domains,)), dma((domains,)), dma((4,)), dma((4,))],
        compiler_params=pltpu.CompilerParams(collective_id=0, has_side_effects=True),
        name="exchange",
    )(outgoing)


def press_call(press, rows, cols):
    dma = pltpu.SemaphoreType.DMA
    return pl.pallas_call(
        functools.partial(press_kernel, rows=rows, cols=cols),
        out_shape=jax.ShapeDtypeStruct((4,) + press.shape, jnp.float32),
        in_specs=[VMEM],
        out_specs=VMEM,
        scratch_shapes=[dma((4,)), dma((4,))],
        compiler_params=pltpu.CompilerParams(collective_id=1, has_side_effects=True),
        name="press",
    )(press)


def density_call(plan, here, there):
    own_tiles = here.shape[0] // 8
    tiles = own_tiles + there.shape[0] // 8
    flat = jax.ShapeDtypeStruct((own_tiles, LANES), jnp.float32)
    return pl.pallas_call(
        density_kernel,
        out_shape=(
            flat,
            flat,
            jax.ShapeDtypeStruct((tiles, LANES, FEATS), jnp.bfloat16),
            jax.ShapeDtypeStruct((5, tiles, LANES), jnp.float32),
            jax.ShapeDtypeStruct((tiles - own_tiles, LANES), jnp.int32),
            jax.ShapeDtypeStruct((1,), jnp.int32),
        ),
        in_specs=[SMEM] * 3 + [VMEM] * 2,
        out_specs=(VMEM, VMEM, VMEM, VMEM, VMEM, SMEM),
        scratch_shapes=[
            pltpu.VMEM((tiles * FEATS, LANES), jnp.float32),
            pltpu.VMEM((own_tiles, FEATS, LANES), jnp.bfloat16),
            pltpu.VMEM((tiles, LANES, LANES), jnp.float32),
            pltpu.VMEM((max(own_tiles, tiles - own_tiles) + 1, 8, LANES), jnp.float32),
        ],
        name="density",
    )(*plan, here, there)


def accel_call(plan, more, far, packed, dest, press, press_far):
    own_tiles = press.shape[0]
    tiles = packed.shape[1]
    return pl.pallas_call(
        accel_kernel,
        out_shape=jax.ShapeDtypeStruct((3, own_tiles, LANES), jnp.float32),
        in_specs=[SMEM] * 4 + [VMEM] * 5,
        out_specs=VMEM,
        scratch_shapes=[
            pltpu.VMEM((tiles * FEATS, LANES), jnp.float32),
            pltpu.VMEM((own_tiles, FEATS, LANES), jnp.bfloat16),
            pltpu.VMEM((own_tiles, LANES), jnp.float32),
            pltpu.VMEM((tiles, LANES, LANES), jnp.float32),
            pltpu.VMEM((tiles, LANES), jnp.float32),
            pltpu.VMEM((own_tiles, 16, 2 * LANES), jnp.bfloat16),
            pltpu.VMEM((2, 2, tiles - own_tiles, 16, 2 * LANES), jnp.bfloat16),
            pltpu.VMEM((own_tiles + 1, 16, LANES), jnp.float32),
        ],
        name="accel",
    )(*plan, more, far, packed, dest, press, press_far)


def as_tiles(blocks):
    count, fields, slots = blocks.shape
    per = LANES // slots
    joined = blocks.reshape(count // per, per, fields, slots).transpose(0, 2, 1, 3)
    return joined.reshape(count // per * fields, LANES)


def as_blocks(tiles, slots):
    count, fields, lanes = tiles.shape
    per = lanes // slots
    split = tiles.reshape(count, fields, per, slots).transpose(0, 2, 1, 3)
    return split.reshape(count * per, fields, slots)


def local(positions, mass, smoothing, energy, destination, pairs, pair_count):
    rows = lax.axis_size("gx")
    cols = lax.axis_size("gy")
    domains = rows * cols
    own_tiles = mass.shape[0] // LANES
    slots = mass.shape[0] // domains
    flat = (own_tiles, LANES)
    sent, sizes, keys, times = route_call(
        pair_count, pairs, positions.reshape((3,) + flat), mass.reshape(flat),
        smoothing.reshape(flat), energy.reshape(flat), destination.reshape(flat), domains)
    plan = (sizes, keys.reshape(-1), times.reshape(-1))
    own, ghost = exchange_call(as_blocks(sent, slots), rows, cols)
    here = as_tiles(own)
    there = as_tiles(ghost.reshape((-1,) + ghost.shape[2:]))
    density, press, far, packed, dest, more = density_call(plan, here, there)
    press_far = press_call(press[:GT], rows, cols).reshape(4 * GT, LANES)
    accel = accel_call(plan, more, far, packed, dest, press, press_far)
    return (density.reshape(-1), accel.reshape(3, -1))


def solution(mesh):
    placed = (
        P(None, ("gx", "gy")),
        P(("gx", "gy")),
        P(("gx", "gy")),
        P(("gx", "gy")),
        P(("gx", "gy"), None),
        P(None, ("gx", "gy")),
        P(("gx", "gy")),
    )
    return jax.shard_map(
        local,
        mesh=mesh,
        in_specs=placed,
        out_specs=(P(("gx", "gy")), P(None, ("gx", "gy"))),
        check_vma=False,
    )
```

```python
import functools
import math

import jax
import jax.numpy as jnp
from jax import lax
from jax.experimental import pallas as pl
from jax.experimental.pallas import tpu as pltpu
from jax.sharding import PartitionSpec as P

GT = 8
LANES = 128
FEATS = 32
TINY = 1e-12
MESH = pl.DeviceIdType.MESH

KERNEL_NORM = 21.0 / (2.0 * math.pi)
GAMMA_LESS = 2.0 / 3.0


def three(x):
    one = x.astype(jnp.bfloat16).astype(jnp.float32)
    rest = x - one
    two = rest.astype(jnp.bfloat16).astype(jnp.float32)
    return one, two, (rest - two).astype(jnp.bfloat16).astype(jnp.float32)


def source_terms(x):
    one, two, low = three(x)
    return [one, two, one, two, low, one]


def target_terms(x):
    one, two, low = three(x)
    return [one, one, two, two, one, low]


def put_rows(stage, rows, width, tiles, first=0):
    for k, row in enumerate(rows):
        stage[pl.ds(first + k, tiles, stride=width), :] = row


def equal_rows(row, height, base=0):
    at = lax.broadcasted_iota(jnp.int32, (height, row.shape[-1]), 0) + base
    return jnp.broadcast_to(row, at.shape) == at


def ones_where(mask):
    return jnp.where(mask, 1.0, 0.0).astype(jnp.bfloat16)


def earlier(size, width):
    row = lax.broadcasted_iota(jnp.int32, (size, width), 0)
    col = lax.broadcasted_iota(jnp.int32, (size, width), 1)
    return row, col


def list_pairs(count_ref, pairs_ref, sizes_ref, key_ref, times_ref, rank_ref, hits_ref, own_tiles,
               tiles):
    slots = pairs_ref.shape[1]
    live = lax.broadcasted_iota(jnp.int32, (1, slots), 1) < count_ref[0]
    target = jnp.where(live, pairs_ref[0:1, :], -1)
    hits = by_last(ones_where(equal_rows(target, own_tiles)),
                   ones_where(equal_rows(pairs_ref[1:2, :], tiles)))
    fresh = jnp.where(hits > 0.0, 1.0, 0.0)
    row, col = earlier(tiles, tiles)
    far_row, far_col = row >= own_tiles, col >= own_tiles
    inside = jnp.dot(fresh.astype(jnp.bfloat16), ones_where((row < col) & (far_row == far_col)),
                     preferred_element_type=jnp.float32)
    total = jnp.dot(fresh.astype(jnp.bfloat16), ones_where(far_row == far_col),
                    preferred_element_type=jnp.float32)
    row, col = earlier(own_tiles, own_tiles)
    above = jnp.dot(ones_where(col < row), total.astype(jnp.bfloat16),
                    preferred_element_type=jnp.float32)
    all_rows = jnp.sum(total, axis=0, keepdims=True).astype(jnp.int32)
    sizes_ref[0:1, :] = all_rows[:, :own_tiles]
    sizes_ref[1:2, :] = all_rows[:, own_tiles:2 * own_tiles]
    column = lax.broadcasted_iota(jnp.int32, (own_tiles, tiles), 1)
    place = jnp.where(hits > 0.0, (inside + above).astype(jnp.int32), -1)
    lists = key_ref.shape[0] // 2
    place = jnp.where((column >= own_tiles) & (place >= 0), place + lists * LANES, place)
    rank_ref[...] = place
    hits_ref[...] = hits.astype(jnp.int32)
    source = lax.broadcasted_iota(jnp.int32, (1, tiles), 1).astype(jnp.float32)
    keys = jnp.zeros((2 * lists, LANES), jnp.float32)
    times = jnp.zeros((2 * lists, LANES), jnp.float32)
    for t in range(own_tiles):
        at = rank_ref[t:t + 1, :]
        high = at // LANES
        many = hits_ref[t:t + 1, :]
        upper = many // LANES
        mine = jnp.where(equal_rows(jnp.where(at < 0, -1, high), 2 * lists), 1.0, 0.0)
        parts = [mine * source, mine, mine * upper.astype(jnp.float32),
                 mine * (many - upper * LANES).astype(jnp.float32)]
        found = by_last(jnp.concatenate(parts, axis=0).astype(jnp.bfloat16),
                        ones_where(equal_rows(jnp.where(at < 0, -1, at - high * LANES), LANES)))
        size = 2 * lists
        keys = keys + found[:size] + float(t * tiles) * found[size:2 * size]
        times = times + float(LANES) * found[2 * size:3 * size] + found[3 * size:]
    key_ref[...] = keys.astype(jnp.int32)
    times_ref[...] = times.astype(jnp.int32)


def order_rows(pos_ref, mass_ref, smooth_ref, energy_ref, dest_ref, sent_ref,
               flags, prefix, rank_ref, rows_ref, index_ref):
    tiles = mass_ref.shape[0]
    domains, width, slots = sent_ref.shape
    row, col = earlier(LANES, 2 * LANES)
    before = ones_where((row < col) | (col >= LANES))
    for t in range(tiles):
        flags[t * domains:(t + 1) * domains] = ones_where(
            equal_rows(dest_ref[t:t + 1, :], domains))
    prefix[...] = jnp.dot(flags[...], before, preferred_element_type=jnp.float32)
    seen = jnp.zeros((domains, LANES), jnp.float32)
    for t in range(tiles):
        part = slice(t * domains, (t + 1) * domains)
        mine = flags[part].astype(jnp.float32)
        rank = jnp.sum(mine * (prefix[part, :LANES] + seen), axis=0, keepdims=True)
        rank_ref[t:t + 1, :] = rank.astype(jnp.int32)
        seen = seen + prefix[part, LANES:]
    place = dest_ref[...] * slots + rank_ref[...]
    block = place // LANES
    rank_ref[...] = place - block * LANES
    lane = lax.broadcasted_iota(jnp.int32, (tiles, LANES), 1).astype(jnp.float32)
    from_lane = jnp.zeros((tiles, LANES), jnp.float32)
    from_tile = jnp.zeros((tiles, LANES), jnp.float32)
    for t in range(tiles):
        picked = equal_rows(block[t:t + 1, :], tiles)
        both = jnp.concatenate([jnp.where(picked, lane, 0.0), jnp.where(picked, 1.0, 0.0)], axis=0)
        found = by_last(both.astype(jnp.bfloat16),
                        ones_where(equal_rows(rank_ref[t:t + 1, :], LANES)))
        from_lane = from_lane + found[:tiles]
        from_tile = from_tile + float(t) * found[tiles:]
    put_rows(rows_ref, [mass_ref[...], smooth_ref[...], energy_ref[...]], width, tiles, 3)
    for t in range(tiles):
        rows_ref[t * width:t * width + 3, :] = pos_ref[:, t * LANES:(t + 1) * LANES]
        rows_ref[t * width + 6:(t + 1) * width, :] = jnp.zeros((width - 6, LANES), jnp.float32)
    index_ref[0] = from_lane.astype(jnp.int32)
    index_ref[1] = from_tile.astype(jnp.int32)
    per = LANES // slots

    def gather(q, carry):
        at = jnp.broadcast_to(index_ref[0, pl.ds(q, 1), :], (width, LANES))
        tile = jnp.broadcast_to(index_ref[1, pl.ds(q, 1), :], (width, LANES))
        out = jnp.zeros((width, LANES), jnp.float32)
        for t in range(tiles):
            moved = jnp.take_along_axis(rows_ref[t * width:(t + 1) * width, :], at, axis=1)
            out = jnp.where(tile == t, moved, out)
        for p in range(per):
            sent_ref[q * per + p] = out[:, p * slots:(p + 1) * slots]
        return carry

    lax.fori_loop(0, tiles, gather, 0)


def beside(i, j, rows, cols):
    return [(i > 0, (i - 1, j), 1), (i < rows - 1, (i + 1, j), 0),
            (j > 0, (i, j - 1), 3), (j < cols - 1, (i, j + 1), 2)]


def exchange_kernel(count_ref, pairs_ref, pos_ref, mass_ref, smooth_ref, energy_ref, dest_ref,
                    own_ref, ghost_ref, sizes_ref, key_ref, times_ref,
                    out_ref, flags, prefix, rank_ref, rows_ref, index_ref, place_ref, hits_ref,
                    send_sem, recv_sem, edge_send, edge_recv, rows, cols):
    domains = rows * cols
    tiles = mass_ref.shape[0]
    edge = ghost_ref.shape[1]
    i, j = lax.axis_index("gx"), lax.axis_index("gy")
    me = i * cols + j
    barrier = pltpu.get_barrier_semaphore()

    def greet(k, carry):
        peer = lax.rem(me + k, domains)
        pl.semaphore_signal(barrier, inc=1, device_id=(peer // cols, lax.rem(peer, cols)),
                            device_id_type=MESH)
        return carry

    lax.fori_loop(1, domains, greet, 0)
    order_rows(pos_ref, mass_ref, smooth_ref, energy_ref, dest_ref, out_ref,
               flags, prefix, rank_ref, rows_ref, index_ref)
    pl.semaphore_wait(barrier, domains - 1)

    def outgoing(peer):
        return pltpu.make_async_remote_copy(
            src_ref=out_ref.at[peer], dst_ref=own_ref.at[me],
            send_sem=send_sem.at[peer], recv_sem=recv_sem.at[me],
            device_id=(peer // cols, lax.rem(peer, cols)), device_id_type=MESH)

    def incoming(source):
        return pltpu.make_async_remote_copy(
            src_ref=out_ref.at[source], dst_ref=own_ref.at[source],
            send_sem=send_sem.at[source], recv_sem=recv_sem.at[source],
            device_id=(source // cols, lax.rem(source, cols)), device_id_type=MESH)

    def send(k, carry):
        outgoing(lax.rem(me + k, domains)).start()
        return carry

    lax.fori_loop(1, domains, send, 0)
    own_ref[me] = out_ref[me]
    list_pairs(count_ref, pairs_ref, sizes_ref, key_ref, times_ref, place_ref, hits_ref, tiles,
               tiles + 4 * GT)

    def arrive(source, carry):
        @pl.when(source != me)
        def _():
            incoming(source).wait_recv()
        return carry

    lax.fori_loop(0, edge, arrive, 0)
    sides = beside(i, j, rows, cols)

    def across(side):
        there, peer, slot = sides[side]
        return pltpu.make_async_remote_copy(
            src_ref=own_ref.at[pl.ds(0, edge)], dst_ref=ghost_ref.at[slot],
            send_sem=edge_send.at[side], recv_sem=edge_recv.at[slot],
            device_id=peer, device_id_type=MESH)

    def back(side):
        there, peer, slot = sides[side]
        return pltpu.make_async_remote_copy(
            src_ref=own_ref.at[pl.ds(0, edge)], dst_ref=ghost_ref.at[side],
            send_sem=edge_send.at[side], recv_sem=edge_recv.at[side],
            device_id=peer, device_id_type=MESH)

    for side in range(4):
        @pl.when(sides[side][0])
        def _():
            across(side).start()

        @pl.when(jnp.logical_not(sides[side][0]))
        def _():
            ghost_ref[side] = jnp.zeros_like(ghost_ref[side])

    lax.fori_loop(edge, domains, arrive, 0)

    def left(k, carry):
        outgoing(lax.rem(me + k, domains)).wait_send()
        return carry

    lax.fori_loop(1, domains, left, 0)
    for side in range(4):
        @pl.when(sides[side][0])
        def _():
            across(side).wait_send()
            back(side).wait_recv()


def press_kernel(press_ref, ghost_ref, send_sem, recv_sem, rows, cols):
    i, j = lax.axis_index("gx"), lax.axis_index("gy")
    sides = beside(i, j, rows, cols)
    barrier = pltpu.get_barrier_semaphore()
    for there, peer, slot in sides:
        @pl.when(there)
        def _():
            pl.semaphore_signal(barrier, inc=1, device_id=peer, device_id_type=MESH)

    pl.semaphore_wait(barrier, sum(there.astype(jnp.int32) for there, peer, slot in sides))

    def across(side, slot):
        return pltpu.make_async_remote_copy(
            src_ref=press_ref, dst_ref=ghost_ref.at[slot],
            send_sem=send_sem.at[side], recv_sem=recv_sem.at[slot],
            device_id=sides[side][1], device_id_type=MESH)

    for side in range(4):
        @pl.when(sides[side][0])
        def _():
            across(side, sides[side][2]).start()

        @pl.when(jnp.logical_not(sides[side][0]))
        def _():
            ghost_ref[side] = jnp.zeros_like(ghost_ref[side])

    for side in range(4):
        @pl.when(sides[side][0])
        def _():
            across(side, sides[side][2]).wait_send()
            across(side, side).wait_recv()


def one_hot_rows(dest):
    rows = lax.broadcasted_iota(jnp.int32, (LANES, LANES), 0)
    wide = jnp.broadcast_to(dest, (LANES, LANES))
    return jnp.where(wide == rows, 1.0, 0.0).astype(jnp.bfloat16)


def by_last(a, b):
    return lax.dot_general(a, b, (((1,), (1,)), ((), ())), preferred_element_type=jnp.float32)


def sweep(key_ref, times_ref, first, size, tiles, dump, unroll, together, body):
    last = key_ref.shape[0] - 1

    def advance(block, carry):
        for u in range(0, unroll, together):
            picked = []
            for v in range(together):
                k = block * unroll + u + v
                live = k < size
                at = jnp.minimum(first + k, last)
                key = jnp.where(live, key_ref[at], 0)
                target = key // tiles
                source = key - target * tiles
                weight = times_ref[at].astype(jnp.float32)
                picked.append((target, source, jnp.where(live, target, dump), weight))
            body(picked)
        return carry

    lax.fori_loop(0, (size + unroll - 1) // unroll, advance, 0)


def keep_rows(stage, near, tiles):
    group = 4

    def keep(block, carry):
        for u in range(group):
            t = block * group + u
            near[t] = stage[pl.ds(t * FEATS, FEATS), :].astype(jnp.bfloat16)
        return carry

    lax.fori_loop(0, tiles // group, keep, 0)


def target_rows(coords, scale, stage, near, tiles):
    norm = sum(c * c for c in coords)
    zero = jnp.zeros_like(norm)
    rows = []
    for c in coords:
        rows += target_terms(-2.0 * c * scale)
    rows += target_terms(scale)
    rows += list(three(norm * scale))
    rows += [zero] * (FEATS - len(rows))
    put_rows(stage, rows, FEATS, tiles)
    keep_rows(stage, near, tiles)


def spread_column(far, first, last, wide):
    row = lax.broadcasted_iota(jnp.int32, (FEATS, LANES), 0)
    pick = jnp.where((row >= first) & (row < last), 1.0, 0.0).astype(jnp.bfloat16)
    group = 4

    def one(block, carry):
        for u in range(group):
            t = block * group + u
            wide[t] = jnp.dot(far[t], pick, preferred_element_type=jnp.float32)
        return carry

    lax.fori_loop(0, wide.shape[0] // group, one, 0)


def density_kernel(sizes_ref, key_ref, times_ref, here_ref, there_ref,
                   dens_ref, press_ref, far, packed_ref, dest_ref, more_ref,
                   stage, near, mass_b, totals):
    own_tiles = dens_ref.shape[0]
    ghosts = there_ref.shape[0] // 8
    tiles = own_tiles + ghosts

    def field(k):
        return here_ref[pl.ds(k, own_tiles, stride=8), :]

    def far_field(k):
        return there_ref[pl.ds(k, ghosts, stride=8), :]

    own, out_of_reach = [], 0.0
    ghost = []
    reach = jnp.maximum(jnp.max(field(4)), jnp.max(far_field(4))) + 0.01
    for k in range(3):
        x = field(k)
        low, high = jnp.min(x), jnp.max(x)
        centre = 0.5 * (low + high)
        far_x = far_field(k)
        gap = jnp.maximum(jnp.maximum(low - far_x, far_x - high), 0.0)
        out_of_reach = out_of_reach + gap * gap
        own.append(x - centre)
        ghost.append(far_x - centre)
    ghost_mass = far_field(3)
    active = (out_of_reach < reach * reach) & (ghost_mass != 0.0)
    upto = lax.broadcasted_iota(jnp.int32, (LANES, LANES), 0) <= lax.broadcasted_iota(
        jnp.int32, (LANES, LANES), 1)
    upto = jnp.where(upto, 1.0, 0.0).astype(jnp.bfloat16)
    flags = jnp.where(active, 1.0, 0.0).astype(jnp.bfloat16)
    rank = jnp.dot(flags, upto, preferred_element_type=jnp.float32)
    dest = jnp.where(active, rank - 1.0, -1.0).astype(jnp.int32)
    dest_ref[...] = dest
    most = jnp.max(rank)
    more = (most > LANES // 2 + 0.5).astype(jnp.int32)
    more_ref[0] = more
    split = [three(x) for x in ghost + [ghost_mass, far_field(4)]]
    zero = jnp.zeros_like(ghost_mass)
    rows = []
    for term in range(3):
        rows += [s[term] for s in split] + [zero] * 3
    put_rows(stage, rows + [zero] * 8, FEATS, ghosts)

    def squeeze(block, carry):
        for u in range(4):
            g = block * 4 + u
            part = stage[pl.ds(g * FEATS, FEATS), :].astype(jnp.bfloat16)
            moved = by_last(part, one_hot_rows(dest_ref[pl.ds(g, 1), :]))
            totals[g] = moved[:8] + moved[8:16] + moved[16:24]
        return carry

    lax.fori_loop(0, ghosts // 4, squeeze, 0)
    fields = []
    for k, x in enumerate(own + [field(3), field(4)]):
        packed_ref[k, :own_tiles] = x
        packed_ref[k, own_tiles:] = totals[:ghosts, k, :]
        fields.append(packed_ref[k])
    norm = sum(c * c for c in fields[:3])
    ones = jnp.ones_like(norm)
    rows = []
    for c in fields[:3] + [norm]:
        rows += source_terms(c)
    rows += [ones, ones, ones] + list(three(0.5 * fields[4])) + list(three(fields[3])[:2])
    put_rows(stage, rows, FEATS, tiles)

    def turn(g, carry):
        for v in range(2):
            at = g * 2 + v
            cols = jnp.transpose(stage[pl.ds(at * LANES, LANES), :]).astype(jnp.bfloat16)
            for u in range(LANES // FEATS):
                far[at * (LANES // FEATS) + u] = cols[:, u * FEATS:(u + 1) * FEATS]
        return carry

    lax.fori_loop(0, tiles * FEATS // LANES // 2, turn, 0)
    radius = fields[4][:own_tiles]
    target_rows(own, 1.0 / (radius * radius), stage, near, own_tiles)
    spread_column(far, 30, 32, mass_b)
    totals[...] = jnp.zeros_like(totals)

    def add(first, height):
        def body(picked):
            (target, source, place, weight), = picked
            sq = jnp.dot(far[source, first:first + height], near[target],
                         preferred_element_type=jnp.float32)
            sq = jnp.maximum(sq, TINY)
            ratio = sq * lax.rsqrt(sq)
            falloff = jnp.maximum(1.0 - ratio, 0.0)
            falloff = falloff * falloff
            term = falloff * falloff * ((ratio + 0.25) * mass_b[source, first:first + height])
            totals[place] += weight * jnp.sum(term.reshape(height // 8, 8, LANES), axis=0)
        return body

    half = LANES // 2
    own_size, ghost_size, start = sizes_ref[0, 0], sizes_ref[1, 0], key_ref.shape[0] // 2
    sweep(key_ref, times_ref, 0, own_size, tiles, own_tiles, 16, 1, add(0, LANES))
    sweep(key_ref, times_ref, start, ghost_size, tiles, own_tiles, 32, 1, add(0, half))

    @pl.when(more > 0)
    def _():
        sweep(key_ref, times_ref, start, ghost_size, tiles, own_tiles, 4, 1, add(half, half))

    summed = jnp.sum(totals[:own_tiles], axis=1)
    norm = KERNEL_NORM / (radius * radius * radius)
    density = norm * (4.0 * summed + field(3))
    dens_ref[...] = density
    press_ref[...] = GAMMA_LESS * field(5) / density


def accel_kernel(sizes_ref, key_ref, times_ref, more_ref, far, packed_ref, dest_ref,
                 press_ref, press_far_ref, out_ref, stage, near, half_a, half_b, press_all, left, left_half,
                 totals):
    own_tiles = out_ref.shape[1]
    tiles = packed_ref.shape[1]
    ghosts = tiles - own_tiles
    half = LANES // 2
    zero = jnp.zeros((ghosts, LANES), jnp.float32)
    put_rows(stage, list(three(press_far_ref[...])) + [zero] * 13, 16, ghosts)

    def squeeze(block, carry):
        for u in range(4):
            g = block * 4 + u
            part = stage[pl.ds(g * 16, 16), :].astype(jnp.bfloat16)
            moved = by_last(part, one_hot_rows(dest_ref[pl.ds(g, 1), :]))
            press_all[pl.ds(own_tiles + g, 1), :] = moved[0:1] + moved[1:2] + moved[2:3]
        return carry

    lax.fori_loop(0, ghosts // 4, squeeze, 0)
    press_all[:own_tiles] = press_ref[...]
    own = [packed_ref[k, :own_tiles] for k in range(3)]
    target_rows(own, jnp.ones_like(own[0]), stage, near, own_tiles)
    spread_column(far, 27, 30, half_b)
    half_a[...] = 0.5 * packed_ref[4, :own_tiles]
    mass = packed_ref[3]
    load = mass * press_all[...]
    coords = [packed_ref[k] for k in range(3)]
    rows = [mass] + [mass * c for c in coords] + [load] + [load * c for c in coords]
    split = [three(row) for row in rows]
    put_rows(stage, [s[0] for s in split] + [s[1] for s in split], 16, tiles)

    def pack(block, carry):
        for u in range(4):
            t = block * 4 + u
            part = stage[pl.ds(t * 16, 16), :].astype(jnp.bfloat16)
            left[t] = jnp.concatenate([part, part], axis=1)
        return carry

    def pack_half(block, carry):
        for u in range(4):
            t = block * 4 + u
            part = stage[pl.ds((t + own_tiles) * 16, 16), :].astype(jnp.bfloat16)
            for v in range(2):
                piece = part[:, v * half:(v + 1) * half]
                two = jnp.concatenate([piece, piece], axis=1)
                none = jnp.zeros_like(two)
                left_half[v, 0, t] = jnp.concatenate([two, none], axis=1)
                left_half[v, 1, t] = jnp.concatenate([none, two], axis=1)
        return carry

    lax.fori_loop(0, own_tiles // 4, pack, 0)
    lax.fori_loop(0, ghosts // 4, pack_half, 0)
    totals[...] = jnp.zeros_like(totals)

    def slopes(source, target, first, height):
        sq = jnp.dot(far[source, first:first + height], near[target],
                     preferred_element_type=jnp.float32)
        sq = jnp.maximum(sq, TINY)
        radius = half_b[source, first:first + height] + half_a[pl.ds(target, 1), :]
        dist = sq * lax.rsqrt(sq)
        inv = pl.reciprocal(radius, approx=True)
        wide = inv * inv
        fall = jnp.maximum(inv - dist * wide, 0.0)
        slope = fall * fall * (fall * wide)
        high = slope.astype(jnp.bfloat16)
        low = (slope - high.astype(jnp.float32)).astype(jnp.bfloat16)
        return [high, low]

    def add_one(picked):
        (target, source, place, weight), = picked
        terms = jnp.concatenate(slopes(source, target, 0, LANES), axis=0)
        totals[place] += weight * jnp.dot(left[source], terms, preferred_element_type=jnp.float32)

    def add_two(v):
        def body(both):
            terms, lhs = [], []
            for side, (target, source, place, weight) in enumerate(both):
                terms += slopes(source, target, v * half, half)
                lhs.append(left_half[v, side, jnp.maximum(source - own_tiles, 0)])
            moved = jnp.dot(jnp.concatenate(lhs, axis=0), jnp.concatenate(terms, axis=0),
                            preferred_element_type=jnp.float32)
            for side, (target, source, place, weight) in enumerate(both):
                totals[place] += weight * moved[side * 16:(side + 1) * 16]
        return body

    own_size, ghost_size, start = sizes_ref[0, 0], sizes_ref[1, 0], key_ref.shape[0] // 2
    sweep(key_ref, times_ref, 0, own_size, tiles, own_tiles, 16, 1, add_one)
    sweep(key_ref, times_ref, start, ghost_size, tiles, own_tiles, 32, 2, add_two(0))

    @pl.when(more_ref[0] > 0)
    def _():
        sweep(key_ref, times_ref, start, ghost_size, tiles, own_tiles, 4, 2, add_two(1))

    folded = totals[:own_tiles, :8] + totals[:own_tiles, 8:]
    mixed = [press_ref[...] * folded[:, k] + folded[:, k + 4] for k in range(4)]
    for k in range(3):
        out_ref[k] = 20.0 * KERNEL_NORM * (own[k] * mixed[0] - mixed[k + 1])


SMEM = pl.BlockSpec(memory_space=pltpu.SMEM)
VMEM = pl.BlockSpec(memory_space=pltpu.VMEM)


def exchange_call(count, pairs, positions, mass, smoothing, energy, destination, rows, cols):
    tiles = mass.shape[0]
    pool_tiles = tiles + 4 * GT
    lists = 2 * pl.cdiv(tiles * max(tiles, 4 * GT), LANES)
    domains = rows * cols
    slots = tiles * LANES // domains
    edge = GT * LANES // slots
    dma = pltpu.SemaphoreType.DMA
    return pl.pallas_call(
        functools.partial(exchange_kernel, rows=rows, cols=cols),
        out_shape=(
            jax.ShapeDtypeStruct((domains, 8, slots), jnp.float32),
            jax.ShapeDtypeStruct((4, edge, 8, slots), jnp.float32),
            jax.ShapeDtypeStruct((2, tiles), jnp.int32),
            jax.ShapeDtypeStruct((lists, LANES), jnp.int32),
            jax.ShapeDtypeStruct((lists, LANES), jnp.int32),
        ),
        in_specs=[SMEM] + [VMEM] * 6,
        out_specs=[VMEM] * 5,
        scratch_shapes=[
            pltpu.VMEM((domains, 8, slots), jnp.float32),
            pltpu.VMEM((tiles * domains, LANES), jnp.bfloat16),
            pltpu.VMEM((tiles * domains, 2 * LANES), jnp.float32),
            pltpu.VMEM((tiles, LANES), jnp.int32),
            pltpu.VMEM((tiles * 8, LANES), jnp.float32),
            pltpu.VMEM((2, tiles, LANES), jnp.int32),
            pltpu.VMEM((tiles, pool_tiles), jnp.int32),
            pltpu.VMEM((tiles, pool_tiles), jnp.int32),
            dma((domains,)), dma((domains,)), dma((4,)), dma((4,)),
        ],
        compiler_params=pltpu.CompilerParams(
            collective_id=0, has_side_effects=True, vmem_limit_bytes=48 * 2 ** 20),
        name="exchange",
    )(count, pairs, positions, mass, smoothing, energy, destination)


def press_call(press, rows, cols):
    dma = pltpu.SemaphoreType.DMA
    return pl.pallas_call(
        functools.partial(press_kernel, rows=rows, cols=cols),
        out_shape=jax.ShapeDtypeStruct((4,) + press.shape, jnp.float32),
        in_specs=[VMEM],
        out_specs=VMEM,
        scratch_shapes=[dma((4,)), dma((4,))],
        compiler_params=pltpu.CompilerParams(collective_id=1, has_side_effects=True),
        name="press",
    )(press)


def density_call(plan, here, there):
    own_tiles = here.shape[0] // 8
    tiles = own_tiles + there.shape[0] // 8
    flat = jax.ShapeDtypeStruct((own_tiles, LANES), jnp.float32)
    return pl.pallas_call(
        density_kernel,
        out_shape=(
            flat,
            flat,
            jax.ShapeDtypeStruct((tiles, LANES, FEATS), jnp.bfloat16),
            jax.ShapeDtypeStruct((5, tiles, LANES), jnp.float32),
            jax.ShapeDtypeStruct((tiles - own_tiles, LANES), jnp.int32),
            jax.ShapeDtypeStruct((1,), jnp.int32),
        ),
        in_specs=[SMEM] * 3 + [VMEM] * 2,
        out_specs=(VMEM, VMEM, VMEM, VMEM, VMEM, SMEM),
        scratch_shapes=[
            pltpu.VMEM((tiles * FEATS, LANES), jnp.float32),
            pltpu.VMEM((own_tiles, FEATS, LANES), jnp.bfloat16),
            pltpu.VMEM((tiles, LANES, LANES), jnp.float32),
            pltpu.VMEM((max(own_tiles, tiles - own_tiles) + 1, 8, LANES), jnp.float32),
        ],
        name="density",
    )(*plan, here, there)


def accel_call(plan, more, far, packed, dest, press, press_far):
    own_tiles = press.shape[0]
    tiles = packed.shape[1]
    return pl.pallas_call(
        accel_kernel,
        out_shape=jax.ShapeDtypeStruct((3, own_tiles, LANES), jnp.float32),
        in_specs=[SMEM] * 4 + [VMEM] * 5,
        out_specs=VMEM,
        scratch_shapes=[
            pltpu.VMEM((tiles * FEATS, LANES), jnp.float32),
            pltpu.VMEM((own_tiles, FEATS, LANES), jnp.bfloat16),
            pltpu.VMEM((own_tiles, LANES), jnp.float32),
            pltpu.VMEM((tiles, LANES, LANES), jnp.float32),
            pltpu.VMEM((tiles, LANES), jnp.float32),
            pltpu.VMEM((own_tiles, 16, 2 * LANES), jnp.bfloat16),
            pltpu.VMEM((2, 2, tiles - own_tiles, 16, 2 * LANES), jnp.bfloat16),
            pltpu.VMEM((own_tiles + 1, 16, LANES), jnp.float32),
        ],
        name="accel",
    )(*plan, more, far, packed, dest, press, press_far)


def as_tiles(blocks):
    count, fields, slots = blocks.shape
    per = LANES // slots
    joined = blocks.reshape(count // per, per, fields, slots).transpose(0, 2, 1, 3)
    return joined.reshape(count // per * fields, LANES)


def local(positions, mass, smoothing, energy, destination, pairs, pair_count):
    rows = lax.axis_size("gx")
    cols = lax.axis_size("gy")
    own_tiles = mass.shape[0] // LANES
    flat = (own_tiles, LANES)
    own, ghost, sizes, keys, times = exchange_call(
        pair_count, pairs, positions, mass.reshape(flat), smoothing.reshape(flat),
        energy.reshape(flat), destination.reshape(flat), rows, cols)
    plan = (sizes, keys.reshape(-1), times.reshape(-1))
    here = as_tiles(own)
    there = as_tiles(ghost.reshape((-1,) + ghost.shape[2:]))
    density, press, far, packed, dest, more = density_call(plan, here, there)
    press_far = press_call(press[:GT], rows, cols).reshape(4 * GT, LANES)
    accel = accel_call(plan, more, far, packed, dest, press, press_far)
    return (density.reshape(-1), accel.reshape(3, -1))


def solution(mesh):
    placed = (
        P(None, ("gx", "gy")),
        P(("gx", "gy")),
        P(("gx", "gy")),
        P(("gx", "gy")),
        P(("gx", "gy"), None),
        P(None, ("gx", "gy")),
        P(("gx", "gy")),
    )
    return jax.shard_map(
        local,
        mesh=mesh,
        in_specs=placed,
        out_specs=(P(("gx", "gy")), P(None, ("gx", "gy"))),
        check_vma=False,
    )
```

```python
import functools
import math

import jax
import jax.numpy as jnp
from jax import lax
from jax.experimental import pallas as pl
from jax.experimental.pallas import tpu as pltpu
from jax.sharding import PartitionSpec as P

GT = 8
LANES = 128
DEPTH = 48
TINY = 1e-12
MESH = pl.DeviceIdType.MESH

KERNEL_NORM = 21.0 / (2.0 * math.pi)
GAMMA_LESS = 2.0 / 3.0


def three(x):
    one = x.astype(jnp.bfloat16).astype(jnp.float32)
    rest = x - one
    two = rest.astype(jnp.bfloat16).astype(jnp.float32)
    return one, two, (rest - two).astype(jnp.bfloat16).astype(jnp.float32)


def source_terms(x):
    one, two, low = three(x)
    return jnp.concatenate([one, two, one, two, low, one], axis=0).astype(jnp.bfloat16)


def target_terms(x):
    one, two, low = three(x)
    return jnp.concatenate([one, one, two, two, one, low], axis=0).astype(jnp.bfloat16)


def put_rows(stage, rows, width, tiles, first=0):
    for k, row in enumerate(rows):
        stage[pl.ds(first + k, tiles, stride=width), :] = row


def equal_rows(row, height, base=0):
    at = lax.broadcasted_iota(jnp.int32, (height, row.shape[-1]), 0) + base
    return jnp.broadcast_to(row, at.shape) == at


def ones_where(mask):
    return jnp.where(mask, 1.0, 0.0).astype(jnp.bfloat16)


def earlier(size, width):
    row = lax.broadcasted_iota(jnp.int32, (size, width), 0)
    col = lax.broadcasted_iota(jnp.int32, (size, width), 1)
    return row, col


def list_pairs(count_ref, pairs_ref, plan_ref, rank_ref, hits_ref, own_tiles, tiles):
    slots = pairs_ref.shape[1]
    live = lax.broadcasted_iota(jnp.int32, (1, slots), 1) < count_ref[0]
    target = jnp.where(live, pairs_ref[0:1, :], -1)
    hits = by_last(ones_where(equal_rows(target, own_tiles)),
                   ones_where(equal_rows(pairs_ref[1:2, :], tiles)))
    fresh = jnp.where(hits > 0.0, 1.0, 0.0)
    row, col = earlier(tiles, tiles)
    far_row, far_col = row >= own_tiles, col >= own_tiles
    inside = jnp.dot(fresh.astype(jnp.bfloat16), ones_where((row < col) & (far_row == far_col)),
                     preferred_element_type=jnp.float32)
    total = jnp.dot(fresh.astype(jnp.bfloat16), ones_where(far_row == far_col),
                    preferred_element_type=jnp.float32)
    row, col = earlier(own_tiles, own_tiles)
    above = jnp.dot(ones_where(col < row), total.astype(jnp.bfloat16),
                    preferred_element_type=jnp.float32)
    all_rows = jnp.sum(total, axis=0, keepdims=True).astype(jnp.int32)
    column = lax.broadcasted_iota(jnp.int32, (own_tiles, tiles), 1)
    place = jnp.where(hits > 0.0, (inside + above).astype(jnp.int32), -1)
    lists = (plan_ref.shape[0] - 2) // 4
    place = jnp.where((column >= own_tiles) & (place >= 0), place + lists * LANES, place)
    rank_ref[...] = place
    hits_ref[...] = hits.astype(jnp.int32)
    source = lax.broadcasted_iota(jnp.int32, (1, tiles), 1).astype(jnp.float32)
    keys = jnp.zeros((2 * lists, LANES), jnp.float32)
    times = jnp.zeros((2 * lists, LANES), jnp.float32)
    for t in range(own_tiles):
        at = rank_ref[t:t + 1, :]
        high = at // LANES
        many = hits_ref[t:t + 1, :]
        upper = many // LANES
        mine = jnp.where(equal_rows(jnp.where(at < 0, -1, high), 2 * lists), 1.0, 0.0)
        parts = [mine * source, mine, mine * upper.astype(jnp.float32),
                 mine * (many - upper * LANES).astype(jnp.float32)]
        found = by_last(jnp.concatenate(parts, axis=0).astype(jnp.bfloat16),
                        ones_where(equal_rows(jnp.where(at < 0, -1, at - high * LANES), LANES)))
        size = 2 * lists
        keys = keys + found[:size] + float(t * tiles) * found[size:2 * size]
        times = times + float(LANES) * found[2 * size:3 * size] + found[3 * size:]
    plan_ref[:2 * lists] = keys.astype(jnp.int32)
    plan_ref[2 * lists:4 * lists] = times.astype(jnp.int32)
    plan_ref[4 * lists:4 * lists + 1] = jnp.broadcast_to(all_rows[:, :1], (1, LANES))
    plan_ref[4 * lists + 1:] = jnp.broadcast_to(all_rows[:, tiles - 1:], (1, LANES))


def order_rows(pos_ref, mass_ref, smooth_ref, energy_ref, dest_ref, sent_ref,
               flags, prefix, rank_ref, rows_ref, index_ref):
    tiles = mass_ref.shape[0]
    domains, width, slots = sent_ref.shape
    row, col = earlier(LANES, 2 * LANES)
    before = ones_where((row < col) | (col >= LANES))
    for t in range(tiles):
        flags[t * domains:(t + 1) * domains] = ones_where(
            equal_rows(dest_ref[t:t + 1, :], domains))
    prefix[...] = jnp.dot(flags[...], before, preferred_element_type=jnp.float32)
    seen = jnp.zeros((domains, LANES), jnp.float32)
    for t in range(tiles):
        part = slice(t * domains, (t + 1) * domains)
        mine = flags[part].astype(jnp.float32)
        rank = jnp.sum(mine * (prefix[part, :LANES] + seen), axis=0, keepdims=True)
        rank_ref[t:t + 1, :] = rank.astype(jnp.int32)
        seen = seen + prefix[part, LANES:]
    place = dest_ref[...] * slots + rank_ref[...]
    block = place // LANES
    rank_ref[...] = place - block * LANES
    lane = lax.broadcasted_iota(jnp.int32, (tiles, LANES), 1).astype(jnp.float32)
    from_lane = jnp.zeros((tiles, LANES), jnp.float32)
    from_tile = jnp.zeros((tiles, LANES), jnp.float32)
    for t in range(tiles):
        picked = equal_rows(block[t:t + 1, :], tiles)
        both = jnp.concatenate([jnp.where(picked, lane, 0.0), jnp.where(picked, 1.0, 0.0)], axis=0)
        found = by_last(both.astype(jnp.bfloat16),
                        ones_where(equal_rows(rank_ref[t:t + 1, :], LANES)))
        from_lane = from_lane + found[:tiles]
        from_tile = from_tile + float(t) * found[tiles:]
    ones = jnp.ones((tiles, LANES), jnp.float32)
    put_rows(rows_ref, [smooth_ref[...], mass_ref[...], energy_ref[...], 0.0 * ones], width, tiles, 4)
    put_rows(rows_ref, [ones], width, tiles, 0)
    for t in range(tiles):
        rows_ref[t * width + 1:t * width + 4, :] = pos_ref[:, t * LANES:(t + 1) * LANES]
    index_ref[0] = from_lane.astype(jnp.int32)
    index_ref[1] = from_tile.astype(jnp.int32)
    per = LANES // slots

    def gather(q, carry):
        at = jnp.broadcast_to(index_ref[0, pl.ds(q, 1), :], (width, LANES))
        tile = jnp.broadcast_to(index_ref[1, pl.ds(q, 1), :], (width, LANES))
        out = jnp.zeros((width, LANES), jnp.float32)
        for t in range(tiles):
            moved = jnp.take_along_axis(rows_ref[t * width:(t + 1) * width, :], at, axis=1)
            out = jnp.where(tile == t, moved, out)
        for p in range(per):
            sent_ref[q * per + p] = out[:, p * slots:(p + 1) * slots]
        return carry

    lax.fori_loop(0, tiles, gather, 0)


def beside(i, j, rows, cols):
    return [(i > 0, (i - 1, j), 1), (i < rows - 1, (i + 1, j), 0),
            (j > 0, (i, j - 1), 3), (j < cols - 1, (i, j + 1), 2)]


def exchange_kernel(count_ref, *refs, rows, cols):
    given, refs = refs[:6], refs[6:]
    own_ref, ghost_ref, listed_ref = refs[:3]
    held, refs = refs[3:9], refs[9:]
    (out_ref, flags, prefix, rank_ref, rows_ref, index_ref, place_ref, hits_ref, plan_ref,
     load_sem, plan_sem, send_sem, recv_sem, edge_send, edge_recv) = refs
    pairs_ref, pos_ref, mass_ref, smooth_ref, energy_ref, dest_ref = held
    loads = [pltpu.make_async_copy(a, b, load_sem.at[k]) for k, (a, b) in enumerate(zip(given, held))]
    for load in loads:
        load.start()
    domains = rows * cols
    tiles = mass_ref.shape[0]
    edge = ghost_ref.shape[1]
    i, j = lax.axis_index("gx"), lax.axis_index("gy")
    me = i * cols + j
    barrier = pltpu.get_barrier_semaphore()

    def greet(k, carry):
        peer = lax.rem(me + k, domains)
        pl.semaphore_signal(barrier, inc=1, device_id=(peer // cols, lax.rem(peer, cols)),
                            device_id_type=MESH)
        return carry

    lax.fori_loop(1, domains, greet, 0)
    for load in loads:
        load.wait()
    order_rows(pos_ref, mass_ref, smooth_ref, energy_ref, dest_ref, out_ref,
               flags, prefix, rank_ref, rows_ref, index_ref)
    pl.semaphore_wait(barrier, domains - 1)

    def outgoing(peer):
        return pltpu.make_async_remote_copy(
            src_ref=out_ref.at[peer], dst_ref=own_ref.at[me],
            send_sem=send_sem.at[peer], recv_sem=recv_sem.at[me],
            device_id=(peer // cols, lax.rem(peer, cols)), device_id_type=MESH)

    def incoming(source):
        return pltpu.make_async_remote_copy(
            src_ref=out_ref.at[source], dst_ref=own_ref.at[source],
            send_sem=send_sem.at[source], recv_sem=recv_sem.at[source],
            device_id=(source // cols, lax.rem(source, cols)), device_id_type=MESH)

    def send(k, carry):
        outgoing(lax.rem(me + k, domains)).start()
        return carry

    lax.fori_loop(1, domains, send, 0)
    own_ref[me] = out_ref[me]
    list_pairs(count_ref, pairs_ref, plan_ref, place_ref, hits_ref, tiles, tiles + 4 * GT)
    listed = pltpu.make_async_copy(plan_ref, listed_ref, plan_sem)
    listed.start()

    def arrive(source, carry):
        @pl.when(source != me)
        def _():
            incoming(source).wait_recv()
        return carry

    lax.fori_loop(0, edge, arrive, 0)
    sides = beside(i, j, rows, cols)

    def across(side):
        there, peer, slot = sides[side]
        return pltpu.make_async_remote_copy(
            src_ref=own_ref.at[pl.ds(0, edge)], dst_ref=ghost_ref.at[slot],
            send_sem=edge_send.at[side], recv_sem=edge_recv.at[slot],
            device_id=peer, device_id_type=MESH)

    def back(side):
        there, peer, slot = sides[side]
        return pltpu.make_async_remote_copy(
            src_ref=own_ref.at[pl.ds(0, edge)], dst_ref=ghost_ref.at[side],
            send_sem=edge_send.at[side], recv_sem=edge_recv.at[side],
            device_id=peer, device_id_type=MESH)

    for side in range(4):
        @pl.when(sides[side][0])
        def _():
            across(side).start()

        @pl.when(jnp.logical_not(sides[side][0]))
        def _():
            ghost_ref[side] = jnp.zeros_like(ghost_ref[side])

    lax.fori_loop(edge, domains, arrive, 0)

    def left(k, carry):
        outgoing(lax.rem(me + k, domains)).wait_send()
        return carry

    lax.fori_loop(1, domains, left, 0)
    for side in range(4):
        @pl.when(sides[side][0])
        def _():
            across(side).wait_send()
            back(side).wait_recv()

    listed.wait()


def press_kernel(press_ref, ghost_ref, send_sem, recv_sem, rows, cols):
    i, j = lax.axis_index("gx"), lax.axis_index("gy")
    sides = beside(i, j, rows, cols)
    barrier = pltpu.get_barrier_semaphore()
    for there, peer, slot in sides:
        @pl.when(there)
        def _():
            pl.semaphore_signal(barrier, inc=1, device_id=peer, device_id_type=MESH)

    pl.semaphore_wait(barrier, sum(there.astype(jnp.int32) for there, peer, slot in sides))

    def across(side, slot):
        return pltpu.make_async_remote_copy(
            src_ref=press_ref, dst_ref=ghost_ref.at[slot],
            send_sem=send_sem.at[side], recv_sem=recv_sem.at[slot],
            device_id=sides[side][1], device_id_type=MESH)

    for side in range(4):
        @pl.when(sides[side][0])
        def _():
            across(side, sides[side][2]).start()

        @pl.when(jnp.logical_not(sides[side][0]))
        def _():
            ghost_ref[side] = jnp.zeros_like(ghost_ref[side])

    for side in range(4):
        @pl.when(sides[side][0])
        def _():
            across(side, sides[side][2]).wait_send()
            across(side, side).wait_recv()


def one_hot_rows(dest):
    rows = lax.broadcasted_iota(jnp.int32, (LANES, LANES), 0)
    wide = jnp.broadcast_to(dest, (LANES, LANES))
    return jnp.where(wide == rows, 1.0, 0.0).astype(jnp.bfloat16)


def by_last(a, b):
    return lax.dot_general(a, b, (((1,), (1,)), ((), ())), preferred_element_type=jnp.float32)


def sweep(plan_ref, which, tiles, dump, unroll, together, body):
    length = (plan_ref.shape[0] - 2 * LANES) // 4
    size = plan_ref[4 * length + which * LANES]

    def advance(block, carry):
        for u in range(0, unroll, together):
            picked = []
            for v in range(together):
                k = block * unroll + u + v
                live = k < size
                at = which * length + jnp.minimum(k, length - 1)
                key = jnp.where(live, plan_ref[at], 0)
                target = key // tiles
                source = key - target * tiles
                weight = plan_ref[2 * length + at].astype(jnp.float32)
                picked.append((target, source, jnp.where(live, target, dump), weight))
            body(picked)
        return carry

    lax.fori_loop(0, (size + unroll - 1) // unroll, advance, 0)


def in_groups(count, group, body):
    def step(block, carry):
        for u in range(group):
            body(block * group + u)
        return carry

    lax.fori_loop(0, count // group, step, 0)


def tile_rows(ref, t, height=8):
    return ref[pl.ds(pl.multiple_of(t * height, height), height), :]


def put_tile(ref, t, value):
    ref[pl.ds(pl.multiple_of(t * 8, 8), 8), :] = value


def spread_row(far, k, wide, tiles, scale):
    row = lax.broadcasted_iota(jnp.int32, (DEPTH, LANES), 0)
    pick = jnp.where((row == k) | (row == 8 + k) | (row == 32 + k), scale, 0.0).astype(jnp.bfloat16)

    def one(t):
        wide[t] = jnp.dot(far[t], pick, preferred_element_type=jnp.float32)

    in_groups(tiles, 8, one)


def density_kernel(plan_ref, here_ref, there_ref,
                   dens_ref, press_ref, edge_ref, far, base_ref, dest_ref, more_ref,
                   near, mass_b, totals):
    own_tiles = dens_ref.shape[0]
    ghosts = dest_ref.shape[0]
    tiles = own_tiles + ghosts
    row = lax.broadcasted_iota(jnp.int32, (8, LANES), 0)
    spatial = (row >= 1) & (row <= 3)
    first = here_ref[0:8, :]
    low, high, most = first, first, there_ref[0:8, :]
    for t in range(1, own_tiles):
        part = here_ref[t * 8:(t + 1) * 8, :]
        low, high = jnp.minimum(low, part), jnp.maximum(high, part)
    for g in range(1, ghosts):
        most = jnp.maximum(most, there_ref[g * 8:(g + 1) * 8, :])
    low = jnp.min(low, axis=1, keepdims=True)
    high = jnp.max(high, axis=1, keepdims=True)
    most = jnp.maximum(jnp.max(most, axis=1, keepdims=True), high)
    reach = most[4:5, :] + 0.01
    reach = reach * reach
    centre = jnp.where(spatial, 0.5 * (low + high), 0.0)

    def shifted(part):
        moved = part - centre
        norm = jnp.sum(jnp.where(spatial, moved * moved, 0.0), axis=0, keepdims=True)
        return jnp.where(row == 7, norm, moved), norm

    def own(t):
        moved, norm = shifted(tile_rows(here_ref, t))
        put_tile(base_ref, t, moved)
        far[t] = by_last(ones_where(equal_rows(same, LANES)),
                         source_terms(moved)).astype(jnp.bfloat16)
        radius = moved[4:5, :]
        wanted = jnp.where(row == 0, norm, jnp.where(spatial, -2.0 * moved, jnp.where(
            row == 7, 1.0, 0.0)))
        near[t] = target_terms(wanted * (1.0 / (radius * radius)))

    same = lax.broadcasted_iota(jnp.int32, (1, LANES), 1)
    in_groups(own_tiles, 8, own)

    def ghost(g):
        part = tile_rows(there_ref, g)
        gap = jnp.maximum(jnp.maximum(low - part, part - high), 0.0)
        beyond = jnp.sum(jnp.where(spatial, gap * gap, 0.0), axis=0, keepdims=True)
        active = (beyond < reach) & (part[5:6, :] != 0.0)
        totals[0, pl.ds(g, 1), :] = jnp.where(active, 1.0, 0.0)
        moved, norm = shifted(part)
        put_tile(base_ref, own_tiles + g, moved)

    in_groups(ghosts, 8, ghost)
    flags = totals[0, :ghosts, :]
    at, upto = earlier(LANES, LANES)
    rank = jnp.dot(flags.astype(jnp.bfloat16), ones_where(at <= upto),
                   preferred_element_type=jnp.float32)
    dest_ref[...] = jnp.where(flags > 0.0, rank - 1.0, -1.0).astype(jnp.int32)
    totals[0, :ghosts, :] = rank
    slot = lax.broadcasted_iota(jnp.int32, (LANES, DEPTH), 0).astype(jnp.float32)
    term = lax.broadcasted_iota(jnp.int32, (LANES, DEPTH), 1)
    unit = (term == 0) | (term == 16) | (term == 40)
    more = (jnp.max(rank) > LANES // 2 + 0.5).astype(jnp.int32)
    more_ref[0] = more

    def squeeze(g):
        moved = by_last(ones_where(equal_rows(dest_ref[pl.ds(g, 1), :], LANES)),
                        source_terms(tile_rows(base_ref, own_tiles + g)))
        unused = slot >= totals[0, pl.ds(g, 1), LANES - 1:]
        far[own_tiles + g] = jnp.where(unit & unused, 1.0, moved).astype(jnp.bfloat16)

    in_groups(ghosts, 8, squeeze)
    spread_row(far, 5, mass_b, tiles, 1.0)
    totals[...] = jnp.zeros_like(totals)

    def add(first, height):
        def body(picked):
            (target, source, place, weight), = picked
            sq = jnp.dot(far[source, first:first + height], near[target],
                         preferred_element_type=jnp.float32)
            sq = jnp.maximum(sq, TINY)
            ratio = sq * lax.rsqrt(sq)
            falloff = jnp.maximum(1.0 - ratio, 0.0)
            falloff = falloff * falloff
            term = falloff * falloff * ((ratio + 0.25) * mass_b[source, first:first + height])
            summed = jnp.sum(term.reshape(height // 8, 8, LANES), axis=0)
            totals[place, :8] += weight * summed
        return body

    half = LANES // 2
    sweep(plan_ref, 0, tiles, own_tiles, 16, 1, add(0, LANES))
    sweep(plan_ref, 1, tiles, own_tiles, 32, 1, add(0, half))

    @pl.when(more > 0)
    def _():
        sweep(plan_ref, 1, tiles, own_tiles, 4, 1, add(half, half))

    def field(k):
        return here_ref[pl.ds(k, own_tiles, stride=8), :]

    summed = jnp.sum(totals[:own_tiles, :8], axis=1)
    radius = field(4)
    density = KERNEL_NORM / (radius * radius * radius) * (4.0 * summed + field(5))
    dens_ref[...] = density
    press = GAMMA_LESS * field(6) / density
    press_ref[...] = press
    edge_ref[...] = press[:GT]


def accel_kernel(plan_ref, more_ref, far, base_ref, dest_ref,
                 press_ref, press_far_ref, out_ref, near, left, left_half, totals, half_a, half_b):
    own_tiles = press_ref.shape[0]
    ghosts = dest_ref.shape[0]
    tiles = own_tiles + ghosts
    half = LANES // 2
    row = lax.broadcasted_iota(jnp.int32, (8, LANES), 0)
    spatial = (row >= 1) & (row <= 3)

    def loaded(part, press):
        twice = jnp.where(row < 4, part, pltpu.roll(part, 4, 0)) * part[5:6, :]
        one, two, low = three(jnp.where(row < 4, twice, twice * press))
        return jnp.concatenate([one, two], axis=0).astype(jnp.bfloat16)

    def own(t):
        part = tile_rows(base_ref, t)
        wanted = jnp.where(row == 0, part[7:8, :], jnp.where(spatial, -2.0 * part, jnp.where(
            row == 7, 1.0, 0.0)))
        half_a[pl.ds(t, 1), :] = 0.5 * part[4:5, :]
        near[t] = target_terms(wanted)
        rows = loaded(part, press_ref[pl.ds(t, 1), :])
        left[t] = jnp.concatenate([rows, rows], axis=1)

    in_groups(own_tiles, 8, own)

    def ghost(g):
        rows = loaded(tile_rows(base_ref, own_tiles + g), press_far_ref[pl.ds(g, 1), :])
        moved = by_last(rows, ones_where(equal_rows(dest_ref[pl.ds(g, 1), :], LANES)))
        moved = moved.astype(jnp.bfloat16)
        none = jnp.zeros((16, LANES), jnp.bfloat16)
        for v in range(2):
            piece = moved[:, v * half:(v + 1) * half]
            two = jnp.concatenate([piece, piece], axis=1)
            left_half[v, 0, g] = jnp.concatenate([two, none], axis=1)
            left_half[v, 1, g] = jnp.concatenate([none, two], axis=1)

    in_groups(ghosts, 8, ghost)
    spread_row(far, 4, half_b, tiles, 0.5)
    totals[...] = jnp.zeros_like(totals)

    def slopes(source, target, first, height):
        sq = jnp.dot(far[source, first:first + height], near[target],
                     preferred_element_type=jnp.float32)
        radius = half_b[source, first:first + height] + half_a[pl.ds(target, 1), :]
        sq = jnp.maximum(sq, TINY)
        dist = sq * lax.rsqrt(sq)
        inv = pl.reciprocal(radius, approx=True)
        wide = inv * inv
        fall = jnp.maximum(inv - dist * wide, 0.0)
        slope = fall * fall * (fall * wide)
        high = slope.astype(jnp.bfloat16)
        low = (slope - high.astype(jnp.float32)).astype(jnp.bfloat16)
        return [high, low]

    def add_one(picked):
        (target, source, place, weight), = picked
        terms = jnp.concatenate(slopes(source, target, 0, LANES), axis=0)
        totals[place] += weight * jnp.dot(left[source], terms, preferred_element_type=jnp.float32)

    def add_two(v):
        def body(both):
            terms, lhs = [], []
            for side, (target, source, place, weight) in enumerate(both):
                terms += slopes(source, target, v * half, half)
                lhs.append(left_half[v, side, jnp.maximum(source - own_tiles, 0)])
            moved = jnp.dot(jnp.concatenate(lhs, axis=0), jnp.concatenate(terms, axis=0),
                            preferred_element_type=jnp.float32)
            for side, (target, source, place, weight) in enumerate(both):
                totals[place] += weight * moved[side * 16:(side + 1) * 16]
        return body

    sweep(plan_ref, 0, tiles, own_tiles, 16, 1, add_one)
    sweep(plan_ref, 1, tiles, own_tiles, 32, 2, add_two(0))

    @pl.when(more_ref[0] > 0)
    def _():
        sweep(plan_ref, 1, tiles, own_tiles, 4, 2, add_two(1))

    for t in range(own_tiles):
        both = totals[t, :8] + totals[t, 8:]
        mixed = jnp.where(row < 4, both * press_ref[t:t + 1, :], both)
        mixed = mixed + pltpu.roll(mixed, 4, 0)
        pulled = 20.0 * KERNEL_NORM * (base_ref[t * 8:(t + 1) * 8, :] * mixed[0:1, :] - mixed)
        out_ref[:, t * LANES:(t + 1) * LANES] = pulled[1:4, :]


SMEM = pl.BlockSpec(memory_space=pltpu.SMEM)
VMEM = pl.BlockSpec(memory_space=pltpu.VMEM)
HBM = pl.BlockSpec(memory_space=pltpu.HBM)
GRANT = 24 * 2 ** 20


def exchange_call(count, pairs, positions, mass, smoothing, energy, destination, rows, cols):
    tiles = mass.shape[0]
    pool_tiles = tiles + 4 * GT
    lists = 2 * pl.cdiv(tiles * max(tiles, 4 * GT), LANES)
    domains = rows * cols
    slots = tiles * LANES // domains
    edge = GT * LANES // slots
    dma = pltpu.SemaphoreType.DMA
    given = (pairs, positions, mass, smoothing, energy, destination)
    return pl.pallas_call(
        functools.partial(exchange_kernel, rows=rows, cols=cols),
        out_shape=(
            jax.ShapeDtypeStruct((domains, 8, slots), jnp.float32),
            jax.ShapeDtypeStruct((4, edge, 8, slots), jnp.float32),
            jax.ShapeDtypeStruct((2 * lists + 2, LANES), jnp.int32),
        ),
        in_specs=[SMEM] + [HBM] * 6,
        out_specs=[VMEM] * 2 + [HBM],
        scratch_shapes=[pltpu.VMEM(x.shape, x.dtype) for x in given] + [
            pltpu.VMEM((domains, 8, slots), jnp.float32),
            pltpu.VMEM((tiles * domains, LANES), jnp.bfloat16),
            pltpu.VMEM((tiles * domains, 2 * LANES), jnp.float32),
            pltpu.VMEM((tiles, LANES), jnp.int32),
            pltpu.VMEM((tiles * 8, LANES), jnp.float32),
            pltpu.VMEM((2, tiles, LANES), jnp.int32),
            pltpu.VMEM((tiles, pool_tiles), jnp.int32),
            pltpu.VMEM((tiles, pool_tiles), jnp.int32),
            pltpu.VMEM((2 * lists + 2, LANES), jnp.int32),
            dma((6,)), dma, dma((domains,)), dma((domains,)), dma((4,)), dma((4,)),
        ],
        compiler_params=pltpu.CompilerParams(
            collective_id=0, has_side_effects=True, vmem_limit_bytes=GRANT),
        name="exchange",
    )(count, *given)


def press_call(press, rows, cols):
    dma = pltpu.SemaphoreType.DMA
    return pl.pallas_call(
        functools.partial(press_kernel, rows=rows, cols=cols),
        out_shape=jax.ShapeDtypeStruct((4,) + press.shape, jnp.float32),
        in_specs=[VMEM],
        out_specs=VMEM,
        scratch_shapes=[dma((4,)), dma((4,))],
        compiler_params=pltpu.CompilerParams(collective_id=1, has_side_effects=True, vmem_limit_bytes=GRANT),
        name="press",
    )(press)


def density_call(plan, here, there):
    own_tiles, ghosts = here.shape[0] // 8, there.shape[0] // 8
    tiles = own_tiles + ghosts
    flat = jax.ShapeDtypeStruct((own_tiles, LANES), jnp.float32)
    return pl.pallas_call(
        density_kernel,
        out_shape=(
            flat,
            flat,
            jax.ShapeDtypeStruct((GT, LANES), jnp.float32),
            jax.ShapeDtypeStruct((tiles, LANES, DEPTH), jnp.bfloat16),
            jax.ShapeDtypeStruct((tiles * 8, LANES), jnp.float32),
            jax.ShapeDtypeStruct((ghosts, LANES), jnp.int32),
            jax.ShapeDtypeStruct((1,), jnp.int32),
        ),
        in_specs=[SMEM] + [VMEM] * 2,
        out_specs=(VMEM,) * 6 + (SMEM,),
        scratch_shapes=[
            pltpu.VMEM((own_tiles, DEPTH, LANES), jnp.bfloat16),
            pltpu.VMEM((tiles, LANES, LANES), jnp.float32),
            pltpu.VMEM((own_tiles + 1, max(8, ghosts), LANES), jnp.float32),
        ],
        compiler_params=pltpu.CompilerParams(vmem_limit_bytes=GRANT),
        name="density",
    )(plan, here, there)


def accel_call(plan, more, far, base, dest, press, press_far):
    own_tiles, ghosts = press.shape[0], dest.shape[0]
    return pl.pallas_call(
        accel_kernel,
        out_shape=jax.ShapeDtypeStruct((3, own_tiles * LANES), jnp.float32),
        in_specs=[SMEM] * 2 + [VMEM] * 5,
        out_specs=VMEM,
        scratch_shapes=[
            pltpu.VMEM((own_tiles, DEPTH, LANES), jnp.bfloat16),
            pltpu.VMEM((own_tiles, 16, 2 * LANES), jnp.bfloat16),
            pltpu.VMEM((2, 2, ghosts, 16, 2 * LANES), jnp.bfloat16),
            pltpu.VMEM((own_tiles + 1, 16, LANES), jnp.float32),
            pltpu.VMEM((own_tiles, LANES), jnp.float32),
            pltpu.VMEM((own_tiles + ghosts, LANES, LANES), jnp.float32),
        ],
        compiler_params=pltpu.CompilerParams(vmem_limit_bytes=GRANT),
        name="accel",
    )(plan, more, far, base, dest, press, press_far)


def as_tiles(blocks):
    count, fields, slots = blocks.shape
    per = LANES // slots
    joined = blocks.reshape(count // per, per, fields, slots).transpose(0, 2, 1, 3)
    return joined.reshape(count // per * fields, LANES)


def local(positions, mass, smoothing, energy, destination, pairs, pair_count):
    rows = lax.axis_size("gx")
    cols = lax.axis_size("gy")
    own_tiles = mass.shape[0] // LANES
    flat = (own_tiles, LANES)
    own, ghost, plan = exchange_call(
        pair_count, pairs, positions, mass.reshape(flat), smoothing.reshape(flat),
        energy.reshape(flat), destination.reshape(flat), rows, cols)
    plan = plan.reshape(-1)
    here = as_tiles(own)
    there = as_tiles(ghost.reshape((-1,) + ghost.shape[2:]))
    density, press, edge, far, base, dest, more = density_call(plan, here, there)
    press_far = press_call(edge, rows, cols).reshape(4 * GT, LANES)
    accel = accel_call(plan, more, far, base, dest, press, press_far)
    return (density.reshape(-1), accel)


def solution(mesh):
    placed = (
        P(None, ("gx", "gy")),
        P(("gx", "gy")),
        P(("gx", "gy")),
        P(("gx", "gy")),
        P(("gx", "gy"), None),
        P(None, ("gx", "gy")),
        P(("gx", "gy")),
    )
    return jax.shard_map(
        local,
        mesh=mesh,
        in_specs=placed,
        out_specs=(P(("gx", "gy")), P(None, ("gx", "gy"))),
        check_vma=False,
    )
```

```python
import functools
import math

import jax
import jax.numpy as jnp
from jax import lax
from jax.experimental import pallas as pl
from jax.experimental.pallas import tpu as pltpu
from jax.sharding import PartitionSpec as P

GT = 8
LANES = 128
DEPTH = 48
TINY = 1e-12
MESH = pl.DeviceIdType.MESH

KERNEL_NORM = 21.0 / (2.0 * math.pi)
GAMMA_LESS = 2.0 / 3.0


def three(x):
    one = x.astype(jnp.bfloat16).astype(jnp.float32)
    rest = x - one
    two = rest.astype(jnp.bfloat16).astype(jnp.float32)
    return one, two, (rest - two).astype(jnp.bfloat16).astype(jnp.float32)


def source_terms(x):
    one, two, low = three(x)
    return jnp.concatenate([one, two, one, two, low, one], axis=0).astype(jnp.bfloat16)


def target_terms(x):
    one, two, low = three(x)
    return jnp.concatenate([one, one, two, two, one, low], axis=0).astype(jnp.bfloat16)


def put_rows(stage, rows, width, tiles, first=0):
    for k, row in enumerate(rows):
        stage[pl.ds(first + k, tiles, stride=width), :] = row


def equal_rows(row, height, base=0):
    at = lax.broadcasted_iota(jnp.int32, (height, row.shape[-1]), 0) + base
    return jnp.broadcast_to(row, at.shape) == at


def ones_where(mask):
    return jnp.where(mask, 1.0, 0.0).astype(jnp.bfloat16)


def earlier(size, width):
    row = lax.broadcasted_iota(jnp.int32, (size, width), 0)
    col = lax.broadcasted_iota(jnp.int32, (size, width), 1)
    return row, col


def list_pairs(count_ref, pairs_ref, plan_ref, rank_ref, hits_ref, own_tiles, tiles):
    slots = pairs_ref.shape[1]
    live = lax.broadcasted_iota(jnp.int32, (1, slots), 1) < count_ref[0]
    target = jnp.where(live, pairs_ref[0:1, :], -1)
    hits = by_last(ones_where(equal_rows(target, own_tiles)),
                   ones_where(equal_rows(pairs_ref[1:2, :], tiles)))
    fresh = jnp.where(hits > 0.0, 1.0, 0.0)
    row, col = earlier(tiles, tiles)
    far_row, far_col = row >= own_tiles, col >= own_tiles
    inside = jnp.dot(fresh.astype(jnp.bfloat16), ones_where((row < col) & (far_row == far_col)),
                     preferred_element_type=jnp.float32)
    total = jnp.dot(fresh.astype(jnp.bfloat16), ones_where(far_row == far_col),
                    preferred_element_type=jnp.float32)
    row, col = earlier(own_tiles, own_tiles)
    above = jnp.dot(ones_where(col < row), total.astype(jnp.bfloat16),
                    preferred_element_type=jnp.float32)
    all_rows = jnp.sum(total, axis=0, keepdims=True).astype(jnp.int32)
    column = lax.broadcasted_iota(jnp.int32, (own_tiles, tiles), 1)
    place = jnp.where(hits > 0.0, (inside + above).astype(jnp.int32), -1)
    lists = (plan_ref.shape[0] - 2) // 4
    place = jnp.where((column >= own_tiles) & (place >= 0), place + lists * LANES, place)
    rank_ref[...] = place
    hits_ref[...] = hits.astype(jnp.int32)
    source = lax.broadcasted_iota(jnp.int32, (1, tiles), 1).astype(jnp.float32)
    keys = jnp.zeros((2 * lists, LANES), jnp.float32)
    times = jnp.zeros((2 * lists, LANES), jnp.float32)
    for t in range(own_tiles):
        at = rank_ref[t:t + 1, :]
        high = at // LANES
        many = hits_ref[t:t + 1, :]
        upper = many // LANES
        mine = jnp.where(equal_rows(jnp.where(at < 0, -1, high), 2 * lists), 1.0, 0.0)
        parts = [mine * source, mine, mine * upper.astype(jnp.float32),
                 mine * (many - upper * LANES).astype(jnp.float32)]
        found = by_last(jnp.concatenate(parts, axis=0).astype(jnp.bfloat16),
                        ones_where(equal_rows(jnp.where(at < 0, -1, at - high * LANES), LANES)))
        size = 2 * lists
        keys = keys + found[:size] + float(t * tiles) * found[size:2 * size]
        times = times + float(LANES) * found[2 * size:3 * size] + found[3 * size:]
    plan_ref[:2 * lists] = keys.astype(jnp.int32)
    plan_ref[2 * lists:4 * lists] = times.astype(jnp.int32)
    plan_ref[4 * lists:4 * lists + 1] = jnp.broadcast_to(all_rows[:, :1], (1, LANES))
    plan_ref[4 * lists + 1:] = jnp.broadcast_to(all_rows[:, tiles - 1:], (1, LANES))


def order_rows(pos_ref, mass_ref, smooth_ref, energy_ref, dest_ref, sent_ref,
               flags, prefix, rank_ref, rows_ref, index_ref):
    tiles = mass_ref.shape[0]
    domains, width, slots = sent_ref.shape
    row, col = earlier(LANES, 2 * LANES)
    before = ones_where((row < col) | (col >= LANES))
    for t in range(tiles):
        flags[t * domains:(t + 1) * domains] = ones_where(
            equal_rows(dest_ref[t:t + 1, :], domains))
    prefix[...] = jnp.dot(flags[...], before, preferred_element_type=jnp.float32)
    seen = jnp.zeros((domains, LANES), jnp.float32)
    for t in range(tiles):
        part = slice(t * domains, (t + 1) * domains)
        mine = flags[part].astype(jnp.float32)
        rank = jnp.sum(mine * (prefix[part, :LANES] + seen), axis=0, keepdims=True)
        rank_ref[t:t + 1, :] = rank.astype(jnp.int32)
        seen = seen + prefix[part, LANES:]
    place = dest_ref[...] * slots + rank_ref[...]
    block = place // LANES
    rank_ref[...] = place - block * LANES
    lane = lax.broadcasted_iota(jnp.int32, (tiles, LANES), 1).astype(jnp.float32)
    from_lane = jnp.zeros((tiles, LANES), jnp.float32)
    from_tile = jnp.zeros((tiles, LANES), jnp.float32)
    for t in range(tiles):
        picked = equal_rows(block[t:t + 1, :], tiles)
        both = jnp.concatenate([jnp.where(picked, lane, 0.0), jnp.where(picked, 1.0, 0.0)], axis=0)
        found = by_last(both.astype(jnp.bfloat16),
                        ones_where(equal_rows(rank_ref[t:t + 1, :], LANES)))
        from_lane = from_lane + found[:tiles]
        from_tile = from_tile + float(t) * found[tiles:]
    ones = jnp.ones((tiles, LANES), jnp.float32)
    put_rows(rows_ref, [smooth_ref[...], mass_ref[...], energy_ref[...], 0.0 * ones], width, tiles, 4)
    put_rows(rows_ref, [ones], width, tiles, 0)
    for t in range(tiles):
        rows_ref[t * width + 1:t * width + 4, :] = pos_ref[:, t * LANES:(t + 1) * LANES]
    index_ref[0] = from_lane.astype(jnp.int32)
    index_ref[1] = from_tile.astype(jnp.int32)
    per = LANES // slots

    def gather(q, carry):
        at = jnp.broadcast_to(index_ref[0, pl.ds(q, 1), :], (width, LANES))
        tile = jnp.broadcast_to(index_ref[1, pl.ds(q, 1), :], (width, LANES))
        out = jnp.zeros((width, LANES), jnp.float32)
        for t in range(tiles):
            moved = jnp.take_along_axis(rows_ref[t * width:(t + 1) * width, :], at, axis=1)
            out = jnp.where(tile == t, moved, out)
        for p in range(per):
            sent_ref[q * per + p] = out[:, p * slots:(p + 1) * slots]
        return carry

    lax.fori_loop(0, tiles, gather, 0)


def beside(i, j, rows, cols):
    return [(i > 0, (i - 1, j), 1), (i < rows - 1, (i + 1, j), 0),
            (j > 0, (i, j - 1), 3), (j < cols - 1, (i, j + 1), 2)]


def exchange_kernel(count_ref, *refs, rows, cols):
    given, refs = refs[:6], refs[6:]
    own_ref, ghost_ref, listed_ref = refs[:3]
    held, refs = refs[3:9], refs[9:]
    (out_ref, flags, prefix, rank_ref, rows_ref, index_ref, place_ref, hits_ref, plan_ref,
     load_sem, plan_sem, send_sem, recv_sem, edge_send, edge_recv) = refs
    pairs_ref, pos_ref, mass_ref, smooth_ref, energy_ref, dest_ref = held
    loads = [pltpu.make_async_copy(a, b, load_sem.at[k]) for k, (a, b) in enumerate(zip(given, held))]
    for load in loads:
        load.start()
    domains = rows * cols
    tiles = mass_ref.shape[0]
    edge = ghost_ref.shape[1]
    i, j = lax.axis_index("gx"), lax.axis_index("gy")
    me = i * cols + j
    barrier = pltpu.get_barrier_semaphore()

    def greet(k, carry):
        peer = lax.rem(me + k, domains)
        pl.semaphore_signal(barrier, inc=1, device_id=(peer // cols, lax.rem(peer, cols)),
                            device_id_type=MESH)
        return carry

    lax.fori_loop(1, domains, greet, 0)
    for load in loads:
        load.wait()
    order_rows(pos_ref, mass_ref, smooth_ref, energy_ref, dest_ref, out_ref,
               flags, prefix, rank_ref, rows_ref, index_ref)
    pl.semaphore_wait(barrier, domains - 1)

    def outgoing(peer):
        return pltpu.make_async_remote_copy(
            src_ref=out_ref.at[peer], dst_ref=own_ref.at[me],
            send_sem=send_sem.at[peer], recv_sem=recv_sem.at[me],
            device_id=(peer // cols, lax.rem(peer, cols)), device_id_type=MESH)

    def incoming(source):
        return pltpu.make_async_remote_copy(
            src_ref=out_ref.at[source], dst_ref=own_ref.at[source],
            send_sem=send_sem.at[source], recv_sem=recv_sem.at[source],
            device_id=(source // cols, lax.rem(source, cols)), device_id_type=MESH)

    def send(k, carry):
        outgoing(lax.rem(me + k, domains)).start()
        return carry

    lax.fori_loop(1, domains, send, 0)
    own_ref[me] = out_ref[me]
    list_pairs(count_ref, pairs_ref, plan_ref, place_ref, hits_ref, tiles, tiles + 4 * GT)
    listed = pltpu.make_async_copy(plan_ref, listed_ref, plan_sem)
    listed.start()

    def arrive(source, carry):
        @pl.when(source != me)
        def _():
            incoming(source).wait_recv()
        return carry

    lax.fori_loop(0, edge, arrive, 0)
    sides = beside(i, j, rows, cols)

    def across(side):
        there, peer, slot = sides[side]
        return pltpu.make_async_remote_copy(
            src_ref=own_ref.at[pl.ds(0, edge)], dst_ref=ghost_ref.at[slot],
            send_sem=edge_send.at[side], recv_sem=edge_recv.at[slot],
            device_id=peer, device_id_type=MESH)

    def back(side):
        there, peer, slot = sides[side]
        return pltpu.make_async_remote_copy(
            src_ref=own_ref.at[pl.ds(0, edge)], dst_ref=ghost_ref.at[side],
            send_sem=edge_send.at[side], recv_sem=edge_recv.at[side],
            device_id=peer, device_id_type=MESH)

    for side in range(4):
        @pl.when(sides[side][0])
        def _():
            across(side).start()

        @pl.when(jnp.logical_not(sides[side][0]))
        def _():
            ghost_ref[side] = jnp.zeros_like(ghost_ref[side])

    lax.fori_loop(edge, domains, arrive, 0)

    def left(k, carry):
        outgoing(lax.rem(me + k, domains)).wait_send()
        return carry

    lax.fori_loop(1, domains, left, 0)
    for side in range(4):
        @pl.when(sides[side][0])
        def _():
            across(side).wait_send()
            back(side).wait_recv()

    listed.wait()


def press_kernel(press_ref, ghost_ref, send_sem, recv_sem, rows, cols):
    i, j = lax.axis_index("gx"), lax.axis_index("gy")
    sides = beside(i, j, rows, cols)
    barrier = pltpu.get_barrier_semaphore()
    for there, peer, slot in sides:
        @pl.when(there)
        def _():
            pl.semaphore_signal(barrier, inc=1, device_id=peer, device_id_type=MESH)

    pl.semaphore_wait(barrier, sum(there.astype(jnp.int32) for there, peer, slot in sides))

    def across(side, slot):
        return pltpu.make_async_remote_copy(
            src_ref=press_ref, dst_ref=ghost_ref.at[slot],
            send_sem=send_sem.at[side], recv_sem=recv_sem.at[slot],
            device_id=sides[side][1], device_id_type=MESH)

    for side in range(4):
        @pl.when(sides[side][0])
        def _():
            across(side, sides[side][2]).start()

        @pl.when(jnp.logical_not(sides[side][0]))
        def _():
            ghost_ref[side] = jnp.zeros_like(ghost_ref[side])

    for side in range(4):
        @pl.when(sides[side][0])
        def _():
            across(side, sides[side][2]).wait_send()
            across(side, side).wait_recv()


def one_hot_rows(dest):
    rows = lax.broadcasted_iota(jnp.int32, (LANES, LANES), 0)
    wide = jnp.broadcast_to(dest, (LANES, LANES))
    return jnp.where(wide == rows, 1.0, 0.0).astype(jnp.bfloat16)


def by_last(a, b):
    return lax.dot_general(a, b, (((1,), (1,)), ((), ())), preferred_element_type=jnp.float32)


def sweep(plan_ref, which, tiles, dump, unrolls, together, body):
    length = (plan_ref.shape[0] - 2 * LANES) // 4
    size = plan_ref[4 * length + which * LANES]

    done = 0
    for unroll in unrolls:
        final = unroll == unrolls[-1]

        def advance(block, carry):
            for u in range(0, unroll, together):
                picked = []
                for v in range(together):
                    k = done + block * unroll + u + v
                    if final:
                        live = k < size
                        at = which * length + jnp.minimum(k, length - 1)
                        key = jnp.where(live, plan_ref[at], 0)
                    else:
                        at = which * length + k
                        key = plan_ref[at]
                    target = lax.div(key, tiles)
                    source = key - target * tiles
                    weight = plan_ref[2 * length + at].astype(jnp.float32)
                    place = jnp.where(live, target, dump) if final else target
                    picked.append((target, source, place, weight))
                body(picked)
            return carry

        blocks = lax.div(size - done + (unroll - 1 if final else 0), unroll)
        lax.fori_loop(0, blocks, advance, 0)
        done = done + blocks * unroll


def in_groups(count, group, body):
    def step(block, carry):
        for u in range(group):
            body(block * group + u)
        return carry

    lax.fori_loop(0, count // group, step, 0)


def tile_rows(ref, t, height=8):
    return ref[pl.ds(pl.multiple_of(t * height, height), height), :]


def put_tile(ref, t, value):
    ref[pl.ds(pl.multiple_of(t * 8, 8), 8), :] = value


def spread_row(far, k, wide, tiles, scale):
    row = lax.broadcasted_iota(jnp.int32, (DEPTH, LANES), 0)
    pick = jnp.where((row == k) | (row == 8 + k) | (row == 32 + k), scale, 0.0).astype(jnp.bfloat16)

    def one(t):
        wide[t] = jnp.dot(far[t], pick, preferred_element_type=jnp.float32)

    in_groups(tiles, 8, one)


def density_kernel(plan_ref, here_ref, there_ref,
                   dens_ref, press_ref, edge_ref, far, base_ref, dest_ref, more_ref,
                   near, mass_b, totals):
    own_tiles = dens_ref.shape[0]
    ghosts = dest_ref.shape[0]
    tiles = own_tiles + ghosts
    row = lax.broadcasted_iota(jnp.int32, (8, LANES), 0)
    spatial = (row >= 1) & (row <= 3)
    first = here_ref[0:8, :]
    low, high, most = first, first, there_ref[0:8, :]
    for t in range(1, own_tiles):
        part = here_ref[t * 8:(t + 1) * 8, :]
        low, high = jnp.minimum(low, part), jnp.maximum(high, part)
    for g in range(1, ghosts):
        most = jnp.maximum(most, there_ref[g * 8:(g + 1) * 8, :])
    low = jnp.min(low, axis=1, keepdims=True)
    high = jnp.max(high, axis=1, keepdims=True)
    most = jnp.maximum(jnp.max(most, axis=1, keepdims=True), high)
    reach = most[4:5, :] + 0.01
    reach = reach * reach
    centre = jnp.where(spatial, 0.5 * (low + high), 0.0)

    def shifted(part):
        moved = part - centre
        norm = jnp.sum(jnp.where(spatial, moved * moved, 0.0), axis=0, keepdims=True)
        return jnp.where(row == 7, norm, moved), norm

    def own(t):
        moved, norm = shifted(tile_rows(here_ref, t))
        put_tile(base_ref, t, moved)
        far[t] = by_last(ones_where(equal_rows(same, LANES)),
                         source_terms(moved)).astype(jnp.bfloat16)
        radius = moved[4:5, :]
        wanted = jnp.where(row == 0, norm, jnp.where(spatial, -2.0 * moved, jnp.where(
            row == 7, 1.0, 0.0)))
        near[t] = target_terms(wanted * (1.0 / (radius * radius)))

    same = lax.broadcasted_iota(jnp.int32, (1, LANES), 1)
    in_groups(own_tiles, 8, own)

    def ghost(g):
        part = tile_rows(there_ref, g)
        gap = jnp.maximum(jnp.maximum(low - part, part - high), 0.0)
        beyond = jnp.sum(jnp.where(spatial, gap * gap, 0.0), axis=0, keepdims=True)
        active = (beyond < reach) & (part[5:6, :] != 0.0)
        totals[0, pl.ds(g, 1), :] = jnp.where(active, 1.0, 0.0)
        moved, norm = shifted(part)
        put_tile(base_ref, own_tiles + g, moved)

    in_groups(ghosts, 8, ghost)
    flags = totals[0, :ghosts, :]
    at, upto = earlier(LANES, LANES)
    rank = jnp.dot(flags.astype(jnp.bfloat16), ones_where(at <= upto),
                   preferred_element_type=jnp.float32)
    dest_ref[...] = jnp.where(flags > 0.0, rank - 1.0, -1.0).astype(jnp.int32)
    totals[0, :ghosts, :] = rank
    slot = lax.broadcasted_iota(jnp.int32, (LANES, DEPTH), 0).astype(jnp.float32)
    term = lax.broadcasted_iota(jnp.int32, (LANES, DEPTH), 1)
    unit = (term == 0) | (term == 16) | (term == 40)
    more = (jnp.max(rank) > LANES // 2 + 0.5).astype(jnp.int32)
    more_ref[0] = more

    def squeeze(g):
        moved = by_last(ones_where(equal_rows(dest_ref[pl.ds(g, 1), :], LANES)),
                        source_terms(tile_rows(base_ref, own_tiles + g)))
        unused = slot >= totals[0, pl.ds(g, 1), LANES - 1:]
        far[own_tiles + g] = jnp.where(unit & unused, 1.0, moved).astype(jnp.bfloat16)

    in_groups(ghosts, 8, squeeze)
    spread_row(far, 5, mass_b, tiles, 1.0)
    totals[...] = jnp.zeros_like(totals)

    def add(first, height):
        def body(picked):
            (target, source, place, weight), = picked
            sq = jnp.dot(far[source, first:first + height], near[target],
                         preferred_element_type=jnp.float32)
            sq = jnp.maximum(sq, TINY)
            ratio = sq * lax.rsqrt(sq)
            falloff = jnp.maximum(1.0 - ratio, 0.0)
            falloff = falloff * falloff
            term = falloff * falloff * ((ratio + 0.25) * mass_b[source, first:first + height])
            summed = jnp.sum(term.reshape(height // 8, 8, LANES), axis=0)
            totals[place, :8] += weight * summed
        return body

    half = LANES // 2
    sweep(plan_ref, 0, tiles, own_tiles, (48, 8), 1, add(0, LANES))
    sweep(plan_ref, 1, tiles, own_tiles, (96, 16), 1, add(0, half))

    @pl.when(more > 0)
    def _():
        sweep(plan_ref, 1, tiles, own_tiles, (4,), 1, add(half, half))

    def field(k):
        return here_ref[pl.ds(k, own_tiles, stride=8), :]

    summed = jnp.sum(totals[:own_tiles, :8], axis=1)
    radius = field(4)
    density = KERNEL_NORM / (radius * radius * radius) * (4.0 * summed + field(5))
    dens_ref[...] = density
    press = GAMMA_LESS * field(6) / density
    press_ref[...] = press
    edge_ref[...] = press[:GT]


def accel_kernel(plan_ref, more_ref, far, base_ref, dest_ref,
                 press_ref, press_far_ref, out_ref, near, left, left_half, totals, half_a, half_b):
    own_tiles = press_ref.shape[0]
    ghosts = dest_ref.shape[0]
    tiles = own_tiles + ghosts
    half = LANES // 2
    row = lax.broadcasted_iota(jnp.int32, (8, LANES), 0)
    spatial = (row >= 1) & (row <= 3)

    def loaded(part, press):
        twice = jnp.where(row < 4, part, pltpu.roll(part, 4, 0)) * part[5:6, :]
        one, two, low = three(jnp.where(row < 4, twice, twice * press))
        return jnp.concatenate([one, two], axis=0).astype(jnp.bfloat16)

    def own(t):
        part = tile_rows(base_ref, t)
        wanted = jnp.where(row == 0, part[7:8, :], jnp.where(spatial, -2.0 * part, jnp.where(
            row == 7, 1.0, 0.0)))
        half_a[pl.ds(t, 1), :] = 0.5 * part[4:5, :]
        near[t] = target_terms(wanted)
        rows = loaded(part, press_ref[pl.ds(t, 1), :])
        left[t] = jnp.concatenate([rows, rows], axis=1)

    in_groups(own_tiles, 8, own)

    def ghost(g):
        rows = loaded(tile_rows(base_ref, own_tiles + g), press_far_ref[pl.ds(g, 1), :])
        moved = by_last(rows, ones_where(equal_rows(dest_ref[pl.ds(g, 1), :], LANES)))
        moved = moved.astype(jnp.bfloat16)
        none = jnp.zeros((16, LANES), jnp.bfloat16)
        for v in range(2):
            piece = moved[:, v * half:(v + 1) * half]
            two = jnp.concatenate([piece, piece], axis=1)
            left_half[v, 0, g] = jnp.concatenate([two, none], axis=1)
            left_half[v, 1, g] = jnp.concatenate([none, two], axis=1)

    in_groups(ghosts, 8, ghost)
    spread_row(far, 4, half_b, tiles, 0.5)
    totals[...] = jnp.zeros_like(totals)

    def slopes(source, target, first, height):
        sq = jnp.dot(far[source, first:first + height], near[target],
                     preferred_element_type=jnp.float32)
        radius = half_b[source, first:first + height] + half_a[pl.ds(target, 1), :]
        sq = jnp.maximum(sq, TINY)
        dist = sq * lax.rsqrt(sq)
        inv = pl.reciprocal(radius, approx=True)
        wide = inv * inv
        fall = jnp.maximum(inv - dist * wide, 0.0)
        slope = fall * fall * (fall * wide)
        high = slope.astype(jnp.bfloat16)
        low = (slope - high.astype(jnp.float32)).astype(jnp.bfloat16)
        return [high, low]

    def add_one(picked):
        (target, source, place, weight), = picked
        terms = jnp.concatenate(slopes(source, target, 0, LANES), axis=0)
        totals[place] += weight * jnp.dot(left[source], terms, preferred_element_type=jnp.float32)

    def add_two(v):
        def body(both):
            terms, lhs = [], []
            for side, (target, source, place, weight) in enumerate(both):
                terms += slopes(source, target, v * half, half)
                lhs.append(left_half[v, side, jnp.maximum(source - own_tiles, 0)])
            moved = jnp.dot(jnp.concatenate(lhs, axis=0), jnp.concatenate(terms, axis=0),
                            preferred_element_type=jnp.float32)
            for side, (target, source, place, weight) in enumerate(both):
                totals[place] += weight * moved[side * 16:(side + 1) * 16]
        return body

    sweep(plan_ref, 0, tiles, own_tiles, (32,), 1, add_one)
    sweep(plan_ref, 1, tiles, own_tiles, (64,), 2, add_two(0))

    @pl.when(more_ref[0] > 0)
    def _():
        sweep(plan_ref, 1, tiles, own_tiles, (4,), 2, add_two(1))

    for t in range(own_tiles):
        both = totals[t, :8] + totals[t, 8:]
        mixed = jnp.where(row < 4, both * press_ref[t:t + 1, :], both)
        mixed = mixed + pltpu.roll(mixed, 4, 0)
        pulled = 20.0 * KERNEL_NORM * (base_ref[t * 8:(t + 1) * 8, :] * mixed[0:1, :] - mixed)
        out_ref[:, t * LANES:(t + 1) * LANES] = pulled[1:4, :]


SMEM = pl.BlockSpec(memory_space=pltpu.SMEM)
VMEM = pl.BlockSpec(memory_space=pltpu.VMEM)
HBM = pl.BlockSpec(memory_space=pltpu.HBM)
GRANT = 60 * 2 ** 20


def exchange_call(count, pairs, positions, mass, smoothing, energy, destination, rows, cols):
    tiles = mass.shape[0]
    pool_tiles = tiles + 4 * GT
    lists = 2 * pl.cdiv(tiles * max(tiles, 4 * GT), LANES)
    domains = rows * cols
    slots = tiles * LANES // domains
    edge = GT * LANES // slots
    dma = pltpu.SemaphoreType.DMA
    given = (pairs, positions, mass, smoothing, energy, destination)
    return pl.pallas_call(
        functools.partial(exchange_kernel, rows=rows, cols=cols),
        out_shape=(
            jax.ShapeDtypeStruct((domains, 8, slots), jnp.float32),
            jax.ShapeDtypeStruct((4, edge, 8, slots), jnp.float32),
            jax.ShapeDtypeStruct((2 * lists + 2, LANES), jnp.int32),
        ),
        in_specs=[SMEM] + [HBM] * 6,
        out_specs=[VMEM] * 2 + [HBM],
        scratch_shapes=[pltpu.VMEM(x.shape, x.dtype) for x in given] + [
            pltpu.VMEM((domains, 8, slots), jnp.float32),
            pltpu.VMEM((tiles * domains, LANES), jnp.bfloat16),
            pltpu.VMEM((tiles * domains, 2 * LANES), jnp.float32),
            pltpu.VMEM((tiles, LANES), jnp.int32),
            pltpu.VMEM((tiles * 8, LANES), jnp.float32),
            pltpu.VMEM((2, tiles, LANES), jnp.int32),
            pltpu.VMEM((tiles, pool_tiles), jnp.int32),
            pltpu.VMEM((tiles, pool_tiles), jnp.int32),
            pltpu.VMEM((2 * lists + 2, LANES), jnp.int32),
            dma((6,)), dma, dma((domains,)), dma((domains,)), dma((4,)), dma((4,)),
        ],
        compiler_params=pltpu.CompilerParams(
            collective_id=0, has_side_effects=True, vmem_limit_bytes=GRANT),
        name="exchange",
    )(count, *given)


def press_call(press, rows, cols):
    dma = pltpu.SemaphoreType.DMA
    return pl.pallas_call(
        functools.partial(press_kernel, rows=rows, cols=cols),
        out_shape=jax.ShapeDtypeStruct((4,) + press.shape, jnp.float32),
        in_specs=[VMEM],
        out_specs=VMEM,
        scratch_shapes=[dma((4,)), dma((4,))],
        compiler_params=pltpu.CompilerParams(collective_id=1, has_side_effects=True, vmem_limit_bytes=GRANT),
        name="press",
    )(press)


def density_call(plan, here, there):
    own_tiles, ghosts = here.shape[0] // 8, there.shape[0] // 8
    tiles = own_tiles + ghosts
    flat = jax.ShapeDtypeStruct((own_tiles, LANES), jnp.float32)
    return pl.pallas_call(
        density_kernel,
        out_shape=(
            flat,
            flat,
            jax.ShapeDtypeStruct((GT, LANES), jnp.float32),
            jax.ShapeDtypeStruct((tiles, LANES, DEPTH), jnp.bfloat16),
            jax.ShapeDtypeStruct((tiles * 8, LANES), jnp.float32),
            jax.ShapeDtypeStruct((ghosts, LANES), jnp.int32),
            jax.ShapeDtypeStruct((1,), jnp.int32),
        ),
        in_specs=[SMEM] + [VMEM] * 2,
        out_specs=(VMEM,) * 6 + (SMEM,),
        scratch_shapes=[
            pltpu.VMEM((own_tiles, DEPTH, LANES), jnp.bfloat16),
            pltpu.VMEM((tiles, LANES, LANES), jnp.float32),
            pltpu.VMEM((own_tiles + 1, max(8, ghosts), LANES), jnp.float32),
        ],
        compiler_params=pltpu.CompilerParams(vmem_limit_bytes=GRANT),
        name="density",
    )(plan, here, there)


def accel_call(plan, more, far, base, dest, press, press_far):
    own_tiles, ghosts = press.shape[0], dest.shape[0]
    return pl.pallas_call(
        accel_kernel,
        out_shape=jax.ShapeDtypeStruct((3, own_tiles * LANES), jnp.float32),
        in_specs=[SMEM] * 2 + [VMEM] * 5,
        out_specs=VMEM,
        scratch_shapes=[
            pltpu.VMEM((own_tiles, DEPTH, LANES), jnp.bfloat16),
            pltpu.VMEM((own_tiles, 16, 2 * LANES), jnp.bfloat16),
            pltpu.VMEM((2, 2, ghosts, 16, 2 * LANES), jnp.bfloat16),
            pltpu.VMEM((own_tiles + 1, 16, LANES), jnp.float32),
            pltpu.VMEM((own_tiles, LANES), jnp.float32),
            pltpu.VMEM((own_tiles + ghosts, LANES, LANES), jnp.float32),
        ],
        compiler_params=pltpu.CompilerParams(vmem_limit_bytes=GRANT),
        name="accel",
    )(plan, more, far, base, dest, press, press_far)


def as_tiles(blocks):
    count, fields, slots = blocks.shape
    per = LANES // slots
    joined = blocks.reshape(count // per, per, fields, slots).transpose(0, 2, 1, 3)
    return joined.reshape(count // per * fields, LANES)


def local(positions, mass, smoothing, energy, destination, pairs, pair_count):
    rows = lax.axis_size("gx")
    cols = lax.axis_size("gy")
    own_tiles = mass.shape[0] // LANES
    flat = (own_tiles, LANES)
    own, ghost, plan = exchange_call(
        pair_count, pairs, positions, mass.reshape(flat), smoothing.reshape(flat),
        energy.reshape(flat), destination.reshape(flat), rows, cols)
    plan = plan.reshape(-1)
    here = as_tiles(own)
    there = as_tiles(ghost.reshape((-1,) + ghost.shape[2:]))
    density, press, edge, far, base, dest, more = density_call(plan, here, there)
    press_far = press_call(edge, rows, cols).reshape(4 * GT, LANES)
    accel = accel_call(plan, more, far, base, dest, press, press_far)
    return (density.reshape(-1), accel)


def solution(mesh):
    placed = (
        P(None, ("gx", "gy")),
        P(("gx", "gy")),
        P(("gx", "gy")),
        P(("gx", "gy")),
        P(("gx", "gy"), None),
        P(None, ("gx", "gy")),
        P(("gx", "gy")),
    )
    return jax.shard_map(
        local,
        mesh=mesh,
        in_specs=placed,
        out_specs=(P(("gx", "gy")), P(None, ("gx", "gy"))),
        check_vma=False,
    )
```

```python
import functools
import math

import jax
import jax.numpy as jnp
from jax import lax
from jax.experimental import pallas as pl
from jax.experimental.pallas import tpu as pltpu
from jax.sharding import PartitionSpec as P

GT = 8
LANES = 128
DEPTH = 48
TINY = 1e-12
MESH = pl.DeviceIdType.MESH

KERNEL_NORM = 21.0 / (2.0 * math.pi)
GAMMA_LESS = 2.0 / 3.0


def three(x):
    one = x.astype(jnp.bfloat16).astype(jnp.float32)
    rest = x - one
    two = rest.astype(jnp.bfloat16).astype(jnp.float32)
    return one, two, (rest - two).astype(jnp.bfloat16).astype(jnp.float32)


def source_terms(x):
    one, two, low = three(x)
    return jnp.concatenate([one, two, one, two, low, one], axis=0).astype(jnp.bfloat16)


def target_terms(x):
    one, two, low = three(x)
    return jnp.concatenate([one, one, two, two, one, low], axis=0).astype(jnp.bfloat16)


def put_rows(stage, rows, width, tiles, first=0):
    for k, row in enumerate(rows):
        stage[pl.ds(first + k, tiles, stride=width), :] = row


def equal_rows(row, height, base=0):
    at = lax.broadcasted_iota(jnp.int32, (height, row.shape[-1]), 0) + base
    return jnp.broadcast_to(row, at.shape) == at


def ones_where(mask):
    return jnp.where(mask, 1.0, 0.0).astype(jnp.bfloat16)


def earlier(size, width):
    row = lax.broadcasted_iota(jnp.int32, (size, width), 0)
    col = lax.broadcasted_iota(jnp.int32, (size, width), 1)
    return row, col


def list_pairs(count_ref, pairs_ref, plan_ref, rank_ref, hits_ref, own_tiles, tiles):
    slots = pairs_ref.shape[1]
    live = lax.broadcasted_iota(jnp.int32, (1, slots), 1) < count_ref[0]
    target = jnp.where(live, pairs_ref[0:1, :], -1)
    hits = by_last(ones_where(equal_rows(target, own_tiles)),
                   ones_where(equal_rows(pairs_ref[1:2, :], tiles)))
    fresh = jnp.where(hits > 0.0, 1.0, 0.0)
    row, col = earlier(tiles, tiles)
    far_row, far_col = row >= own_tiles, col >= own_tiles
    inside = jnp.dot(fresh.astype(jnp.bfloat16), ones_where((row < col) & (far_row == far_col)),
                     preferred_element_type=jnp.float32)
    total = jnp.dot(fresh.astype(jnp.bfloat16), ones_where(far_row == far_col),
                    preferred_element_type=jnp.float32)
    row, col = earlier(own_tiles, own_tiles)
    above = jnp.dot(ones_where(col < row), total.astype(jnp.bfloat16),
                    preferred_element_type=jnp.float32)
    all_rows = jnp.sum(total, axis=0, keepdims=True).astype(jnp.int32)
    column = lax.broadcasted_iota(jnp.int32, (own_tiles, tiles), 1)
    place = jnp.where(hits > 0.0, (inside + above).astype(jnp.int32), -1)
    lists = (plan_ref.shape[0] - 2) // 4
    place = jnp.where((column >= own_tiles) & (place >= 0), place + lists * LANES, place)
    rank_ref[...] = place
    hits_ref[...] = hits.astype(jnp.int32)
    source = lax.broadcasted_iota(jnp.int32, (1, tiles), 1).astype(jnp.float32)
    keys = jnp.zeros((2 * lists, LANES), jnp.float32)
    times = jnp.zeros((2 * lists, LANES), jnp.float32)
    for t in range(own_tiles):
        at = rank_ref[t:t + 1, :]
        high = at // LANES
        many = hits_ref[t:t + 1, :]
        upper = many // LANES
        mine = jnp.where(equal_rows(jnp.where(at < 0, -1, high), 2 * lists), 1.0, 0.0)
        parts = [mine * source, mine, mine * upper.astype(jnp.float32),
                 mine * (many - upper * LANES).astype(jnp.float32)]
        found = by_last(jnp.concatenate(parts, axis=0).astype(jnp.bfloat16),
                        ones_where(equal_rows(jnp.where(at < 0, -1, at - high * LANES), LANES)))
        size = 2 * lists
        keys = keys + found[:size] + float(t * tiles) * found[size:2 * size]
        times = times + float(LANES) * found[2 * size:3 * size] + found[3 * size:]
    plan_ref[:2 * lists] = keys.astype(jnp.int32)
    plan_ref[2 * lists:4 * lists] = times.astype(jnp.int32)
    plan_ref[4 * lists:4 * lists + 1] = jnp.broadcast_to(all_rows[:, :1], (1, LANES))
    plan_ref[4 * lists + 1:] = jnp.broadcast_to(all_rows[:, tiles - 1:], (1, LANES))


def order_rows(pos_ref, mass_ref, smooth_ref, energy_ref, dest_ref, sent_ref,
               flags, prefix, rank_ref, rows_ref, index_ref):
    tiles = mass_ref.shape[0]
    domains, width, slots = sent_ref.shape
    row, col = earlier(LANES, 2 * LANES)
    before = ones_where((row < col) | (col >= LANES))
    for t in range(tiles):
        flags[t * domains:(t + 1) * domains] = ones_where(
            equal_rows(dest_ref[t:t + 1, :], domains))
    prefix[...] = jnp.dot(flags[...], before, preferred_element_type=jnp.float32)
    seen = jnp.zeros((domains, LANES), jnp.float32)
    for t in range(tiles):
        part = slice(t * domains, (t + 1) * domains)
        mine = flags[part].astype(jnp.float32)
        rank = jnp.sum(mine * (prefix[part, :LANES] + seen), axis=0, keepdims=True)
        rank_ref[t:t + 1, :] = rank.astype(jnp.int32)
        seen = seen + prefix[part, LANES:]
    place = dest_ref[...] * slots + rank_ref[...]
    block = place // LANES
    rank_ref[...] = place - block * LANES
    lane = lax.broadcasted_iota(jnp.int32, (tiles, LANES), 1).astype(jnp.float32)
    from_lane = jnp.zeros((tiles, LANES), jnp.float32)
    from_tile = jnp.zeros((tiles, LANES), jnp.float32)
    for t in range(tiles):
        picked = equal_rows(block[t:t + 1, :], tiles)
        both = jnp.concatenate([jnp.where(picked, lane, 0.0), jnp.where(picked, 1.0, 0.0)], axis=0)
        found = by_last(both.astype(jnp.bfloat16),
                        ones_where(equal_rows(rank_ref[t:t + 1, :], LANES)))
        from_lane = from_lane + found[:tiles]
        from_tile = from_tile + float(t) * found[tiles:]
    ones = jnp.ones((tiles, LANES), jnp.float32)
    put_rows(rows_ref, [smooth_ref[...], mass_ref[...], energy_ref[...], 0.0 * ones], width, tiles, 4)
    put_rows(rows_ref, [ones], width, tiles, 0)
    for t in range(tiles):
        rows_ref[t * width + 1:t * width + 4, :] = pos_ref[:, t * LANES:(t + 1) * LANES]
    index_ref[0] = from_lane.astype(jnp.int32)
    index_ref[1] = from_tile.astype(jnp.int32)
    per = LANES // slots

    def gather(q, carry):
        at = jnp.broadcast_to(index_ref[0, pl.ds(q, 1), :], (width, LANES))
        tile = jnp.broadcast_to(index_ref[1, pl.ds(q, 1), :], (width, LANES))
        out = jnp.zeros((width, LANES), jnp.float32)
        for t in range(tiles):
            moved = jnp.take_along_axis(rows_ref[t * width:(t + 1) * width, :], at, axis=1)
            out = jnp.where(tile == t, moved, out)
        for p in range(per):
            sent_ref[q * per + p] = out[:, p * slots:(p + 1) * slots]
        return carry

    lax.fori_loop(0, tiles, gather, 0)


def beside(i, j, rows, cols):
    return [(i > 0, (i - 1, j), 1), (i < rows - 1, (i + 1, j), 0),
            (j > 0, (i, j - 1), 3), (j < cols - 1, (i, j + 1), 2)]


def exchange_kernel(count_ref, *refs, rows, cols):
    given, refs = refs[:6], refs[6:]
    pool_ref, listed_ref = refs[:2]
    held, refs = refs[2:8], refs[8:]
    (out_ref, flags, prefix, rank_ref, rows_ref, index_ref, place_ref, hits_ref, plan_ref,
     load_sem, plan_sem, send_sem, recv_sem, edge_send, edge_recv) = refs
    pairs_ref, pos_ref, mass_ref, smooth_ref, energy_ref, dest_ref = held
    loads = [pltpu.make_async_copy(a, b, load_sem.at[k]) for k, (a, b) in enumerate(zip(given, held))]
    for load in loads:
        load.start()
    domains = rows * cols
    tiles = mass_ref.shape[0]
    edge = (pool_ref.shape[0] - domains) // 4
    i, j = lax.axis_index("gx"), lax.axis_index("gy")
    me = i * cols + j
    barrier = pltpu.get_barrier_semaphore()

    def greet(k, carry):
        peer = lax.rem(me + k, domains)
        pl.semaphore_signal(barrier, inc=1, device_id=(peer // cols, lax.rem(peer, cols)),
                            device_id_type=MESH)
        return carry

    lax.fori_loop(1, domains, greet, 0)
    for load in loads:
        load.wait()
    order_rows(pos_ref, mass_ref, smooth_ref, energy_ref, dest_ref, out_ref,
               flags, prefix, rank_ref, rows_ref, index_ref)
    pl.semaphore_wait(barrier, domains - 1)

    def outgoing(peer):
        return pltpu.make_async_remote_copy(
            src_ref=out_ref.at[peer], dst_ref=pool_ref.at[me],
            send_sem=send_sem.at[peer], recv_sem=recv_sem.at[me],
            device_id=(peer // cols, lax.rem(peer, cols)), device_id_type=MESH)

    def incoming(source):
        return pltpu.make_async_remote_copy(
            src_ref=out_ref.at[source], dst_ref=pool_ref.at[source],
            send_sem=send_sem.at[source], recv_sem=recv_sem.at[source],
            device_id=(source // cols, lax.rem(source, cols)), device_id_type=MESH)

    def send(k, carry):
        outgoing(lax.rem(me + k, domains)).start()
        return carry

    lax.fori_loop(1, domains, send, 0)
    pool_ref[me] = out_ref[me]
    list_pairs(count_ref, pairs_ref, plan_ref, place_ref, hits_ref, tiles, tiles + 4 * GT)
    listed = pltpu.make_async_copy(plan_ref, listed_ref, plan_sem)
    listed.start()

    def arrive(source, carry):
        @pl.when(source != me)
        def _():
            incoming(source).wait_recv()
        return carry

    lax.fori_loop(0, edge, arrive, 0)
    sides = beside(i, j, rows, cols)

    def across(side):
        there, peer, slot = sides[side]
        return pltpu.make_async_remote_copy(
            src_ref=pool_ref.at[pl.ds(0, edge)], dst_ref=pool_ref.at[pl.ds(domains + slot * edge, edge)],
            send_sem=edge_send.at[side], recv_sem=edge_recv.at[slot],
            device_id=peer, device_id_type=MESH)

    def back(side):
        there, peer, slot = sides[side]
        return pltpu.make_async_remote_copy(
            src_ref=pool_ref.at[pl.ds(0, edge)], dst_ref=pool_ref.at[pl.ds(domains + side * edge, edge)],
            send_sem=edge_send.at[side], recv_sem=edge_recv.at[side],
            device_id=peer, device_id_type=MESH)

    for side in range(4):
        @pl.when(sides[side][0])
        def _():
            across(side).start()

        @pl.when(jnp.logical_not(sides[side][0]))
        def _():
            pool_ref[domains + side * edge:domains + (side + 1) * edge] = jnp.zeros(
                (edge,) + pool_ref.shape[1:], jnp.float32)

    lax.fori_loop(edge, domains, arrive, 0)

    def left(k, carry):
        outgoing(lax.rem(me + k, domains)).wait_send()
        return carry

    lax.fori_loop(1, domains, left, 0)
    for side in range(4):
        @pl.when(sides[side][0])
        def _():
            across(side).wait_send()
            back(side).wait_recv()

    listed.wait()


def press_kernel(press_ref, ghost_ref, send_sem, recv_sem, rows, cols):
    i, j = lax.axis_index("gx"), lax.axis_index("gy")
    sides = beside(i, j, rows, cols)
    barrier = pltpu.get_barrier_semaphore()
    for there, peer, slot in sides:
        @pl.when(there)
        def _():
            pl.semaphore_signal(barrier, inc=1, device_id=peer, device_id_type=MESH)

    pl.semaphore_wait(barrier, sum(there.astype(jnp.int32) for there, peer, slot in sides))

    def across(side, slot):
        return pltpu.make_async_remote_copy(
            src_ref=press_ref, dst_ref=ghost_ref.at[slot],
            send_sem=send_sem.at[side], recv_sem=recv_sem.at[slot],
            device_id=sides[side][1], device_id_type=MESH)

    for side in range(4):
        @pl.when(sides[side][0])
        def _():
            across(side, sides[side][2]).start()

        @pl.when(jnp.logical_not(sides[side][0]))
        def _():
            ghost_ref[side] = jnp.zeros_like(ghost_ref[side])

    for side in range(4):
        @pl.when(sides[side][0])
        def _():
            across(side, sides[side][2]).wait_send()
            across(side, side).wait_recv()


def one_hot_rows(dest):
    rows = lax.broadcasted_iota(jnp.int32, (LANES, LANES), 0)
    wide = jnp.broadcast_to(dest, (LANES, LANES))
    return jnp.where(wide == rows, 1.0, 0.0).astype(jnp.bfloat16)


def by_last(a, b):
    return lax.dot_general(a, b, (((1,), (1,)), ((), ())), preferred_element_type=jnp.float32)


def sweep(plan_ref, which, tiles, dump, unrolls, together, body):
    length = (plan_ref.shape[0] - 2 * LANES) // 4
    size = plan_ref[4 * length + which * LANES]

    done = 0
    for unroll in unrolls:
        final = unroll == unrolls[-1]

        def advance(block, carry):
            for u in range(0, unroll, together):
                picked = []
                for v in range(together):
                    k = done + block * unroll + u + v
                    if final:
                        live = k < size
                        at = which * length + jnp.minimum(k, length - 1)
                        key = jnp.where(live, plan_ref[at], 0)
                    else:
                        at = which * length + k
                        key = plan_ref[at]
                    target = lax.div(key, tiles)
                    source = key - target * tiles
                    weight = plan_ref[2 * length + at].astype(jnp.float32)
                    place = jnp.where(live, target, dump) if final else target
                    picked.append((target, source, place, weight))
                body(picked)
            return carry

        blocks = lax.div(size - done + (unroll - 1 if final else 0), unroll)
        lax.fori_loop(0, blocks, advance, 0)
        done = done + blocks * unroll


def in_groups(count, group, body):
    def step(block, carry):
        for u in range(group):
            body(block * group + u)
        return carry

    lax.fori_loop(0, count // group, step, 0)


def tile_rows(ref, t, height=8):
    return ref[pl.ds(pl.multiple_of(t * height, height), height), :]


def put_tile(ref, t, value):
    ref[pl.ds(pl.multiple_of(t * 8, 8), 8), :] = value


def spread_rows(far, wides, first, tiles, height):
    row = lax.broadcasted_iota(jnp.int32, (DEPTH, LANES), 0)
    picks = [jnp.where((row == k) | (row == 8 + k) | (row == 32 + k), scale, 0.0)
             for k, scale, wide in wides]
    picks = jnp.concatenate(picks, axis=1).astype(jnp.bfloat16)

    def one(t):
        spread = jnp.dot(far[first + t, :height], picks, preferred_element_type=jnp.float32)
        for n, (k, scale, wide) in enumerate(wides):
            wide[first + t, :height] = spread[:, n * LANES:(n + 1) * LANES]

    in_groups(tiles, 8, one)


def density_kernel(plan_ref, pool_ref,
                   dens_ref, press_ref, edge_ref, far, base_ref, half_b, dest_ref, more_ref,
                   near, mass_b, totals):
    own_tiles = dens_ref.shape[0]
    ghosts = dest_ref.shape[0]
    here_ref = pool_ref.at[pl.ds(0, own_tiles * 8)]
    there_ref = pool_ref.at[pl.ds(own_tiles * 8, ghosts * 8)]
    tiles = own_tiles + ghosts
    row = lax.broadcasted_iota(jnp.int32, (8, LANES), 0)
    spatial = (row >= 1) & (row <= 3)
    first = here_ref[0:8, :]
    low, high, most = first, first, there_ref[0:8, :]
    for t in range(1, own_tiles):
        part = here_ref[t * 8:(t + 1) * 8, :]
        low, high = jnp.minimum(low, part), jnp.maximum(high, part)
    for g in range(1, ghosts):
        most = jnp.maximum(most, there_ref[g * 8:(g + 1) * 8, :])
    low = jnp.min(low, axis=1, keepdims=True)
    high = jnp.max(high, axis=1, keepdims=True)
    most = jnp.maximum(jnp.max(most, axis=1, keepdims=True), high)
    reach = most[4:5, :] + 0.01
    reach = reach * reach
    centre = jnp.where(spatial, 0.5 * (low + high), 0.0)

    def shifted(part):
        moved = part - centre
        norm = jnp.sum(jnp.where(spatial, moved * moved, 0.0), axis=0, keepdims=True)
        return jnp.where(row == 7, norm, moved), norm

    def own(t):
        moved, norm = shifted(tile_rows(here_ref, t))
        put_tile(base_ref, t, moved)
        far[t] = by_last(ones_where(equal_rows(same, LANES)),
                         source_terms(moved)).astype(jnp.bfloat16)
        radius = moved[4:5, :]
        wanted = jnp.where(row == 0, norm, jnp.where(spatial, -2.0 * moved, jnp.where(
            row == 7, 1.0, 0.0)))
        near[t] = target_terms(wanted * (1.0 / (radius * radius)))

    same = lax.broadcasted_iota(jnp.int32, (1, LANES), 1)
    in_groups(own_tiles, 8, own)

    def ghost(g):
        part = tile_rows(there_ref, g)
        gap = jnp.maximum(jnp.maximum(low - part, part - high), 0.0)
        beyond = jnp.sum(jnp.where(spatial, gap * gap, 0.0), axis=0, keepdims=True)
        active = (beyond < reach) & (part[5:6, :] != 0.0)
        totals[0, pl.ds(g, 1), :] = jnp.where(active, 1.0, 0.0)
        moved, norm = shifted(part)
        put_tile(base_ref, own_tiles + g, moved)

    in_groups(ghosts, 8, ghost)
    flags = totals[0, :ghosts, :]
    at, upto = earlier(LANES, LANES)
    rank = jnp.dot(flags.astype(jnp.bfloat16), ones_where(at <= upto),
                   preferred_element_type=jnp.float32)
    dest_ref[...] = jnp.where(flags > 0.0, rank - 1.0, -1.0).astype(jnp.int32)
    totals[0, :ghosts, :] = rank
    slot = lax.broadcasted_iota(jnp.int32, (LANES, DEPTH), 0).astype(jnp.float32)
    term = lax.broadcasted_iota(jnp.int32, (LANES, DEPTH), 1)
    unit = (term == 0) | (term == 16) | (term == 40)
    more = (jnp.max(rank) > LANES // 2 + 0.5).astype(jnp.int32)
    more_ref[0] = more

    def squeeze(g):
        moved = by_last(ones_where(equal_rows(dest_ref[pl.ds(g, 1), :], LANES)),
                        source_terms(tile_rows(base_ref, own_tiles + g)))
        unused = slot >= totals[0, pl.ds(g, 1), LANES - 1:]
        far[own_tiles + g] = jnp.where(unit & unused, 1.0, moved).astype(jnp.bfloat16)

    in_groups(ghosts, 8, squeeze)
    wides = [(5, 1.0, mass_b), (4, 0.5, half_b)]
    half = LANES // 2
    spread_rows(far, wides, 0, own_tiles, LANES)
    spread_rows(far, wides, own_tiles, ghosts, half)

    @pl.when(more > 0)
    def _():
        spread_rows(far, wides, own_tiles, ghosts, LANES)

    totals[...] = jnp.zeros_like(totals)

    def add(first, height):
        def body(picked):
            (target, source, place, weight), = picked
            sq = jnp.dot(far[source, first:first + height], near[target],
                         preferred_element_type=jnp.float32)
            sq = jnp.maximum(sq, TINY)
            ratio = sq * lax.rsqrt(sq)
            falloff = jnp.maximum(1.0 - ratio, 0.0)
            falloff = falloff * falloff
            term = falloff * falloff * ((ratio + 0.25) * mass_b[source, first:first + height])
            summed = jnp.sum(term.reshape(height // 8, 8, LANES), axis=0)
            totals[place, :8] += weight * summed
        return body

    sweep(plan_ref, 0, tiles, own_tiles, (48, 8), 1, add(0, LANES))
    sweep(plan_ref, 1, tiles, own_tiles, (96, 16), 1, add(0, half))

    @pl.when(more > 0)
    def _():
        sweep(plan_ref, 1, tiles, own_tiles, (4,), 1, add(half, half))

    def field(k):
        return here_ref[pl.ds(k, own_tiles, stride=8), :]

    summed = jnp.sum(totals[:own_tiles, :8], axis=1)
    radius = field(4)
    density = KERNEL_NORM / (radius * radius * radius) * (4.0 * summed + field(5))
    dens_ref[...] = density
    press = GAMMA_LESS * field(6) / density
    press_ref[...] = press
    edge_ref[...] = press[:GT]


def accel_kernel(plan_ref, more_ref, far, base_ref, half_b, dest_ref,
                 press_ref, press_far_ref, out_ref, near, left, left_half, totals, half_a):
    own_tiles = press_ref.shape[0]
    ghosts = dest_ref.shape[0]
    tiles = own_tiles + ghosts
    half = LANES // 2
    row = lax.broadcasted_iota(jnp.int32, (8, LANES), 0)
    spatial = (row >= 1) & (row <= 3)

    def loaded(part, press):
        twice = jnp.where(row < 4, part, pltpu.roll(part, 4, 0)) * part[5:6, :]
        one, two, low = three(jnp.where(row < 4, twice, twice * press))
        return jnp.concatenate([one, two], axis=0).astype(jnp.bfloat16)

    def own(t):
        part = tile_rows(base_ref, t)
        wanted = jnp.where(row == 0, part[7:8, :], jnp.where(spatial, -2.0 * part, jnp.where(
            row == 7, 1.0, 0.0)))
        half_a[pl.ds(t, 1), :] = 0.5 * part[4:5, :]
        near[t] = target_terms(wanted)
        rows = loaded(part, press_ref[pl.ds(t, 1), :])
        left[t] = jnp.concatenate([rows, rows], axis=1)

    in_groups(own_tiles, 8, own)

    def ghost(g):
        rows = loaded(tile_rows(base_ref, own_tiles + g), press_far_ref[pl.ds(g, 1), :])
        moved = by_last(rows, ones_where(equal_rows(dest_ref[pl.ds(g, 1), :], LANES)))
        moved = moved.astype(jnp.bfloat16)
        none = jnp.zeros((16, LANES), jnp.bfloat16)
        for v in range(2):
            piece = moved[:, v * half:(v + 1) * half]
            two = jnp.concatenate([piece, piece], axis=1)
            left_half[v, 0, g] = jnp.concatenate([two, none], axis=1)
            left_half[v, 1, g] = jnp.concatenate([none, two], axis=1)

    in_groups(ghosts, 8, ghost)
    totals[...] = jnp.zeros_like(totals)

    def slopes(source, target, first, height):
        sq = jnp.dot(far[source, first:first + height], near[target],
                     preferred_element_type=jnp.float32)
        radius = half_b[source, first:first + height] + half_a[pl.ds(target, 1), :]
        sq = jnp.maximum(sq, TINY)
        dist = sq * lax.rsqrt(sq)
        inv = pl.reciprocal(radius, approx=True)
        wide = inv * inv
        fall = jnp.maximum(inv - dist * wide, 0.0)
        slope = fall * fall * (fall * wide)
        high = slope.astype(jnp.bfloat16)
        low = (slope - high.astype(jnp.float32)).astype(jnp.bfloat16)
        return [high, low]

    def add_one(picked):
        (target, source, place, weight), = picked
        terms = jnp.concatenate(slopes(source, target, 0, LANES), axis=0)
        totals[place] += weight * jnp.dot(left[source], terms, preferred_element_type=jnp.float32)

    def add_two(v):
        def body(both):
            terms, lhs = [], []
            for side, (target, source, place, weight) in enumerate(both):
                terms += slopes(source, target, v * half, half)
                lhs.append(left_half[v, side, jnp.maximum(source - own_tiles, 0)])
            moved = jnp.dot(jnp.concatenate(lhs, axis=0), jnp.concatenate(terms, axis=0),
                            preferred_element_type=jnp.float32)
            for side, (target, source, place, weight) in enumerate(both):
                totals[place] += weight * moved[side * 16:(side + 1) * 16]
        return body

    sweep(plan_ref, 0, tiles, own_tiles, (32,), 1, add_one)
    sweep(plan_ref, 1, tiles, own_tiles, (64,), 2, add_two(0))

    @pl.when(more_ref[0] > 0)
    def _():
        sweep(plan_ref, 1, tiles, own_tiles, (4,), 2, add_two(1))

    for t in range(own_tiles):
        both = totals[t, :8] + totals[t, 8:]
        mixed = jnp.where(row < 4, both * press_ref[t:t + 1, :], both)
        mixed = mixed + pltpu.roll(mixed, 4, 0)
        pulled = 20.0 * KERNEL_NORM * (base_ref[t * 8:(t + 1) * 8, :] * mixed[0:1, :] - mixed)
        out_ref[:, t * LANES:(t + 1) * LANES] = pulled[1:4, :]


SMEM = pl.BlockSpec(memory_space=pltpu.SMEM)
VMEM = pl.BlockSpec(memory_space=pltpu.VMEM)
HBM = pl.BlockSpec(memory_space=pltpu.HBM)
GRANT = 24 * 2 ** 20
WHOLE = 60 * 2 ** 20


def exchange_call(count, pairs, positions, mass, smoothing, energy, destination, rows, cols):
    tiles = mass.shape[0]
    pool_tiles = tiles + 4 * GT
    lists = 2 * pl.cdiv(tiles * max(tiles, 4 * GT), LANES)
    domains = rows * cols
    slots = tiles * LANES // domains
    edge = GT * LANES // slots
    dma = pltpu.SemaphoreType.DMA
    given = (pairs, positions, mass, smoothing, energy, destination)
    return pl.pallas_call(
        functools.partial(exchange_kernel, rows=rows, cols=cols),
        out_shape=(
            jax.ShapeDtypeStruct((domains + 4 * edge, 8, slots), jnp.float32),
            jax.ShapeDtypeStruct((2 * lists + 2, LANES), jnp.int32),
        ),
        in_specs=[SMEM] + [HBM] * 6,
        out_specs=[VMEM, HBM],
        scratch_shapes=[pltpu.VMEM(x.shape, x.dtype) for x in given] + [
            pltpu.VMEM((domains, 8, slots), jnp.float32),
            pltpu.VMEM((tiles * domains, LANES), jnp.bfloat16),
            pltpu.VMEM((tiles * domains, 2 * LANES), jnp.float32),
            pltpu.VMEM((tiles, LANES), jnp.int32),
            pltpu.VMEM((tiles * 8, LANES), jnp.float32),
            pltpu.VMEM((2, tiles, LANES), jnp.int32),
            pltpu.VMEM((tiles, pool_tiles), jnp.int32),
            pltpu.VMEM((tiles, pool_tiles), jnp.int32),
            pltpu.VMEM((2 * lists + 2, LANES), jnp.int32),
            dma((6,)), dma, dma((domains,)), dma((domains,)), dma((4,)), dma((4,)),
        ],
        compiler_params=pltpu.CompilerParams(
            collective_id=0, has_side_effects=True, vmem_limit_bytes=WHOLE),
        name="exchange",
    )(count, *given)


def press_call(press, rows, cols):
    dma = pltpu.SemaphoreType.DMA
    return pl.pallas_call(
        functools.partial(press_kernel, rows=rows, cols=cols),
        out_shape=jax.ShapeDtypeStruct((4,) + press.shape, jnp.float32),
        in_specs=[VMEM],
        out_specs=VMEM,
        scratch_shapes=[dma((4,)), dma((4,))],
        compiler_params=pltpu.CompilerParams(collective_id=1, has_side_effects=True, vmem_limit_bytes=GRANT),
        name="press",
    )(press)


def density_call(plan, pool, own_tiles):
    tiles = pool.shape[0] // 8
    ghosts = tiles - own_tiles
    flat = jax.ShapeDtypeStruct((own_tiles, LANES), jnp.float32)
    return pl.pallas_call(
        density_kernel,
        out_shape=(
            flat,
            flat,
            jax.ShapeDtypeStruct((GT, LANES), jnp.float32),
            jax.ShapeDtypeStruct((tiles, LANES, DEPTH), jnp.bfloat16),
            jax.ShapeDtypeStruct((tiles * 8, LANES), jnp.float32),
            jax.ShapeDtypeStruct((tiles, LANES, LANES), jnp.float32),
            jax.ShapeDtypeStruct((ghosts, LANES), jnp.int32),
            jax.ShapeDtypeStruct((1,), jnp.int32),
        ),
        in_specs=[SMEM, VMEM],
        out_specs=(VMEM,) * 7 + (SMEM,),
        scratch_shapes=[
            pltpu.VMEM((own_tiles, DEPTH, LANES), jnp.bfloat16),
            pltpu.VMEM((tiles, LANES, LANES), jnp.float32),
            pltpu.VMEM((own_tiles + 1, max(8, ghosts), LANES), jnp.float32),
        ],
        compiler_params=pltpu.CompilerParams(vmem_limit_bytes=GRANT),
        name="density",
    )(plan, pool)


def accel_call(plan, more, far, base, half, dest, press, press_far):
    own_tiles, ghosts = press.shape[0], dest.shape[0]
    return pl.pallas_call(
        accel_kernel,
        out_shape=jax.ShapeDtypeStruct((3, own_tiles * LANES), jnp.float32),
        in_specs=[SMEM] * 2 + [VMEM] * 6,
        out_specs=VMEM,
        scratch_shapes=[
            pltpu.VMEM((own_tiles, DEPTH, LANES), jnp.bfloat16),
            pltpu.VMEM((own_tiles, 16, 2 * LANES), jnp.bfloat16),
            pltpu.VMEM((2, 2, ghosts, 16, 2 * LANES), jnp.bfloat16),
            pltpu.VMEM((own_tiles + 1, 16, LANES), jnp.float32),
            pltpu.VMEM((own_tiles, LANES), jnp.float32),
        ],
        compiler_params=pltpu.CompilerParams(vmem_limit_bytes=GRANT),
        name="accel",
    )(plan, more, far, base, half, dest, press, press_far)


def as_tiles(blocks):
    count, fields, slots = blocks.shape
    per = LANES // slots
    joined = blocks.reshape(count // per, per, fields, slots).transpose(0, 2, 1, 3)
    return joined.reshape(count // per * fields, LANES)


def local(positions, mass, smoothing, energy, destination, pairs, pair_count):
    rows = lax.axis_size("gx")
    cols = lax.axis_size("gy")
    own_tiles = mass.shape[0] // LANES
    flat = (own_tiles, LANES)
    pool, plan = exchange_call(
        pair_count, pairs, positions, mass.reshape(flat), smoothing.reshape(flat),
        energy.reshape(flat), destination.reshape(flat), rows, cols)
    plan = plan.reshape(-1)
    density, press, edge, far, base, half, dest, more = density_call(
        plan, as_tiles(pool), own_tiles)
    press_far = press_call(edge, rows, cols).reshape(4 * GT, LANES)
    accel = accel_call(plan, more, far, base, half, dest, press, press_far)
    return (density.reshape(-1), accel)


def solution(mesh):
    placed = (
        P(None, ("gx", "gy")),
        P(("gx", "gy")),
        P(("gx", "gy")),
        P(("gx", "gy")),
        P(("gx", "gy"), None),
        P(None, ("gx", "gy")),
        P(("gx", "gy")),
    )
    return jax.shard_map(
        local,
        mesh=mesh,
        in_specs=placed,
        out_specs=(P(("gx", "gy")), P(None, ("gx", "gy"))),
        check_vma=False,
    )
```

```python
import functools
import math

import jax
import jax.numpy as jnp
from jax import lax
from jax.experimental import pallas as pl
from jax.experimental.pallas import tpu as pltpu
from jax.sharding import PartitionSpec as P

GT = 8
LANES = 128
DEPTH = 48
TINY = 1e-12
MESH = pl.DeviceIdType.MESH

KERNEL_NORM = 21.0 / (2.0 * math.pi)
GAMMA_LESS = 2.0 / 3.0


def three(x):
    one = x.astype(jnp.bfloat16).astype(jnp.float32)
    rest = x - one
    two = rest.astype(jnp.bfloat16).astype(jnp.float32)
    return one, two, (rest - two).astype(jnp.bfloat16).astype(jnp.float32)


def source_terms(x):
    one, two, low = three(x)
    return jnp.concatenate([one, two, one, two, low, one], axis=0).astype(jnp.bfloat16)


def target_terms(x):
    one, two, low = three(x)
    return jnp.concatenate([one, one, two, two, one, low], axis=0).astype(jnp.bfloat16)


def put_rows(stage, rows, width, tiles, first=0):
    for k, row in enumerate(rows):
        stage[pl.ds(first + k, tiles, stride=width), :] = row


def equal_rows(row, height, base=0):
    at = lax.broadcasted_iota(jnp.int32, (height, row.shape[-1]), 0) + base
    return jnp.broadcast_to(row, at.shape) == at


def ones_where(mask):
    return jnp.where(mask, 1.0, 0.0).astype(jnp.bfloat16)


def earlier(size, width):
    row = lax.broadcasted_iota(jnp.int32, (size, width), 0)
    col = lax.broadcasted_iota(jnp.int32, (size, width), 1)
    return row, col


def list_pairs(count_ref, pairs_ref, plan_ref, rank_ref, hits_ref, own_tiles, tiles):
    slots = pairs_ref.shape[1]
    live = lax.broadcasted_iota(jnp.int32, (1, slots), 1) < count_ref[0]
    target = jnp.where(live, pairs_ref[0:1, :], -1)
    hits = by_last(ones_where(equal_rows(target, own_tiles)),
                   ones_where(equal_rows(pairs_ref[1:2, :], tiles)))
    fresh = jnp.where(hits > 0.0, 1.0, 0.0)
    row, col = earlier(tiles, tiles)
    far_row, far_col = row >= own_tiles, col >= own_tiles
    inside = jnp.dot(fresh.astype(jnp.bfloat16), ones_where((row < col) & (far_row == far_col)),
                     preferred_element_type=jnp.float32)
    total = jnp.dot(fresh.astype(jnp.bfloat16), ones_where(far_row == far_col),
                    preferred_element_type=jnp.float32)
    row, col = earlier(own_tiles, own_tiles)
    above = jnp.dot(ones_where(col < row), total.astype(jnp.bfloat16),
                    preferred_element_type=jnp.float32)
    all_rows = jnp.sum(total, axis=0, keepdims=True).astype(jnp.int32)
    column = lax.broadcasted_iota(jnp.int32, (own_tiles, tiles), 1)
    place = jnp.where(hits > 0.0, (inside + above).astype(jnp.int32), -1)
    lists = (plan_ref.shape[0] - 2) // 4
    place = jnp.where((column >= own_tiles) & (place >= 0), place + lists * LANES, place)
    rank_ref[...] = place
    hits_ref[...] = hits.astype(jnp.int32)
    source = lax.broadcasted_iota(jnp.int32, (1, tiles), 1).astype(jnp.float32)
    keys = jnp.zeros((2 * lists, LANES), jnp.float32)
    times = jnp.zeros((2 * lists, LANES), jnp.float32)
    for t in range(own_tiles):
        at = rank_ref[t:t + 1, :]
        high = at // LANES
        many = hits_ref[t:t + 1, :]
        upper = many // LANES
        mine = jnp.where(equal_rows(jnp.where(at < 0, -1, high), 2 * lists), 1.0, 0.0)
        parts = [mine * source, mine, mine * upper.astype(jnp.float32),
                 mine * (many - upper * LANES).astype(jnp.float32)]
        found = by_last(jnp.concatenate(parts, axis=0).astype(jnp.bfloat16),
                        ones_where(equal_rows(jnp.where(at < 0, -1, at - high * LANES), LANES)))
        size = 2 * lists
        keys = keys + found[:size] + float(t * tiles) * found[size:2 * size]
        times = times + float(LANES) * found[2 * size:3 * size] + found[3 * size:]
    plan_ref[:2 * lists] = keys.astype(jnp.int32)
    plan_ref[2 * lists:4 * lists] = times.astype(jnp.int32)
    plan_ref[4 * lists:4 * lists + 1] = jnp.broadcast_to(all_rows[:, :1], (1, LANES))
    plan_ref[4 * lists + 1:] = jnp.broadcast_to(all_rows[:, tiles - 1:], (1, LANES))


def order_rows(pos_ref, mass_ref, smooth_ref, energy_ref, dest_ref, sent_ref,
               flags, prefix, rank_ref, rows_ref, index_ref):
    tiles = mass_ref.shape[0]
    domains, width, slots = sent_ref.shape
    row, col = earlier(LANES, 2 * LANES)
    before = ones_where((row < col) | (col >= LANES))
    for t in range(tiles):
        flags[t * domains:(t + 1) * domains] = ones_where(
            equal_rows(dest_ref[t:t + 1, :], domains))
    prefix[...] = jnp.dot(flags[...], before, preferred_element_type=jnp.float32)
    seen = jnp.zeros((domains, LANES), jnp.float32)
    for t in range(tiles):
        part = slice(t * domains, (t + 1) * domains)
        mine = flags[part].astype(jnp.float32)
        rank = jnp.sum(mine * (prefix[part, :LANES] + seen), axis=0, keepdims=True)
        rank_ref[t:t + 1, :] = rank.astype(jnp.int32)
        seen = seen + prefix[part, LANES:]
    place = dest_ref[...] * slots + rank_ref[...]
    block = place // LANES
    rank_ref[...] = place - block * LANES
    lane = lax.broadcasted_iota(jnp.int32, (tiles, LANES), 1).astype(jnp.float32)
    from_lane = jnp.zeros((tiles, LANES), jnp.float32)
    from_tile = jnp.zeros((tiles, LANES), jnp.float32)
    for t in range(tiles):
        picked = equal_rows(block[t:t + 1, :], tiles)
        both = jnp.concatenate([jnp.where(picked, lane, 0.0), jnp.where(picked, 1.0, 0.0)], axis=0)
        found = by_last(both.astype(jnp.bfloat16),
                        ones_where(equal_rows(rank_ref[t:t + 1, :], LANES)))
        from_lane = from_lane + found[:tiles]
        from_tile = from_tile + float(t) * found[tiles:]
    ones = jnp.ones((tiles, LANES), jnp.float32)
    put_rows(rows_ref, [smooth_ref[...], mass_ref[...], energy_ref[...], 0.0 * ones], width, tiles, 4)
    put_rows(rows_ref, [ones], width, tiles, 0)
    for t in range(tiles):
        rows_ref[t * width + 1:t * width + 4, :] = pos_ref[:, t * LANES:(t + 1) * LANES]
    index_ref[0] = from_lane.astype(jnp.int32)
    index_ref[1] = from_tile.astype(jnp.int32)
    per = LANES // slots

    def gather(q, carry):
        at = jnp.broadcast_to(index_ref[0, pl.ds(q, 1), :], (width, LANES))
        tile = jnp.broadcast_to(index_ref[1, pl.ds(q, 1), :], (width, LANES))
        out = jnp.zeros((width, LANES), jnp.float32)
        for t in range(tiles):
            moved = jnp.take_along_axis(rows_ref[t * width:(t + 1) * width, :], at, axis=1)
            out = jnp.where(tile == t, moved, out)
        for p in range(per):
            sent_ref[q * per + p] = out[:, p * slots:(p + 1) * slots]
        return carry

    lax.fori_loop(0, tiles, gather, 0)


def beside(i, j, rows, cols):
    return [(i > 0, (i - 1, j), 1), (i < rows - 1, (i + 1, j), 0),
            (j > 0, (i, j - 1), 3), (j < cols - 1, (i, j + 1), 2)]


def exchange_kernel(count_ref, *refs, rows, cols):
    given, refs = refs[:6], refs[6:]
    pool_ref, listed_ref = refs[:2]
    held, refs = refs[2:8], refs[8:]
    (out_ref, flags, prefix, rank_ref, rows_ref, index_ref, place_ref, hits_ref, plan_ref,
     load_sem, plan_sem, send_sem, recv_sem, edge_send, edge_recv) = refs
    pairs_ref, pos_ref, mass_ref, smooth_ref, energy_ref, dest_ref = held
    loads = [pltpu.make_async_copy(a, b, load_sem.at[k]) for k, (a, b) in enumerate(zip(given, held))]
    for load in loads:
        load.start()
    domains = rows * cols
    tiles = mass_ref.shape[0]
    edge = (pool_ref.shape[0] - domains) // 4
    i, j = lax.axis_index("gx"), lax.axis_index("gy")
    me = i * cols + j
    barrier = pltpu.get_barrier_semaphore()

    def greet(k, carry):
        peer = lax.rem(me + k, domains)
        pl.semaphore_signal(barrier, inc=1, device_id=(peer // cols, lax.rem(peer, cols)),
                            device_id_type=MESH)
        return carry

    lax.fori_loop(1, domains, greet, 0)
    for load in loads:
        load.wait()
    order_rows(pos_ref, mass_ref, smooth_ref, energy_ref, dest_ref, out_ref,
               flags, prefix, rank_ref, rows_ref, index_ref)
    pl.semaphore_wait(barrier, domains - 1)

    def outgoing(peer):
        return pltpu.make_async_remote_copy(
            src_ref=out_ref.at[peer], dst_ref=pool_ref.at[me],
            send_sem=send_sem.at[peer], recv_sem=recv_sem.at[me],
            device_id=(peer // cols, lax.rem(peer, cols)), device_id_type=MESH)

    def incoming(source):
        return pltpu.make_async_remote_copy(
            src_ref=out_ref.at[source], dst_ref=pool_ref.at[source],
            send_sem=send_sem.at[source], recv_sem=recv_sem.at[source],
            device_id=(source // cols, lax.rem(source, cols)), device_id_type=MESH)

    def send(k, carry):
        outgoing(lax.rem(me + k, domains)).start()
        return carry

    lax.fori_loop(1, domains, send, 0)
    pool_ref[me] = out_ref[me]
    list_pairs(count_ref, pairs_ref, plan_ref, place_ref, hits_ref, tiles, tiles + 4 * GT)
    listed = pltpu.make_async_copy(plan_ref, listed_ref, plan_sem)
    listed.start()

    def arrive(source, carry):
        @pl.when(source != me)
        def _():
            incoming(source).wait_recv()
        return carry

    lax.fori_loop(0, edge, arrive, 0)
    sides = beside(i, j, rows, cols)

    def across(side):
        there, peer, slot = sides[side]
        return pltpu.make_async_remote_copy(
            src_ref=pool_ref.at[pl.ds(0, edge)], dst_ref=pool_ref.at[pl.ds(domains + slot * edge, edge)],
            send_sem=edge_send.at[side], recv_sem=edge_recv.at[slot],
            device_id=peer, device_id_type=MESH)

    def back(side):
        there, peer, slot = sides[side]
        return pltpu.make_async_remote_copy(
            src_ref=pool_ref.at[pl.ds(0, edge)], dst_ref=pool_ref.at[pl.ds(domains + side * edge, edge)],
            send_sem=edge_send.at[side], recv_sem=edge_recv.at[side],
            device_id=peer, device_id_type=MESH)

    for side in range(4):
        @pl.when(sides[side][0])
        def _():
            across(side).start()

        @pl.when(jnp.logical_not(sides[side][0]))
        def _():
            pool_ref[domains + side * edge:domains + (side + 1) * edge] = jnp.zeros(
                (edge,) + pool_ref.shape[1:], jnp.float32)

    lax.fori_loop(edge, domains, arrive, 0)

    def left(k, carry):
        outgoing(lax.rem(me + k, domains)).wait_send()
        return carry

    lax.fori_loop(1, domains, left, 0)
    for side in range(4):
        @pl.when(sides[side][0])
        def _():
            across(side).wait_send()
            back(side).wait_recv()

    listed.wait()


def press_kernel(press_ref, ghost_ref, send_sem, recv_sem, rows, cols):
    i, j = lax.axis_index("gx"), lax.axis_index("gy")
    sides = beside(i, j, rows, cols)
    barrier = pltpu.get_barrier_semaphore()
    for there, peer, slot in sides:
        @pl.when(there)
        def _():
            pl.semaphore_signal(barrier, inc=1, device_id=peer, device_id_type=MESH)

    pl.semaphore_wait(barrier, sum(there.astype(jnp.int32) for there, peer, slot in sides))

    def across(side, slot):
        return pltpu.make_async_remote_copy(
            src_ref=press_ref, dst_ref=ghost_ref.at[slot],
            send_sem=send_sem.at[side], recv_sem=recv_sem.at[slot],
            device_id=sides[side][1], device_id_type=MESH)

    for side in range(4):
        @pl.when(sides[side][0])
        def _():
            across(side, sides[side][2]).start()

        @pl.when(jnp.logical_not(sides[side][0]))
        def _():
            ghost_ref[side] = jnp.zeros_like(ghost_ref[side])

    for side in range(4):
        @pl.when(sides[side][0])
        def _():
            across(side, sides[side][2]).wait_send()
            across(side, side).wait_recv()


def one_hot_rows(dest):
    rows = lax.broadcasted_iota(jnp.int32, (LANES, LANES), 0)
    wide = jnp.broadcast_to(dest, (LANES, LANES))
    return jnp.where(wide == rows, 1.0, 0.0).astype(jnp.bfloat16)


def by_last(a, b):
    return lax.dot_general(a, b, (((1,), (1,)), ((), ())), preferred_element_type=jnp.float32)


def sweep(plan_ref, which, tiles, dump, unrolls, together, body):
    length = (plan_ref.shape[0] - 2 * LANES) // 4
    size = plan_ref[4 * length + which * LANES]

    done = 0
    for unroll in unrolls:
        final = unroll == unrolls[-1]

        def advance(block, carry):
            for u in range(0, unroll, together):
                picked = []
                for v in range(together):
                    k = done + block * unroll + u + v
                    if final:
                        live = k < size
                        at = which * length + jnp.minimum(k, length - 1)
                        key = jnp.where(live, plan_ref[at], 0)
                    else:
                        at = which * length + k
                        key = plan_ref[at]
                    target = lax.div(key, tiles)
                    source = key - target * tiles
                    weight = plan_ref[2 * length + at].astype(jnp.float32)
                    place = jnp.where(live, target, dump) if final else target
                    picked.append((target, source, place, weight))
                body(picked)
            return carry

        blocks = lax.div(size - done + (unroll - 1 if final else 0), unroll)
        lax.fori_loop(0, blocks, advance, 0)
        done = done + blocks * unroll


def sweep_extra(plan_ref, extra_ref, tiles, dump, unroll, together, body):
    length = (plan_ref.shape[0] - 2 * LANES) // 4
    size = extra_ref[0]

    def advance(block, carry):
        for u in range(0, unroll, together):
            picked = []
            for v in range(together):
                k = block * unroll + u + v
                live = k < size
                at = length + jnp.where(live, extra_ref[1 + jnp.minimum(k, length - 1)], 0)
                key = jnp.where(live, plan_ref[at], 0)
                target = lax.div(key, tiles)
                source = key - target * tiles
                weight = plan_ref[2 * length + at].astype(jnp.float32)
                picked.append((target, source, jnp.where(live, target, dump), weight))
            body(picked)
        return carry

    lax.fori_loop(0, lax.div(size + unroll - 1, unroll), advance, 0)


def list_extra(plan_ref, rank_ref, extra_ref, own_tiles, tiles, height):
    length = (plan_ref.shape[0] - 2 * LANES) // 4
    size = plan_ref[4 * length + LANES]

    def look(block, found):
        for u in range(8):
            k = jnp.minimum(block * 8 + u, length - 1)
            key = plan_ref[length + k]
            ghost = jnp.maximum(key - lax.div(key, tiles) * tiles - own_tiles, 0)
            long = (block * 8 + u < size) & (rank_ref[ghost, LANES - 1] > height)
            extra_ref[1 + found] = k
            found = found + long.astype(jnp.int32)
        return found

    extra_ref[0] = lax.fori_loop(0, lax.div(size + 7, 8), look, 0)


def in_groups(count, group, body):
    def step(block, carry):
        for u in range(group):
            body(block * group + u)
        return carry

    lax.fori_loop(0, count // group, step, 0)


def tile_rows(ref, t, height=8):
    return ref[pl.ds(pl.multiple_of(t * height, height), height), :]


def put_tile(ref, t, value):
    ref[pl.ds(pl.multiple_of(t * 8, 8), 8), :] = value


def spread_rows(far, wides, first, tiles, height):
    row = lax.broadcasted_iota(jnp.int32, (DEPTH, LANES), 0)
    picks = [jnp.where((row == k) | (row == 8 + k) | (row == 32 + k), scale, 0.0)
             for k, scale, wide in wides]
    picks = jnp.concatenate(picks, axis=1).astype(jnp.bfloat16)

    def one(t):
        spread = jnp.dot(far[first + t, :height], picks, preferred_element_type=jnp.float32)
        for n, (k, scale, wide) in enumerate(wides):
            wide[first + t, :height] = spread[:, n * LANES:(n + 1) * LANES]

    in_groups(tiles, 8, one)


def density_kernel(plan_ref, pool_ref,
                   dens_ref, press_ref, edge_ref, far, base_ref, half_b, dest_ref, extra_ref,
                   near, mass_b, totals, whole, scalar_rank, rank_sem):
    own_tiles = dens_ref.shape[0]
    ghosts = dest_ref.shape[0]
    here_ref = pool_ref.at[pl.ds(0, own_tiles * 8)]
    there_ref = pool_ref.at[pl.ds(own_tiles * 8, ghosts * 8)]
    tiles = own_tiles + ghosts
    row = lax.broadcasted_iota(jnp.int32, (8, LANES), 0)
    spatial = (row >= 1) & (row <= 3)
    first = here_ref[0:8, :]
    low, high, most = first, first, there_ref[0:8, :]
    for t in range(1, own_tiles):
        part = here_ref[t * 8:(t + 1) * 8, :]
        low, high = jnp.minimum(low, part), jnp.maximum(high, part)
    for g in range(1, ghosts):
        most = jnp.maximum(most, there_ref[g * 8:(g + 1) * 8, :])
    low = jnp.min(low, axis=1, keepdims=True)
    high = jnp.max(high, axis=1, keepdims=True)
    most = jnp.maximum(jnp.max(most, axis=1, keepdims=True), high)
    reach = most[4:5, :] + 0.01
    reach = reach * reach
    centre = jnp.where(spatial, 0.5 * (low + high), 0.0)

    def shifted(part):
        moved = part - centre
        norm = jnp.sum(jnp.where(spatial, moved * moved, 0.0), axis=0, keepdims=True)
        return jnp.where(row == 7, norm, moved), norm

    def own(t):
        moved, norm = shifted(tile_rows(here_ref, t))
        put_tile(base_ref, t, moved)
        far[t] = by_last(ones_where(equal_rows(same, LANES)),
                         source_terms(moved)).astype(jnp.bfloat16)
        radius = moved[4:5, :]
        wanted = jnp.where(row == 0, norm, jnp.where(spatial, -2.0 * moved, jnp.where(
            row == 7, 1.0, 0.0)))
        near[t] = target_terms(wanted * (1.0 / (radius * radius)))

    same = lax.broadcasted_iota(jnp.int32, (1, LANES), 1)
    in_groups(own_tiles, 8, own)

    def ghost(g):
        part = tile_rows(there_ref, g)
        gap = jnp.maximum(jnp.maximum(low - part, part - high), 0.0)
        beyond = jnp.sum(jnp.where(spatial, gap * gap, 0.0), axis=0, keepdims=True)
        active = (beyond < reach) & (part[5:6, :] != 0.0)
        totals[0, pl.ds(g, 1), :] = jnp.where(active, 1.0, 0.0)
        moved, norm = shifted(part)
        put_tile(base_ref, own_tiles + g, moved)

    in_groups(ghosts, 8, ghost)
    flags = totals[0, :ghosts, :]
    at, upto = earlier(LANES, LANES)
    rank = jnp.dot(flags.astype(jnp.bfloat16), ones_where(at <= upto),
                   preferred_element_type=jnp.float32)
    dest_ref[...] = jnp.where(flags > 0.0, rank - 1.0, -1.0).astype(jnp.int32)
    totals[0, :ghosts, :] = rank
    slot = lax.broadcasted_iota(jnp.int32, (LANES, DEPTH), 0).astype(jnp.float32)
    term = lax.broadcasted_iota(jnp.int32, (LANES, DEPTH), 1)
    unit = (term == 0) | (term == 16) | (term == 40)
    half = LANES // 2
    more = (jnp.max(rank) > half + 0.5).astype(jnp.int32)
    extra_ref[0] = 0

    @pl.when(more > 0)
    def _():
        whole[...] = rank.astype(jnp.int32)
        copy = pltpu.make_async_copy(whole, scalar_rank, rank_sem)
        copy.start()
        copy.wait()
        list_extra(plan_ref, scalar_rank, extra_ref, own_tiles, tiles, half)


    def squeeze(g):
        moved = by_last(ones_where(equal_rows(dest_ref[pl.ds(g, 1), :], LANES)),
                        source_terms(tile_rows(base_ref, own_tiles + g)))
        unused = slot >= totals[0, pl.ds(g, 1), LANES - 1:]
        far[own_tiles + g] = jnp.where(unit & unused, 1.0, moved).astype(jnp.bfloat16)

    in_groups(ghosts, 8, squeeze)
    wides = [(5, 1.0, mass_b), (4, 0.5, half_b)]
    spread_rows(far, wides, 0, own_tiles, LANES)
    spread_rows(far, wides, own_tiles, ghosts, half)

    @pl.when(more > 0)
    def _():
        spread_rows(far, wides, own_tiles, ghosts, LANES)

    totals[...] = jnp.zeros_like(totals)

    def add(first, height):
        def body(picked):
            (target, source, place, weight), = picked
            sq = jnp.dot(far[source, first:first + height], near[target],
                         preferred_element_type=jnp.float32)
            sq = jnp.maximum(sq, TINY)
            ratio = sq * lax.rsqrt(sq)
            falloff = jnp.maximum(1.0 - ratio, 0.0)
            falloff = falloff * falloff
            term = falloff * falloff * ((ratio + 0.25) * mass_b[source, first:first + height])
            summed = jnp.sum(term.reshape(height // 8, 8, LANES), axis=0)
            totals[place, :8] += weight * summed
        return body

    sweep(plan_ref, 0, tiles, own_tiles, (48, 8), 1, add(0, LANES))
    sweep(plan_ref, 1, tiles, own_tiles, (96, 16), 1, add(0, half))

    @pl.when(more > 0)
    def _():
        sweep_extra(plan_ref, extra_ref, tiles, own_tiles, 8, 1, add(half, half))

    def field(k):
        return here_ref[pl.ds(k, own_tiles, stride=8), :]

    summed = jnp.sum(totals[:own_tiles, :8], axis=1)
    radius = field(4)
    density = KERNEL_NORM / (radius * radius * radius) * (4.0 * summed + field(5))
    dens_ref[...] = density
    press = GAMMA_LESS * field(6) / density
    press_ref[...] = press
    edge_ref[...] = press[:GT]


def accel_kernel(plan_ref, extra_ref, far, base_ref, half_b, dest_ref,
                 press_ref, press_far_ref, out_ref, near, left, left_half, totals, half_a):
    own_tiles = press_ref.shape[0]
    ghosts = dest_ref.shape[0]
    tiles = own_tiles + ghosts
    half = LANES // 2
    row = lax.broadcasted_iota(jnp.int32, (8, LANES), 0)
    spatial = (row >= 1) & (row <= 3)

    def loaded(part, press):
        twice = jnp.where(row < 4, part, pltpu.roll(part, 4, 0)) * part[5:6, :]
        one, two, low = three(jnp.where(row < 4, twice, twice * press))
        return jnp.concatenate([one, two], axis=0).astype(jnp.bfloat16)

    def own(t):
        part = tile_rows(base_ref, t)
        wanted = jnp.where(row == 0, part[7:8, :], jnp.where(spatial, -2.0 * part, jnp.where(
            row == 7, 1.0, 0.0)))
        half_a[pl.ds(t, 1), :] = 0.5 * part[4:5, :]
        near[t] = target_terms(wanted)
        rows = loaded(part, press_ref[pl.ds(t, 1), :])
        left[t] = jnp.concatenate([rows, rows], axis=1)

    in_groups(own_tiles, 8, own)

    def ghost(g):
        rows = loaded(tile_rows(base_ref, own_tiles + g), press_far_ref[pl.ds(g, 1), :])
        moved = by_last(rows, ones_where(equal_rows(dest_ref[pl.ds(g, 1), :], LANES)))
        moved = moved.astype(jnp.bfloat16)
        none = jnp.zeros((16, LANES), jnp.bfloat16)
        for v in range(2):
            piece = moved[:, v * half:(v + 1) * half]
            two = jnp.concatenate([piece, piece], axis=1)
            left_half[v, 0, g] = jnp.concatenate([two, none], axis=1)
            left_half[v, 1, g] = jnp.concatenate([none, two], axis=1)

    in_groups(ghosts, 8, ghost)
    totals[...] = jnp.zeros_like(totals)

    def slopes(source, target, first, height):
        sq = jnp.dot(far[source, first:first + height], near[target],
                     preferred_element_type=jnp.float32)
        radius = half_b[source, first:first + height] + half_a[pl.ds(target, 1), :]
        sq = jnp.maximum(sq, TINY)
        dist = sq * lax.rsqrt(sq)
        inv = pl.reciprocal(radius, approx=True)
        wide = inv * inv
        fall = jnp.maximum(inv - dist * wide, 0.0)
        slope = fall * fall * (fall * wide)
        high = slope.astype(jnp.bfloat16)
        low = (slope - high.astype(jnp.float32)).astype(jnp.bfloat16)
        return [high, low]

    def add_one(picked):
        (target, source, place, weight), = picked
        terms = jnp.concatenate(slopes(source, target, 0, LANES), axis=0)
        totals[place] += weight * jnp.dot(left[source], terms, preferred_element_type=jnp.float32)

    def add_two(v):
        def body(both):
            terms, lhs = [], []
            for side, (target, source, place, weight) in enumerate(both):
                terms += slopes(source, target, v * half, half)
                lhs.append(left_half[v, side, jnp.maximum(source - own_tiles, 0)])
            moved = jnp.dot(jnp.concatenate(lhs, axis=0), jnp.concatenate(terms, axis=0),
                            preferred_element_type=jnp.float32)
            for side, (target, source, place, weight) in enumerate(both):
                totals[place] += weight * moved[side * 16:(side + 1) * 16]
        return body

    sweep(plan_ref, 0, tiles, own_tiles, (32,), 1, add_one)
    sweep(plan_ref, 1, tiles, own_tiles, (64,), 2, add_two(0))

    @pl.when(extra_ref[0] > 0)
    def _():
        sweep_extra(plan_ref, extra_ref, tiles, own_tiles, 8, 2, add_two(1))

    for t in range(own_tiles):
        both = totals[t, :8] + totals[t, 8:]
        mixed = jnp.where(row < 4, both * press_ref[t:t + 1, :], both)
        mixed = mixed + pltpu.roll(mixed, 4, 0)
        pulled = 20.0 * KERNEL_NORM * (base_ref[t * 8:(t + 1) * 8, :] * mixed[0:1, :] - mixed)
        out_ref[:, t * LANES:(t + 1) * LANES] = pulled[1:4, :]


SMEM = pl.BlockSpec(memory_space=pltpu.SMEM)
VMEM = pl.BlockSpec(memory_space=pltpu.VMEM)
HBM = pl.BlockSpec(memory_space=pltpu.HBM)
GRANT = 24 * 2 ** 20
WHOLE = 60 * 2 ** 20


def exchange_call(count, pairs, positions, mass, smoothing, energy, destination, rows, cols):
    tiles = mass.shape[0]
    pool_tiles = tiles + 4 * GT
    lists = 2 * pl.cdiv(tiles * max(tiles, 4 * GT), LANES)
    domains = rows * cols
    slots = tiles * LANES // domains
    edge = GT * LANES // slots
    dma = pltpu.SemaphoreType.DMA
    given = (pairs, positions, mass, smoothing, energy, destination)
    return pl.pallas_call(
        functools.partial(exchange_kernel, rows=rows, cols=cols),
        out_shape=(
            jax.ShapeDtypeStruct((domains + 4 * edge, 8, slots), jnp.float32),
            jax.ShapeDtypeStruct((2 * lists + 2, LANES), jnp.int32),
        ),
        in_specs=[SMEM] + [HBM] * 6,
        out_specs=[VMEM, HBM],
        scratch_shapes=[pltpu.VMEM(x.shape, x.dtype) for x in given] + [
            pltpu.VMEM((domains, 8, slots), jnp.float32),
            pltpu.VMEM((tiles * domains, LANES), jnp.bfloat16),
            pltpu.VMEM((tiles * domains, 2 * LANES), jnp.float32),
            pltpu.VMEM((tiles, LANES), jnp.int32),
            pltpu.VMEM((tiles * 8, LANES), jnp.float32),
            pltpu.VMEM((2, tiles, LANES), jnp.int32),
            pltpu.VMEM((tiles, pool_tiles), jnp.int32),
            pltpu.VMEM((tiles, pool_tiles), jnp.int32),
            pltpu.VMEM((2 * lists + 2, LANES), jnp.int32),
            dma((6,)), dma, dma((domains,)), dma((domains,)), dma((4,)), dma((4,)),
        ],
        compiler_params=pltpu.CompilerParams(
            collective_id=0, has_side_effects=True, vmem_limit_bytes=WHOLE),
        name="exchange",
    )(count, *given)


def press_call(press, rows, cols):
    dma = pltpu.SemaphoreType.DMA
    return pl.pallas_call(
        functools.partial(press_kernel, rows=rows, cols=cols),
        out_shape=jax.ShapeDtypeStruct((4,) + press.shape, jnp.float32),
        in_specs=[VMEM],
        out_specs=VMEM,
        scratch_shapes=[dma((4,)), dma((4,))],
        compiler_params=pltpu.CompilerParams(collective_id=1, has_side_effects=True, vmem_limit_bytes=GRANT),
        name="press",
    )(press)


def density_call(plan, pool, own_tiles):
    tiles = pool.shape[0] // 8
    ghosts = tiles - own_tiles
    lists = (plan.shape[0] // LANES - 2) // 4
    flat = jax.ShapeDtypeStruct((own_tiles, LANES), jnp.float32)
    return pl.pallas_call(
        density_kernel,
        out_shape=(
            flat,
            flat,
            jax.ShapeDtypeStruct((GT, LANES), jnp.float32),
            jax.ShapeDtypeStruct((tiles, LANES, DEPTH), jnp.bfloat16),
            jax.ShapeDtypeStruct((tiles * 8, LANES), jnp.float32),
            jax.ShapeDtypeStruct((tiles, LANES, LANES), jnp.float32),
            jax.ShapeDtypeStruct((ghosts, LANES), jnp.int32),
            jax.ShapeDtypeStruct((lists * LANES + LANES,), jnp.int32),
        ),
        in_specs=[SMEM, VMEM],
        out_specs=(VMEM,) * 7 + (SMEM,),
        scratch_shapes=[
            pltpu.VMEM((own_tiles, DEPTH, LANES), jnp.bfloat16),
            pltpu.VMEM((tiles, LANES, LANES), jnp.float32),
            pltpu.VMEM((own_tiles + 1, max(8, ghosts), LANES), jnp.float32),
            pltpu.VMEM((ghosts, LANES), jnp.int32),
            pltpu.SMEM((ghosts, LANES), jnp.int32),
            pltpu.SemaphoreType.DMA,
        ],
        compiler_params=pltpu.CompilerParams(vmem_limit_bytes=GRANT),
        name="density",
    )(plan, pool)


def accel_call(plan, extra, far, base, half, dest, press, press_far):
    own_tiles, ghosts = press.shape[0], dest.shape[0]
    return pl.pallas_call(
        accel_kernel,
        out_shape=jax.ShapeDtypeStruct((3, own_tiles * LANES), jnp.float32),
        in_specs=[SMEM] * 2 + [VMEM] * 6,
        out_specs=VMEM,
        scratch_shapes=[
            pltpu.VMEM((own_tiles, DEPTH, LANES), jnp.bfloat16),
            pltpu.VMEM((own_tiles, 16, 2 * LANES), jnp.bfloat16),
            pltpu.VMEM((2, 2, ghosts, 16, 2 * LANES), jnp.bfloat16),
            pltpu.VMEM((own_tiles + 1, 16, LANES), jnp.float32),
            pltpu.VMEM((own_tiles, LANES), jnp.float32),
        ],
        compiler_params=pltpu.CompilerParams(vmem_limit_bytes=GRANT),
        name="accel",
    )(plan, extra, far, base, half, dest, press, press_far)


def as_tiles(blocks):
    count, fields, slots = blocks.shape
    per = LANES // slots
    joined = blocks.reshape(count // per, per, fields, slots).transpose(0, 2, 1, 3)
    return joined.reshape(count // per * fields, LANES)


def local(positions, mass, smoothing, energy, destination, pairs, pair_count):
    rows = lax.axis_size("gx")
    cols = lax.axis_size("gy")
    own_tiles = mass.shape[0] // LANES
    flat = (own_tiles, LANES)
    pool, plan = exchange_call(
        pair_count, pairs, positions, mass.reshape(flat), smoothing.reshape(flat),
        energy.reshape(flat), destination.reshape(flat), rows, cols)
    plan = plan.reshape(-1)
    density, press, edge, far, base, half, dest, extra = density_call(
        plan, as_tiles(pool), own_tiles)
    press_far = press_call(edge, rows, cols).reshape(4 * GT, LANES)
    accel = accel_call(plan, extra, far, base, half, dest, press, press_far)
    return (density.reshape(-1), accel)


def solution(mesh):
    placed = (
        P(None, ("gx", "gy")),
        P(("gx", "gy")),
        P(("gx", "gy")),
        P(("gx", "gy")),
        P(("gx", "gy"), None),
        P(None, ("gx", "gy")),
        P(("gx", "gy")),
    )
    return jax.shard_map(
        local,
        mesh=mesh,
        in_specs=placed,
        out_specs=(P(("gx", "gy")), P(None, ("gx", "gy"))),
        check_vma=False,
    )
```

```python
import functools
import math

import jax
import jax.numpy as jnp
from jax import lax
from jax.experimental import pallas as pl
from jax.experimental.pallas import tpu as pltpu
from jax.sharding import PartitionSpec as P

GT = 8
LANES = 128
DEPTH = 48
TINY = 1e-12
MESH = pl.DeviceIdType.MESH

KERNEL_NORM = 21.0 / (2.0 * math.pi)
GAMMA_LESS = 2.0 / 3.0


def three(x):
    one = x.astype(jnp.bfloat16).astype(jnp.float32)
    rest = x - one
    two = rest.astype(jnp.bfloat16).astype(jnp.float32)
    return one, two, (rest - two).astype(jnp.bfloat16).astype(jnp.float32)


def source_terms(x):
    one, two, low = three(x)
    return jnp.concatenate([one, two, one, two, low, one], axis=0).astype(jnp.bfloat16)


def target_terms(x):
    one, two, low = three(x)
    return jnp.concatenate([one, one, two, two, one, low], axis=0).astype(jnp.bfloat16)


def put_rows(stage, rows, width, tiles, first=0):
    for k, row in enumerate(rows):
        stage[pl.ds(first + k, tiles, stride=width), :] = row


def equal_rows(row, height, base=0):
    at = lax.broadcasted_iota(jnp.int32, (height, row.shape[-1]), 0) + base
    return jnp.broadcast_to(row, at.shape) == at


def ones_where(mask):
    return jnp.where(mask, 1.0, 0.0).astype(jnp.bfloat16)


def earlier(size, width):
    row = lax.broadcasted_iota(jnp.int32, (size, width), 0)
    col = lax.broadcasted_iota(jnp.int32, (size, width), 1)
    return row, col


def list_pairs(count_ref, pairs_ref, plan_ref, rank_ref, hits_ref, own_tiles, tiles):
    slots = pairs_ref.shape[1]
    live = lax.broadcasted_iota(jnp.int32, (1, slots), 1) < count_ref[0]
    target = jnp.where(live, pairs_ref[0:1, :], -1)
    hits = by_last(ones_where(equal_rows(target, own_tiles)),
                   ones_where(equal_rows(pairs_ref[1:2, :], tiles)))
    fresh = jnp.where(hits > 0.0, 1.0, 0.0)
    row, col = earlier(tiles, tiles)
    far_row, far_col = row >= own_tiles, col >= own_tiles
    inside = jnp.dot(fresh.astype(jnp.bfloat16), ones_where((row < col) & (far_row == far_col)),
                     preferred_element_type=jnp.float32)
    total = jnp.dot(fresh.astype(jnp.bfloat16), ones_where(far_row == far_col),
                    preferred_element_type=jnp.float32)
    row, col = earlier(own_tiles, own_tiles)
    above = jnp.dot(ones_where(col < row), total.astype(jnp.bfloat16),
                    preferred_element_type=jnp.float32)
    all_rows = jnp.sum(total, axis=0, keepdims=True).astype(jnp.int32)
    column = lax.broadcasted_iota(jnp.int32, (own_tiles, tiles), 1)
    place = jnp.where(hits > 0.0, (inside + above).astype(jnp.int32), -1)
    lists = (plan_ref.shape[0] - 2) // 4
    place = jnp.where((column >= own_tiles) & (place >= 0), place + lists * LANES, place)
    rank_ref[...] = place
    hits_ref[...] = hits.astype(jnp.int32)
    source = lax.broadcasted_iota(jnp.int32, (1, tiles), 1).astype(jnp.float32)
    keys = jnp.zeros((2 * lists, LANES), jnp.float32)
    times = jnp.zeros((2 * lists, LANES), jnp.float32)
    for t in range(own_tiles):
        at = rank_ref[t:t + 1, :]
        high = at // LANES
        many = hits_ref[t:t + 1, :]
        upper = many // LANES
        mine = jnp.where(equal_rows(jnp.where(at < 0, -1, high), 2 * lists), 1.0, 0.0)
        parts = [mine * source, mine, mine * upper.astype(jnp.float32),
                 mine * (many - upper * LANES).astype(jnp.float32)]
        found = by_last(jnp.concatenate(parts, axis=0).astype(jnp.bfloat16),
                        ones_where(equal_rows(jnp.where(at < 0, -1, at - high * LANES), LANES)))
        size = 2 * lists
        keys = keys + found[:size] + float(t * tiles) * found[size:2 * size]
        times = times + float(LANES) * found[2 * size:3 * size] + found[3 * size:]
    plan_ref[:2 * lists] = keys.astype(jnp.int32)
    plan_ref[2 * lists:4 * lists] = times.astype(jnp.int32)
    plan_ref[4 * lists:4 * lists + 1] = jnp.broadcast_to(all_rows[:, :1], (1, LANES))
    plan_ref[4 * lists + 1:] = jnp.broadcast_to(all_rows[:, tiles - 1:], (1, LANES))


def order_rows(pos_ref, mass_ref, smooth_ref, energy_ref, dest_ref, sent_ref,
               flags, prefix, rank_ref, rows_ref, index_ref):
    tiles = mass_ref.shape[0]
    domains, width, slots = sent_ref.shape
    row, col = earlier(LANES, 2 * LANES)
    before = ones_where((row < col) | (col >= LANES))
    for t in range(tiles):
        flags[t * domains:(t + 1) * domains] = ones_where(
            equal_rows(dest_ref[t:t + 1, :], domains))
    prefix[...] = jnp.dot(flags[...], before, preferred_element_type=jnp.float32)
    seen = jnp.zeros((domains, LANES), jnp.float32)
    for t in range(tiles):
        part = slice(t * domains, (t + 1) * domains)
        mine = flags[part].astype(jnp.float32)
        rank = jnp.sum(mine * (prefix[part, :LANES] + seen), axis=0, keepdims=True)
        rank_ref[t:t + 1, :] = rank.astype(jnp.int32)
        seen = seen + prefix[part, LANES:]
    place = dest_ref[...] * slots + rank_ref[...]
    block = place // LANES
    rank_ref[...] = place - block * LANES
    lane = lax.broadcasted_iota(jnp.int32, (tiles, LANES), 1).astype(jnp.float32)
    from_lane = jnp.zeros((tiles, LANES), jnp.float32)
    from_tile = jnp.zeros((tiles, LANES), jnp.float32)
    for t in range(tiles):
        picked = equal_rows(block[t:t + 1, :], tiles)
        both = jnp.concatenate([jnp.where(picked, lane, 0.0), jnp.where(picked, 1.0, 0.0)], axis=0)
        found = by_last(both.astype(jnp.bfloat16),
                        ones_where(equal_rows(rank_ref[t:t + 1, :], LANES)))
        from_lane = from_lane + found[:tiles]
        from_tile = from_tile + float(t) * found[tiles:]
    ones = jnp.ones((tiles, LANES), jnp.float32)
    put_rows(rows_ref, [smooth_ref[...], mass_ref[...], energy_ref[...], 0.0 * ones], width, tiles, 4)
    put_rows(rows_ref, [ones], width, tiles, 0)
    for t in range(tiles):
        rows_ref[t * width + 1:t * width + 4, :] = pos_ref[:, t * LANES:(t + 1) * LANES]
    index_ref[0] = from_lane.astype(jnp.int32)
    index_ref[1] = from_tile.astype(jnp.int32)
    per = LANES // slots

    def gather(q, carry):
        at = jnp.broadcast_to(index_ref[0, pl.ds(q, 1), :], (width, LANES))
        tile = jnp.broadcast_to(index_ref[1, pl.ds(q, 1), :], (width, LANES))
        out = jnp.zeros((width, LANES), jnp.float32)
        for t in range(tiles):
            moved = jnp.take_along_axis(rows_ref[t * width:(t + 1) * width, :], at, axis=1)
            out = jnp.where(tile == t, moved, out)
        for p in range(per):
            sent_ref[q * per + p] = out[:, p * slots:(p + 1) * slots]
        return carry

    lax.fori_loop(0, tiles, gather, 0)


def beside(i, j, rows, cols):
    return [(i > 0, (i - 1, j), 1), (i < rows - 1, (i + 1, j), 0),
            (j > 0, (i, j - 1), 3), (j < cols - 1, (i, j + 1), 2)]


def exchange_kernel(count_ref, *refs, rows, cols):
    given, refs = refs[:6], refs[6:]
    pool_ref, listed_ref = refs[:2]
    held, refs = refs[2:8], refs[8:]
    (out_ref, flags, prefix, rank_ref, rows_ref, index_ref, place_ref, hits_ref, plan_ref,
     load_sem, plan_sem, send_sem, recv_sem, edge_send, edge_recv) = refs
    pairs_ref, pos_ref, mass_ref, smooth_ref, energy_ref, dest_ref = held
    loads = [pltpu.make_async_copy(a, b, load_sem.at[k]) for k, (a, b) in enumerate(zip(given, held))]
    for load in loads:
        load.start()
    domains = rows * cols
    tiles = mass_ref.shape[0]
    edge = (pool_ref.shape[0] - domains) // 4
    i, j = lax.axis_index("gx"), lax.axis_index("gy")
    me = i * cols + j
    barrier = pltpu.get_barrier_semaphore()

    def greet(k, carry):
        peer = lax.rem(me + k, domains)
        pl.semaphore_signal(barrier, inc=1, device_id=(peer // cols, lax.rem(peer, cols)),
                            device_id_type=MESH)
        return carry

    lax.fori_loop(1, domains, greet, 0)
    for load in loads:
        load.wait()
    order_rows(pos_ref, mass_ref, smooth_ref, energy_ref, dest_ref, out_ref,
               flags, prefix, rank_ref, rows_ref, index_ref)
    pl.semaphore_wait(barrier, domains - 1)

    def outgoing(peer):
        return pltpu.make_async_remote_copy(
            src_ref=out_ref.at[peer], dst_ref=pool_ref.at[me],
            send_sem=send_sem.at[peer], recv_sem=recv_sem.at[me],
            device_id=(peer // cols, lax.rem(peer, cols)), device_id_type=MESH)

    def incoming(source):
        return pltpu.make_async_remote_copy(
            src_ref=out_ref.at[source], dst_ref=pool_ref.at[source],
            send_sem=send_sem.at[source], recv_sem=recv_sem.at[source],
            device_id=(source // cols, lax.rem(source, cols)), device_id_type=MESH)

    def send(k, carry):
        outgoing(lax.rem(me + k, domains)).start()
        return carry

    lax.fori_loop(1, domains, send, 0)
    pool_ref[me] = out_ref[me]
    list_pairs(count_ref, pairs_ref, plan_ref, place_ref, hits_ref, tiles, tiles + 4 * GT)
    listed = pltpu.make_async_copy(plan_ref, listed_ref, plan_sem)
    listed.start()

    def arrive(source, carry):
        @pl.when(source != me)
        def _():
            incoming(source).wait_recv()
        return carry

    lax.fori_loop(0, edge, arrive, 0)
    sides = beside(i, j, rows, cols)

    def across(side):
        there, peer, slot = sides[side]
        return pltpu.make_async_remote_copy(
            src_ref=pool_ref.at[pl.ds(0, edge)], dst_ref=pool_ref.at[pl.ds(domains + slot * edge, edge)],
            send_sem=edge_send.at[side], recv_sem=edge_recv.at[slot],
            device_id=peer, device_id_type=MESH)

    def back(side):
        there, peer, slot = sides[side]
        return pltpu.make_async_remote_copy(
            src_ref=pool_ref.at[pl.ds(0, edge)], dst_ref=pool_ref.at[pl.ds(domains + side * edge, edge)],
            send_sem=edge_send.at[side], recv_sem=edge_recv.at[side],
            device_id=peer, device_id_type=MESH)

    for side in range(4):
        @pl.when(sides[side][0])
        def _():
            across(side).start()

        @pl.when(jnp.logical_not(sides[side][0]))
        def _():
            pool_ref[domains + side * edge:domains + (side + 1) * edge] = jnp.zeros(
                (edge,) + pool_ref.shape[1:], jnp.float32)

    lax.fori_loop(edge, domains, arrive, 0)

    def left(k, carry):
        outgoing(lax.rem(me + k, domains)).wait_send()
        return carry

    lax.fori_loop(1, domains, left, 0)
    for side in range(4):
        @pl.when(sides[side][0])
        def _():
            across(side).wait_send()
            back(side).wait_recv()

    listed.wait()


def press_kernel(press_ref, ghost_ref, send_sem, recv_sem, rows, cols):
    i, j = lax.axis_index("gx"), lax.axis_index("gy")
    sides = beside(i, j, rows, cols)
    barrier = pltpu.get_barrier_semaphore()
    for there, peer, slot in sides:
        @pl.when(there)
        def _():
            pl.semaphore_signal(barrier, inc=1, device_id=peer, device_id_type=MESH)

    pl.semaphore_wait(barrier, sum(there.astype(jnp.int32) for there, peer, slot in sides))

    def across(side, slot):
        return pltpu.make_async_remote_copy(
            src_ref=press_ref, dst_ref=ghost_ref.at[slot],
            send_sem=send_sem.at[side], recv_sem=recv_sem.at[slot],
            device_id=sides[side][1], device_id_type=MESH)

    for side in range(4):
        @pl.when(sides[side][0])
        def _():
            across(side, sides[side][2]).start()

        @pl.when(jnp.logical_not(sides[side][0]))
        def _():
            ghost_ref[side] = jnp.zeros_like(ghost_ref[side])

    for side in range(4):
        @pl.when(sides[side][0])
        def _():
            across(side, sides[side][2]).wait_send()
            across(side, side).wait_recv()


def one_hot_rows(dest):
    rows = lax.broadcasted_iota(jnp.int32, (LANES, LANES), 0)
    wide = jnp.broadcast_to(dest, (LANES, LANES))
    return jnp.where(wide == rows, 1.0, 0.0).astype(jnp.bfloat16)


def by_last(a, b):
    return lax.dot_general(a, b, (((1,), (1,)), ((), ())), preferred_element_type=jnp.float32)


def sweep(plan_ref, which, tiles, dump, unrolls, together, body):
    length = (plan_ref.shape[0] - 2 * LANES) // 4
    size = plan_ref[4 * length + which * LANES]

    done = 0
    for unroll in unrolls:
        final = unroll == unrolls[-1]

        def advance(block, carry):
            for u in range(0, unroll, together):
                picked = []
                for v in range(together):
                    k = done + block * unroll + u + v
                    if final:
                        live = k < size
                        at = which * length + jnp.minimum(k, length - 1)
                        key = jnp.where(live, plan_ref[at], 0)
                    else:
                        at = which * length + k
                        key = plan_ref[at]
                    target = lax.div(key, tiles)
                    source = key - target * tiles
                    weight = plan_ref[2 * length + at].astype(jnp.float32)
                    place = jnp.where(live, target, dump) if final else target
                    picked.append((target, source, place, weight))
                body(picked)
            return carry

        blocks = lax.div(size - done + (unroll - 1 if final else 0), unroll)
        lax.fori_loop(0, blocks, advance, 0)
        done = done + blocks * unroll


def sweep_extra(plan_ref, extra_ref, tiles, dump, unroll, together, body):
    length = (plan_ref.shape[0] - 2 * LANES) // 4
    size = extra_ref[0]

    def advance(block, carry):
        for u in range(0, unroll, together):
            picked = []
            for v in range(together):
                k = block * unroll + u + v
                live = k < size
                at = length + jnp.where(live, extra_ref[1 + jnp.minimum(k, length - 1)], 0)
                key = jnp.where(live, plan_ref[at], 0)
                target = lax.div(key, tiles)
                source = key - target * tiles
                weight = plan_ref[2 * length + at].astype(jnp.float32)
                picked.append((target, source, jnp.where(live, target, dump), weight))
            body(picked)
        return carry

    lax.fori_loop(0, lax.div(size + unroll - 1, unroll), advance, 0)


def list_extra(plan_ref, rank_ref, extra_ref, own_tiles, tiles, height):
    length = (plan_ref.shape[0] - 2 * LANES) // 4
    size = plan_ref[4 * length + LANES]

    def look(block, found):
        for u in range(8):
            k = jnp.minimum(block * 8 + u, length - 1)
            key = plan_ref[length + k]
            ghost = jnp.maximum(key - lax.div(key, tiles) * tiles - own_tiles, 0)
            long = (block * 8 + u < size) & (rank_ref[ghost, LANES - 1] > height)
            extra_ref[1 + found] = k
            found = found + long.astype(jnp.int32)
        return found

    extra_ref[0] = lax.fori_loop(0, lax.div(size + 7, 8), look, 0)


def in_groups(count, group, body):
    def step(block, carry):
        for u in range(group):
            body(block * group + u)
        return carry

    lax.fori_loop(0, count // group, step, 0)


def tile_rows(ref, t, height=8):
    return ref[pl.ds(pl.multiple_of(t * height, height), height), :]


def put_tile(ref, t, value):
    ref[pl.ds(pl.multiple_of(t * 8, 8), 8), :] = value


def spread_rows(far, wides, first, tiles, height):
    row = lax.broadcasted_iota(jnp.int32, (DEPTH, LANES), 0)
    picks = [jnp.where((row == k) | (row == 8 + k) | (row == 32 + k), scale, 0.0)
             for k, scale, wide in wides]
    picks = jnp.concatenate(picks, axis=1).astype(jnp.bfloat16)

    def one(t):
        spread = jnp.dot(far[first + t, :height], picks, preferred_element_type=jnp.float32)
        for n, (k, scale, wide) in enumerate(wides):
            wide[first + t, :height] = spread[:, n * LANES:(n + 1) * LANES]

    in_groups(tiles, 8, one)


def density_kernel(plan_ref, pool_ref,
                   dens_ref, press_ref, edge_ref, far, base_ref, half_b, dest_ref, extra_ref,
                   near, mass_b, totals, whole, scalar_rank, rank_sem):
    own_tiles = dens_ref.shape[0]
    ghosts = dest_ref.shape[0]
    here_ref = pool_ref.at[pl.ds(0, own_tiles * 8)]
    there_ref = pool_ref.at[pl.ds(own_tiles * 8, ghosts * 8)]
    tiles = own_tiles + ghosts
    row = lax.broadcasted_iota(jnp.int32, (8, LANES), 0)
    spatial = (row >= 1) & (row <= 3)
    first = here_ref[0:8, :]
    low, high, most = first, first, there_ref[0:8, :]
    for t in range(1, own_tiles):
        part = here_ref[t * 8:(t + 1) * 8, :]
        low, high = jnp.minimum(low, part), jnp.maximum(high, part)
    for g in range(1, ghosts):
        most = jnp.maximum(most, there_ref[g * 8:(g + 1) * 8, :])
    low = jnp.min(low, axis=1, keepdims=True)
    high = jnp.max(high, axis=1, keepdims=True)
    most = jnp.maximum(jnp.max(most, axis=1, keepdims=True), high)
    reach = most[4:5, :] + 0.01
    reach = reach * reach
    centre = jnp.where(spatial, 0.5 * (low + high), 0.0)

    def shifted(part):
        moved = part - centre
        norm = jnp.sum(jnp.where(spatial, moved * moved, 0.0), axis=0, keepdims=True)
        return jnp.where(row == 7, norm, moved), norm

    def own(t):
        moved, norm = shifted(tile_rows(here_ref, t))
        put_tile(base_ref, t, moved)
        far[t] = by_last(ones_where(equal_rows(same, LANES)),
                         source_terms(moved)).astype(jnp.bfloat16)
        radius = moved[4:5, :]
        wanted = jnp.where(row == 0, norm, jnp.where(spatial, -2.0 * moved, jnp.where(
            row == 7, 1.0, 0.0)))
        near[t] = target_terms(wanted * (1.0 / (radius * radius)))

    same = lax.broadcasted_iota(jnp.int32, (1, LANES), 1)
    in_groups(own_tiles, 8, own)

    def ghost(g):
        part = tile_rows(there_ref, g)
        gap = jnp.maximum(jnp.maximum(low - part, part - high), 0.0)
        beyond = jnp.sum(jnp.where(spatial, gap * gap, 0.0), axis=0, keepdims=True)
        active = (beyond < reach) & (part[5:6, :] != 0.0)
        totals[0, pl.ds(g, 1), :] = jnp.where(active, 1.0, 0.0)
        moved, norm = shifted(part)
        put_tile(base_ref, own_tiles + g, moved)

    in_groups(ghosts, 8, ghost)
    flags = totals[0, :ghosts, :]
    at, upto = earlier(LANES, LANES)
    rank = jnp.dot(flags.astype(jnp.bfloat16), ones_where(at <= upto),
                   preferred_element_type=jnp.float32)
    dest_ref[...] = jnp.where(flags > 0.0, rank - 1.0, -1.0).astype(jnp.int32)
    totals[0, :ghosts, :] = rank
    slot = lax.broadcasted_iota(jnp.int32, (LANES, DEPTH), 0).astype(jnp.float32)
    term = lax.broadcasted_iota(jnp.int32, (LANES, DEPTH), 1)
    unit = (term == 0) | (term == 16) | (term == 40)
    half = LANES // 2
    more = (jnp.max(rank) > half + 0.5).astype(jnp.int32)
    extra_ref[0] = 0

    @pl.when(more > 0)
    def _():
        whole[...] = rank.astype(jnp.int32)
        copy = pltpu.make_async_copy(whole, scalar_rank, rank_sem)
        copy.start()
        copy.wait()
        list_extra(plan_ref, scalar_rank, extra_ref, own_tiles, tiles, half)


    def squeeze(g):
        moved = by_last(ones_where(equal_rows(dest_ref[pl.ds(g, 1), :], LANES)),
                        source_terms(tile_rows(base_ref, own_tiles + g)))
        unused = slot >= totals[0, pl.ds(g, 1), LANES - 1:]
        far[own_tiles + g] = jnp.where(unit & unused, 1.0, moved).astype(jnp.bfloat16)

    in_groups(ghosts, 8, squeeze)
    wides = [(5, 1.0, mass_b), (4, 0.5, half_b)]
    spread_rows(far, wides, 0, own_tiles, LANES)
    spread_rows(far, wides, own_tiles, ghosts, half)

    @pl.when(more > 0)
    def _():
        spread_rows(far, wides, own_tiles, ghosts, LANES)

    totals[...] = jnp.zeros_like(totals)

    def add(first, height):
        def body(picked):
            (target, source, place, weight), = picked
            sq = jnp.dot(far[source, first:first + height], near[target],
                         preferred_element_type=jnp.float32)
            sq = jnp.maximum(sq, TINY)
            ratio = sq * lax.rsqrt(sq)
            falloff = jnp.maximum(1.0 - ratio, 0.0)
            falloff = falloff * falloff
            term = falloff * falloff * ((ratio + 0.25) * mass_b[source, first:first + height])
            summed = jnp.sum(term.reshape(height // 8, 8, LANES), axis=0)
            totals[place, :8] += weight * summed
        return body

    sweep(plan_ref, 0, tiles, own_tiles, (64, 16), 1, add(0, LANES))
    sweep(plan_ref, 1, tiles, own_tiles, (96, 32), 1, add(0, half))

    @pl.when(more > 0)
    def _():
        sweep_extra(plan_ref, extra_ref, tiles, own_tiles, 8, 1, add(half, half))

    def field(k):
        return here_ref[pl.ds(k, own_tiles, stride=8), :]

    summed = jnp.sum(totals[:own_tiles, :8], axis=1)
    radius = field(4)
    density = KERNEL_NORM / (radius * radius * radius) * (4.0 * summed + field(5))
    dens_ref[...] = density
    press = GAMMA_LESS * field(6) / density
    press_ref[...] = press
    edge_ref[...] = press[:GT]


def accel_kernel(plan_ref, extra_ref, far, base_ref, half_b, dest_ref,
                 press_ref, press_far_ref, out_ref, near, left, left_half, totals, half_a):
    own_tiles = press_ref.shape[0]
    ghosts = dest_ref.shape[0]
    tiles = own_tiles + ghosts
    half = LANES // 2
    row = lax.broadcasted_iota(jnp.int32, (8, LANES), 0)
    spatial = (row >= 1) & (row <= 3)

    def loaded(part, press):
        twice = jnp.where(row < 4, part, pltpu.roll(part, 4, 0)) * part[5:6, :]
        one, two, low = three(jnp.where(row < 4, twice, twice * press))
        return jnp.concatenate([one, two], axis=0).astype(jnp.bfloat16)

    def own(t):
        part = tile_rows(base_ref, t)
        wanted = jnp.where(row == 0, part[7:8, :], jnp.where(spatial, -2.0 * part, jnp.where(
            row == 7, 1.0, 0.0)))
        half_a[pl.ds(t, 1), :] = 0.5 * part[4:5, :]
        near[t] = target_terms(wanted)
        rows = loaded(part, press_ref[pl.ds(t, 1), :])
        left[t] = jnp.concatenate([rows, rows], axis=1)

    in_groups(own_tiles, 8, own)

    def ghost(g):
        rows = loaded(tile_rows(base_ref, own_tiles + g), press_far_ref[pl.ds(g, 1), :])
        moved = by_last(rows, ones_where(equal_rows(dest_ref[pl.ds(g, 1), :], LANES)))
        moved = moved.astype(jnp.bfloat16)
        none = jnp.zeros((16, LANES), jnp.bfloat16)
        for v in range(2):
            piece = moved[:, v * half:(v + 1) * half]
            two = jnp.concatenate([piece, piece], axis=1)
            left_half[v, 0, g] = jnp.concatenate([two, none], axis=1)
            left_half[v, 1, g] = jnp.concatenate([none, two], axis=1)

    in_groups(ghosts, 8, ghost)
    totals[...] = jnp.zeros_like(totals)

    def slopes(source, target, first, height):
        sq = jnp.dot(far[source, first:first + height], near[target],
                     preferred_element_type=jnp.float32)
        radius = half_b[source, first:first + height] + half_a[pl.ds(target, 1), :]
        sq = jnp.maximum(sq, TINY)
        dist = sq * lax.rsqrt(sq)
        inv = pl.reciprocal(radius, approx=True)
        wide = inv * inv
        fall = jnp.maximum(inv - dist * wide, 0.0)
        slope = fall * fall * (fall * wide)
        high = slope.astype(jnp.bfloat16)
        low = (slope - high.astype(jnp.float32)).astype(jnp.bfloat16)
        return [high, low]

    def add_one(picked):
        (target, source, place, weight), = picked
        terms = jnp.concatenate(slopes(source, target, 0, LANES), axis=0)
        totals[place] += weight * jnp.dot(left[source], terms, preferred_element_type=jnp.float32)

    def add_two(v):
        def body(both):
            terms, lhs = [], []
            for side, (target, source, place, weight) in enumerate(both):
                terms += slopes(source, target, v * half, half)
                lhs.append(left_half[v, side, jnp.maximum(source - own_tiles, 0)])
            moved = jnp.dot(jnp.concatenate(lhs, axis=0), jnp.concatenate(terms, axis=0),
                            preferred_element_type=jnp.float32)
            for side, (target, source, place, weight) in enumerate(both):
                totals[place] += weight * moved[side * 16:(side + 1) * 16]
        return body

    sweep(plan_ref, 0, tiles, own_tiles, (64, 16), 1, add_one)
    sweep(plan_ref, 1, tiles, own_tiles, (64, 32), 2, add_two(0))

    @pl.when(extra_ref[0] > 0)
    def _():
        sweep_extra(plan_ref, extra_ref, tiles, own_tiles, 8, 2, add_two(1))

    for t in range(own_tiles):
        both = totals[t, :8] + totals[t, 8:]
        mixed = jnp.where(row < 4, both * press_ref[t:t + 1, :], both)
        mixed = mixed + pltpu.roll(mixed, 4, 0)
        pulled = 20.0 * KERNEL_NORM * (base_ref[t * 8:(t + 1) * 8, :] * mixed[0:1, :] - mixed)
        out_ref[:, t * LANES:(t + 1) * LANES] = pulled[1:4, :]


SMEM = pl.BlockSpec(memory_space=pltpu.SMEM)
VMEM = pl.BlockSpec(memory_space=pltpu.VMEM)
HBM = pl.BlockSpec(memory_space=pltpu.HBM)
GRANT = 24 * 2 ** 20
WHOLE = 60 * 2 ** 20


def exchange_call(count, pairs, positions, mass, smoothing, energy, destination, rows, cols):
    tiles = mass.shape[0]
    pool_tiles = tiles + 4 * GT
    lists = 2 * pl.cdiv(tiles * max(tiles, 4 * GT), LANES)
    domains = rows * cols
    slots = tiles * LANES // domains
    edge = GT * LANES // slots
    dma = pltpu.SemaphoreType.DMA
    given = (pairs, positions, mass, smoothing, energy, destination)
    return pl.pallas_call(
        functools.partial(exchange_kernel, rows=rows, cols=cols),
        out_shape=(
            jax.ShapeDtypeStruct((domains + 4 * edge, 8, slots), jnp.float32),
            jax.ShapeDtypeStruct((2 * lists + 2, LANES), jnp.int32),
        ),
        in_specs=[SMEM] + [HBM] * 6,
        out_specs=[VMEM, HBM],
        scratch_shapes=[pltpu.VMEM(x.shape, x.dtype) for x in given] + [
            pltpu.VMEM((domains, 8, slots), jnp.float32),
            pltpu.VMEM((tiles * domains, LANES), jnp.bfloat16),
            pltpu.VMEM((tiles * domains, 2 * LANES), jnp.float32),
            pltpu.VMEM((tiles, LANES), jnp.int32),
            pltpu.VMEM((tiles * 8, LANES), jnp.float32),
            pltpu.VMEM((2, tiles, LANES), jnp.int32),
            pltpu.VMEM((tiles, pool_tiles), jnp.int32),
            pltpu.VMEM((tiles, pool_tiles), jnp.int32),
            pltpu.VMEM((2 * lists + 2, LANES), jnp.int32),
            dma((6,)), dma, dma((domains,)), dma((domains,)), dma((4,)), dma((4,)),
        ],
        compiler_params=pltpu.CompilerParams(
            collective_id=0, has_side_effects=True, vmem_limit_bytes=WHOLE),
        name="exchange",
    )(count, *given)


def press_call(press, rows, cols):
    dma = pltpu.SemaphoreType.DMA
    return pl.pallas_call(
        functools.partial(press_kernel, rows=rows, cols=cols),
        out_shape=jax.ShapeDtypeStruct((4,) + press.shape, jnp.float32),
        in_specs=[VMEM],
        out_specs=VMEM,
        scratch_shapes=[dma((4,)), dma((4,))],
        compiler_params=pltpu.CompilerParams(collective_id=1, has_side_effects=True, vmem_limit_bytes=GRANT),
        name="press",
    )(press)


def density_call(plan, pool, own_tiles):
    tiles = pool.shape[0] // 8
    ghosts = tiles - own_tiles
    lists = (plan.shape[0] // LANES - 2) // 4
    flat = jax.ShapeDtypeStruct((own_tiles, LANES), jnp.float32)
    return pl.pallas_call(
        density_kernel,
        out_shape=(
            flat,
            flat,
            jax.ShapeDtypeStruct((GT, LANES), jnp.float32),
            jax.ShapeDtypeStruct((tiles, LANES, DEPTH), jnp.bfloat16),
            jax.ShapeDtypeStruct((tiles * 8, LANES), jnp.float32),
            jax.ShapeDtypeStruct((tiles, LANES, LANES), jnp.float32),
            jax.ShapeDtypeStruct((ghosts, LANES), jnp.int32),
            jax.ShapeDtypeStruct((lists * LANES + LANES,), jnp.int32),
        ),
        in_specs=[SMEM, VMEM],
        out_specs=(VMEM,) * 7 + (SMEM,),
        scratch_shapes=[
            pltpu.VMEM((own_tiles, DEPTH, LANES), jnp.bfloat16),
            pltpu.VMEM((tiles, LANES, LANES), jnp.float32),
            pltpu.VMEM((own_tiles + 1, max(8, ghosts), LANES), jnp.float32),
            pltpu.VMEM((ghosts, LANES), jnp.int32),
            pltpu.SMEM((ghosts, LANES), jnp.int32),
            pltpu.SemaphoreType.DMA,
        ],
        compiler_params=pltpu.CompilerParams(vmem_limit_bytes=GRANT),
        name="density",
    )(plan, pool)


def accel_call(plan, extra, far, base, half, dest, press, press_far):
    own_tiles, ghosts = press.shape[0], dest.shape[0]
    return pl.pallas_call(
        accel_kernel,
        out_shape=jax.ShapeDtypeStruct((3, own_tiles * LANES), jnp.float32),
        in_specs=[SMEM] * 2 + [VMEM] * 6,
        out_specs=VMEM,
        scratch_shapes=[
            pltpu.VMEM((own_tiles, DEPTH, LANES), jnp.bfloat16),
            pltpu.VMEM((own_tiles, 16, 2 * LANES), jnp.bfloat16),
            pltpu.VMEM((2, 2, ghosts, 16, 2 * LANES), jnp.bfloat16),
            pltpu.VMEM((own_tiles + 1, 16, LANES), jnp.float32),
            pltpu.VMEM((own_tiles, LANES), jnp.float32),
        ],
        compiler_params=pltpu.CompilerParams(vmem_limit_bytes=GRANT),
        name="accel",
    )(plan, extra, far, base, half, dest, press, press_far)


def as_tiles(blocks):
    count, fields, slots = blocks.shape
    per = LANES // slots
    joined = blocks.reshape(count // per, per, fields, slots).transpose(0, 2, 1, 3)
    return joined.reshape(count // per * fields, LANES)


def local(positions, mass, smoothing, energy, destination, pairs, pair_count):
    rows = lax.axis_size("gx")
    cols = lax.axis_size("gy")
    own_tiles = mass.shape[0] // LANES
    flat = (own_tiles, LANES)
    pool, plan = exchange_call(
        pair_count, pairs, positions, mass.reshape(flat), smoothing.reshape(flat),
        energy.reshape(flat), destination.reshape(flat), rows, cols)
    plan = plan.reshape(-1)
    density, press, edge, far, base, half, dest, extra = density_call(
        plan, as_tiles(pool), own_tiles)
    press_far = press_call(edge, rows, cols).reshape(4 * GT, LANES)
    accel = accel_call(plan, extra, far, base, half, dest, press, press_far)
    return (density.reshape(-1), accel)


def solution(mesh):
    placed = (
        P(None, ("gx", "gy")),
        P(("gx", "gy")),
        P(("gx", "gy")),
        P(("gx", "gy")),
        P(("gx", "gy"), None),
        P(None, ("gx", "gy")),
        P(("gx", "gy")),
    )
    return jax.shard_map(
        local,
        mesh=mesh,
        in_specs=placed,
        out_specs=(P(("gx", "gy")), P(None, ("gx", "gy"))),
        check_vma=False,
    )
```

```python
import functools
import math

import jax
import jax.numpy as jnp
from jax import lax
from jax.experimental import pallas as pl
from jax.experimental.pallas import tpu as pltpu
from jax.sharding import PartitionSpec as P

GT = 8
LANES = 128
DEPTH = 48
TINY = 1e-12
MESH = pl.DeviceIdType.MESH

KERNEL_NORM = 21.0 / (2.0 * math.pi)
GAMMA_LESS = 2.0 / 3.0


def three(x):
    one = x.astype(jnp.bfloat16).astype(jnp.float32)
    rest = x - one
    two = rest.astype(jnp.bfloat16).astype(jnp.float32)
    return one, two, (rest - two).astype(jnp.bfloat16).astype(jnp.float32)


def source_terms(x):
    one, two, low = three(x)
    return jnp.concatenate([one, two, one, two, low, one], axis=0).astype(jnp.bfloat16)


def target_terms(x):
    one, two, low = three(x)
    return jnp.concatenate([one, one, two, two, one, low], axis=0).astype(jnp.bfloat16)


def put_rows(stage, rows, width, tiles, first=0):
    for k, row in enumerate(rows):
        stage[pl.ds(first + k, tiles, stride=width), :] = row


def equal_rows(row, height, base=0):
    at = lax.broadcasted_iota(jnp.int32, (height, row.shape[-1]), 0) + base
    return jnp.broadcast_to(row, at.shape) == at


def ones_where(mask):
    return jnp.where(mask, 1.0, 0.0).astype(jnp.bfloat16)


def earlier(size, width):
    row = lax.broadcasted_iota(jnp.int32, (size, width), 0)
    col = lax.broadcasted_iota(jnp.int32, (size, width), 1)
    return row, col


def list_pairs(count_ref, pairs_ref, plan_ref, rank_ref, hits_ref, own_tiles, tiles):
    slots = pairs_ref.shape[1]
    live = lax.broadcasted_iota(jnp.int32, (1, slots), 1) < count_ref[0]
    target = jnp.where(live, pairs_ref[0:1, :], -1)
    hits = by_last(ones_where(equal_rows(target, own_tiles)),
                   ones_where(equal_rows(pairs_ref[1:2, :], tiles)))
    fresh = jnp.where(hits > 0.0, 1.0, 0.0)
    row, col = earlier(tiles, tiles)
    far_row, far_col = row >= own_tiles, col >= own_tiles
    inside = jnp.dot(fresh.astype(jnp.bfloat16), ones_where((row < col) & (far_row == far_col)),
                     preferred_element_type=jnp.float32)
    total = jnp.dot(fresh.astype(jnp.bfloat16), ones_where(far_row == far_col),
                    preferred_element_type=jnp.float32)
    row, col = earlier(own_tiles, own_tiles)
    above = jnp.dot(ones_where(col < row), total.astype(jnp.bfloat16),
                    preferred_element_type=jnp.float32)
    all_rows = jnp.sum(total, axis=0, keepdims=True).astype(jnp.int32)
    column = lax.broadcasted_iota(jnp.int32, (own_tiles, tiles), 1)
    place = jnp.where(hits > 0.0, (inside + above).astype(jnp.int32), -1)
    lists = (plan_ref.shape[0] - 2) // 4
    place = jnp.where((column >= own_tiles) & (place >= 0), place + lists * LANES, place)
    rank_ref[...] = place
    hits_ref[...] = hits.astype(jnp.int32)
    source = lax.broadcasted_iota(jnp.int32, (1, tiles), 1).astype(jnp.float32)
    keys = jnp.zeros((2 * lists, LANES), jnp.float32)
    times = jnp.zeros((2 * lists, LANES), jnp.float32)
    for t in range(own_tiles):
        at = rank_ref[t:t + 1, :]
        high = at // LANES
        many = hits_ref[t:t + 1, :]
        upper = many // LANES
        mine = jnp.where(equal_rows(jnp.where(at < 0, -1, high), 2 * lists), 1.0, 0.0)
        parts = [mine * source, mine, mine * upper.astype(jnp.float32),
                 mine * (many - upper * LANES).astype(jnp.float32)]
        found = by_last(jnp.concatenate(parts, axis=0).astype(jnp.bfloat16),
                        ones_where(equal_rows(jnp.where(at < 0, -1, at - high * LANES), LANES)))
        size = 2 * lists
        keys = keys + found[:size] + float(t * tiles) * found[size:2 * size]
        times = times + float(LANES) * found[2 * size:3 * size] + found[3 * size:]
    plan_ref[:2 * lists] = keys.astype(jnp.int32)
    plan_ref[2 * lists:4 * lists] = times.astype(jnp.int32)
    plan_ref[4 * lists:4 * lists + 1] = jnp.broadcast_to(all_rows[:, :1], (1, LANES))
    plan_ref[4 * lists + 1:] = jnp.broadcast_to(all_rows[:, tiles - 1:], (1, LANES))


def order_rows(pos_ref, mass_ref, smooth_ref, energy_ref, dest_ref, sent_ref,
               flags, prefix, rank_ref, rows_ref, index_ref):
    tiles = mass_ref.shape[0]
    domains, width, slots = sent_ref.shape
    row, col = earlier(LANES, 2 * LANES)
    before = ones_where((row < col) | (col >= LANES))
    for t in range(tiles):
        flags[t * domains:(t + 1) * domains] = ones_where(
            equal_rows(dest_ref[t:t + 1, :], domains))
    prefix[...] = jnp.dot(flags[...], before, preferred_element_type=jnp.float32)
    seen = jnp.zeros((domains, LANES), jnp.float32)
    for t in range(tiles):
        part = slice(t * domains, (t + 1) * domains)
        mine = flags[part].astype(jnp.float32)
        rank = jnp.sum(mine * (prefix[part, :LANES] + seen), axis=0, keepdims=True)
        rank_ref[t:t + 1, :] = rank.astype(jnp.int32)
        seen = seen + prefix[part, LANES:]
    place = dest_ref[...] * slots + rank_ref[...]
    block = place // LANES
    rank_ref[...] = place - block * LANES
    lane = lax.broadcasted_iota(jnp.int32, (tiles, LANES), 1).astype(jnp.float32)
    from_lane = jnp.zeros((tiles, LANES), jnp.float32)
    from_tile = jnp.zeros((tiles, LANES), jnp.float32)
    for t in range(tiles):
        picked = equal_rows(block[t:t + 1, :], tiles)
        both = jnp.concatenate([jnp.where(picked, lane, 0.0), jnp.where(picked, 1.0, 0.0)], axis=0)
        found = by_last(both.astype(jnp.bfloat16),
                        ones_where(equal_rows(rank_ref[t:t + 1, :], LANES)))
        from_lane = from_lane + found[:tiles]
        from_tile = from_tile + float(t) * found[tiles:]
    ones = jnp.ones((tiles, LANES), jnp.float32)
    put_rows(rows_ref, [smooth_ref[...], mass_ref[...], energy_ref[...], 0.0 * ones], width, tiles, 4)
    put_rows(rows_ref, [ones], width, tiles, 0)
    for t in range(tiles):
        rows_ref[t * width + 1:t * width + 4, :] = pos_ref[:, t * LANES:(t + 1) * LANES]
    index_ref[0] = from_lane.astype(jnp.int32)
    index_ref[1] = from_tile.astype(jnp.int32)
    per = LANES // slots

    def gather(q, carry):
        at = jnp.broadcast_to(index_ref[0, pl.ds(q, 1), :], (width, LANES))
        tile = jnp.broadcast_to(index_ref[1, pl.ds(q, 1), :], (width, LANES))
        out = jnp.zeros((width, LANES), jnp.float32)
        for t in range(tiles):
            moved = jnp.take_along_axis(rows_ref[t * width:(t + 1) * width, :], at, axis=1)
            out = jnp.where(tile == t, moved, out)
        for p in range(per):
            sent_ref[q * per + p] = out[:, p * slots:(p + 1) * slots]
        return carry

    lax.fori_loop(0, tiles, gather, 0)


def beside(i, j, rows, cols):
    return [(i > 0, (i - 1, j), 1), (i < rows - 1, (i + 1, j), 0),
            (j > 0, (i, j - 1), 3), (j < cols - 1, (i, j + 1), 2)]


def exchange_kernel(count_ref, *refs, rows, cols):
    given, refs = refs[:6], refs[6:]
    pool_ref, listed_ref = refs[:2]
    held, refs = refs[2:8], refs[8:]
    (out_ref, flags, prefix, rank_ref, rows_ref, index_ref, place_ref, hits_ref, plan_ref,
     blank, load_sem, plan_sem, stay_sem, send_sem, recv_sem, edge_send, edge_recv) = refs
    pairs_ref, pos_ref, mass_ref, smooth_ref, energy_ref, dest_ref = held
    loads = [pltpu.make_async_copy(a, b, load_sem.at[k]) for k, (a, b) in enumerate(zip(given, held))]
    for load in loads:
        load.start()
    domains = rows * cols
    tiles = mass_ref.shape[0]
    edge = (pool_ref.shape[0] - domains) // 4
    i, j = lax.axis_index("gx"), lax.axis_index("gy")
    me = i * cols + j
    barrier = pltpu.get_barrier_semaphore()

    def greet(k, carry):
        peer = lax.rem(me + k, domains)
        pl.semaphore_signal(barrier, inc=1, device_id=(peer // cols, lax.rem(peer, cols)),
                            device_id_type=MESH)
        return carry

    lax.fori_loop(1, domains, greet, 0)
    for load in loads:
        load.wait()
    order_rows(pos_ref, mass_ref, smooth_ref, energy_ref, dest_ref, out_ref,
               flags, prefix, rank_ref, rows_ref, index_ref)
    pl.semaphore_wait(barrier, domains - 1)

    def outgoing(peer):
        return pltpu.make_async_remote_copy(
            src_ref=out_ref.at[peer], dst_ref=pool_ref.at[me],
            send_sem=send_sem.at[peer], recv_sem=recv_sem.at[me],
            device_id=(peer // cols, lax.rem(peer, cols)), device_id_type=MESH)

    def incoming(source):
        return pltpu.make_async_remote_copy(
            src_ref=out_ref.at[source], dst_ref=pool_ref.at[source],
            send_sem=send_sem.at[source], recv_sem=recv_sem.at[source],
            device_id=(source // cols, lax.rem(source, cols)), device_id_type=MESH)

    def send(k, carry):
        outgoing(lax.rem(me + k, domains)).start()
        return carry

    lax.fori_loop(1, domains, send, 0)
    stay = pltpu.make_async_copy(out_ref.at[me], pool_ref.at[me], stay_sem)
    stay.start()
    blank[...] = jnp.zeros_like(blank)
    list_pairs(count_ref, pairs_ref, plan_ref, place_ref, hits_ref, tiles, tiles + 4 * GT)
    listed = pltpu.make_async_copy(plan_ref, listed_ref, plan_sem)
    listed.start()

    def arrive(source, carry):
        @pl.when(source != me)
        def _():
            incoming(source).wait_recv()
        return carry

    stay.wait()
    lax.fori_loop(0, edge, arrive, 0)
    sides = beside(i, j, rows, cols)

    def across(side):
        there, peer, slot = sides[side]
        return pltpu.make_async_remote_copy(
            src_ref=pool_ref.at[pl.ds(0, edge)], dst_ref=pool_ref.at[pl.ds(domains + slot * edge, edge)],
            send_sem=edge_send.at[side], recv_sem=edge_recv.at[slot],
            device_id=peer, device_id_type=MESH)

    def clear(side):
        return pltpu.make_async_copy(
            blank, pool_ref.at[pl.ds(domains + side * edge, edge)], edge_recv.at[side])

    def back(side):
        there, peer, slot = sides[side]
        return pltpu.make_async_remote_copy(
            src_ref=pool_ref.at[pl.ds(0, edge)], dst_ref=pool_ref.at[pl.ds(domains + side * edge, edge)],
            send_sem=edge_send.at[side], recv_sem=edge_recv.at[side],
            device_id=peer, device_id_type=MESH)

    for side in range(4):
        @pl.when(sides[side][0])
        def _():
            across(side).start()

        @pl.when(jnp.logical_not(sides[side][0]))
        def _():
            clear(side).start()

    lax.fori_loop(edge, domains, arrive, 0)

    def left(k, carry):
        outgoing(lax.rem(me + k, domains)).wait_send()
        return carry

    lax.fori_loop(1, domains, left, 0)
    for side in range(4):
        @pl.when(sides[side][0])
        def _():
            across(side).wait_send()
            back(side).wait_recv()

        @pl.when(jnp.logical_not(sides[side][0]))
        def _():
            clear(side).wait()

    listed.wait()


def press_kernel(press_ref, ghost_ref, send_sem, recv_sem, rows, cols):
    i, j = lax.axis_index("gx"), lax.axis_index("gy")
    sides = beside(i, j, rows, cols)
    barrier = pltpu.get_barrier_semaphore()
    for there, peer, slot in sides:
        @pl.when(there)
        def _():
            pl.semaphore_signal(barrier, inc=1, device_id=peer, device_id_type=MESH)

    pl.semaphore_wait(barrier, sum(there.astype(jnp.int32) for there, peer, slot in sides))

    def across(side, slot):
        return pltpu.make_async_remote_copy(
            src_ref=press_ref, dst_ref=ghost_ref.at[slot],
            send_sem=send_sem.at[side], recv_sem=recv_sem.at[slot],
            device_id=sides[side][1], device_id_type=MESH)

    for side in range(4):
        @pl.when(sides[side][0])
        def _():
            across(side, sides[side][2]).start()

        @pl.when(jnp.logical_not(sides[side][0]))
        def _():
            ghost_ref[side] = jnp.zeros_like(ghost_ref[side])

    for side in range(4):
        @pl.when(sides[side][0])
        def _():
            across(side, sides[side][2]).wait_send()
            across(side, side).wait_recv()


def one_hot_rows(dest):
    rows = lax.broadcasted_iota(jnp.int32, (LANES, LANES), 0)
    wide = jnp.broadcast_to(dest, (LANES, LANES))
    return jnp.where(wide == rows, 1.0, 0.0).astype(jnp.bfloat16)


def by_last(a, b):
    return lax.dot_general(a, b, (((1,), (1,)), ((), ())), preferred_element_type=jnp.float32)


def sweep(plan_ref, which, tiles, dump, unrolls, together, body):
    length = (plan_ref.shape[0] - 2 * LANES) // 4
    size = plan_ref[4 * length + which * LANES]

    done = 0
    for unroll in unrolls:
        final = unroll == unrolls[-1]

        def advance(block, carry):
            for u in range(0, unroll, together):
                picked = []
                for v in range(together):
                    k = done + block * unroll + u + v
                    if final:
                        live = k < size
                        at = which * length + jnp.minimum(k, length - 1)
                        key = jnp.where(live, plan_ref[at], 0)
                    else:
                        at = which * length + k
                        key = plan_ref[at]
                    target = lax.div(key, tiles)
                    source = key - target * tiles
                    weight = plan_ref[2 * length + at].astype(jnp.float32)
                    place = jnp.where(live, target, dump) if final else target
                    picked.append((target, source, place, weight))
                body(picked)
            return carry

        blocks = lax.div(size - done + (unroll - 1 if final else 0), unroll)
        lax.fori_loop(0, blocks, advance, 0)
        done = done + blocks * unroll


def sweep_extra(plan_ref, extra_ref, tiles, dump, unroll, together, body):
    length = (plan_ref.shape[0] - 2 * LANES) // 4
    size = extra_ref[0]

    def advance(block, carry):
        for u in range(0, unroll, together):
            picked = []
            for v in range(together):
                k = block * unroll + u + v
                live = k < size
                at = length + jnp.where(live, extra_ref[1 + jnp.minimum(k, length - 1)], 0)
                key = jnp.where(live, plan_ref[at], 0)
                target = lax.div(key, tiles)
                source = key - target * tiles
                weight = plan_ref[2 * length + at].astype(jnp.float32)
                picked.append((target, source, jnp.where(live, target, dump), weight))
            body(picked)
        return carry

    lax.fori_loop(0, lax.div(size + unroll - 1, unroll), advance, 0)


def list_extra(plan_ref, rank_ref, extra_ref, own_tiles, tiles, height):
    length = (plan_ref.shape[0] - 2 * LANES) // 4
    size = plan_ref[4 * length + LANES]

    def look(block, found):
        for u in range(8):
            k = jnp.minimum(block * 8 + u, length - 1)
            key = plan_ref[length + k]
            ghost = jnp.maximum(key - lax.div(key, tiles) * tiles - own_tiles, 0)
            long = (block * 8 + u < size) & (rank_ref[ghost, LANES - 1] > height)
            extra_ref[1 + found] = k
            found = found + long.astype(jnp.int32)
        return found

    extra_ref[0] = lax.fori_loop(0, lax.div(size + 7, 8), look, 0)


def in_groups(count, group, body):
    def step(block, carry):
        for u in range(group):
            body(block * group + u)
        return carry

    lax.fori_loop(0, count // group, step, 0)


def tile_rows(ref, t, height=8):
    return ref[pl.ds(pl.multiple_of(t * height, height), height), :]


def put_tile(ref, t, value):
    ref[pl.ds(pl.multiple_of(t * 8, 8), 8), :] = value


def spread_rows(far, wides, first, tiles, height):
    row = lax.broadcasted_iota(jnp.int32, (DEPTH, LANES), 0)
    picks = [jnp.where((row == k) | (row == 8 + k) | (row == 32 + k), scale, 0.0)
             for k, scale, wide in wides]
    picks = jnp.concatenate(picks, axis=1).astype(jnp.bfloat16)

    def one(t):
        spread = jnp.dot(far[first + t, :height], picks, preferred_element_type=jnp.float32)
        for n, (k, scale, wide) in enumerate(wides):
            wide[first + t, :height] = spread[:, n * LANES:(n + 1) * LANES]

    in_groups(tiles, 8, one)


def density_kernel(plan_ref, pool_ref,
                   dens_ref, press_ref, edge_ref, far, base_ref, half_b, dest_ref, extra_ref,
                   near, mass_b, totals, whole, scalar_rank, rank_sem):
    own_tiles = dens_ref.shape[0]
    ghosts = dest_ref.shape[0]
    here_ref = pool_ref.at[pl.ds(0, own_tiles * 8)]
    there_ref = pool_ref.at[pl.ds(own_tiles * 8, ghosts * 8)]
    tiles = own_tiles + ghosts
    row = lax.broadcasted_iota(jnp.int32, (8, LANES), 0)
    spatial = (row >= 1) & (row <= 3)
    first = here_ref[0:8, :]
    low, high, most = first, first, there_ref[0:8, :]
    for t in range(1, own_tiles):
        part = here_ref[t * 8:(t + 1) * 8, :]
        low, high = jnp.minimum(low, part), jnp.maximum(high, part)
    for g in range(1, ghosts):
        most = jnp.maximum(most, there_ref[g * 8:(g + 1) * 8, :])
    low = jnp.min(low, axis=1, keepdims=True)
    high = jnp.max(high, axis=1, keepdims=True)
    most = jnp.maximum(jnp.max(most, axis=1, keepdims=True), high)
    reach = most[4:5, :] + 0.01
    reach = reach * reach
    centre = jnp.where(spatial, 0.5 * (low + high), 0.0)

    def shifted(part):
        moved = part - centre
        norm = jnp.sum(jnp.where(spatial, moved * moved, 0.0), axis=0, keepdims=True)
        return jnp.where(row == 7, norm, moved), norm

    def own(t):
        moved, norm = shifted(tile_rows(here_ref, t))
        put_tile(base_ref, t, moved)
        far[t] = by_last(ones_where(equal_rows(same, LANES)),
                         source_terms(moved)).astype(jnp.bfloat16)
        radius = moved[4:5, :]
        wanted = jnp.where(row == 0, norm, jnp.where(spatial, -2.0 * moved, jnp.where(
            row == 7, 1.0, 0.0)))
        near[t] = target_terms(wanted * (1.0 / (radius * radius)))

    same = lax.broadcasted_iota(jnp.int32, (1, LANES), 1)
    in_groups(own_tiles, 8, own)

    def ghost(g):
        part = tile_rows(there_ref, g)
        gap = jnp.maximum(jnp.maximum(low - part, part - high), 0.0)
        beyond = jnp.sum(jnp.where(spatial, gap * gap, 0.0), axis=0, keepdims=True)
        active = (beyond < reach) & (part[5:6, :] != 0.0)
        totals[0, pl.ds(g, 1), :] = jnp.where(active, 1.0, 0.0)
        moved, norm = shifted(part)
        put_tile(base_ref, own_tiles + g, moved)

    in_groups(ghosts, 8, ghost)
    flags = totals[0, :ghosts, :]
    at, upto = earlier(LANES, LANES)
    rank = jnp.dot(flags.astype(jnp.bfloat16), ones_where(at <= upto),
                   preferred_element_type=jnp.float32)
    dest_ref[...] = jnp.where(flags > 0.0, rank - 1.0, -1.0).astype(jnp.int32)
    totals[0, :ghosts, :] = rank
    slot = lax.broadcasted_iota(jnp.int32, (LANES // 2, DEPTH), 0).astype(jnp.float32)
    term = lax.broadcasted_iota(jnp.int32, (LANES // 2, DEPTH), 1)
    unit = (term == 0) | (term == 16) | (term == 40)
    half = LANES // 2
    more = (jnp.max(rank) > half + 0.5).astype(jnp.int32)
    extra_ref[0] = 0

    @pl.when(more > 0)
    def _():
        whole[...] = rank.astype(jnp.int32)
        copy = pltpu.make_async_copy(whole, scalar_rank, rank_sem)
        copy.start()
        copy.wait()
        list_extra(plan_ref, scalar_rank, extra_ref, own_tiles, tiles, half)


    def squeeze(first):
        def body(g):
            moved = by_last(ones_where(equal_rows(dest_ref[pl.ds(g, 1), :], half, first)),
                            source_terms(tile_rows(base_ref, own_tiles + g)))
            unused = slot >= totals[0, pl.ds(g, 1), LANES - 1:] - float(first)
            far[own_tiles + g, first:first + half] = jnp.where(
                unit & unused, 1.0, moved).astype(jnp.bfloat16)
        return body

    in_groups(ghosts, 8, squeeze(0))

    @pl.when(more > 0)
    def _():
        in_groups(ghosts, 8, squeeze(half))

    wides = [(5, 1.0, mass_b), (4, 0.5, half_b)]
    spread_rows(far, wides, 0, own_tiles, LANES)
    spread_rows(far, wides, own_tiles, ghosts, half)

    @pl.when(more > 0)
    def _():
        spread_rows(far, wides, own_tiles, ghosts, LANES)

    totals[...] = jnp.zeros_like(totals)

    def add(first, height):
        def body(picked):
            (target, source, place, weight), = picked
            sq = jnp.dot(far[source, first:first + height], near[target],
                         preferred_element_type=jnp.float32)
            sq = jnp.maximum(sq, TINY)
            ratio = sq * lax.rsqrt(sq)
            falloff = jnp.maximum(1.0 - ratio, 0.0)
            falloff = falloff * falloff
            term = falloff * falloff * ((ratio + 0.25) * mass_b[source, first:first + height])
            summed = jnp.sum(term.reshape(height // 8, 8, LANES), axis=0)
            totals[place, :8] += weight * summed
        return body

    sweep(plan_ref, 0, tiles, own_tiles, (64, 16), 1, add(0, LANES))
    sweep(plan_ref, 1, tiles, own_tiles, (96, 32), 1, add(0, half))

    @pl.when(more > 0)
    def _():
        sweep_extra(plan_ref, extra_ref, tiles, own_tiles, 8, 1, add(half, half))

    def field(k):
        return here_ref[pl.ds(k, own_tiles, stride=8), :]

    summed = jnp.sum(totals[:own_tiles, :8], axis=1)
    radius = field(4)
    density = KERNEL_NORM / (radius * radius * radius) * (4.0 * summed + field(5))
    dens_ref[...] = density
    press = GAMMA_LESS * field(6) / density
    press_ref[...] = press
    edge_ref[...] = press[:GT]


def accel_kernel(plan_ref, extra_ref, far, base_ref, half_b, dest_ref,
                 press_ref, press_far_ref, out_ref, near, left, left_half, totals, half_a):
    own_tiles = press_ref.shape[0]
    ghosts = dest_ref.shape[0]
    tiles = own_tiles + ghosts
    half = LANES // 2
    row = lax.broadcasted_iota(jnp.int32, (8, LANES), 0)
    spatial = (row >= 1) & (row <= 3)

    def loaded(part, press):
        twice = jnp.where(row < 4, part, pltpu.roll(part, 4, 0)) * part[5:6, :]
        one, two, low = three(jnp.where(row < 4, twice, twice * press))
        return jnp.concatenate([one, two], axis=0).astype(jnp.bfloat16)

    def own(t):
        part = tile_rows(base_ref, t)
        wanted = jnp.where(row == 0, part[7:8, :], jnp.where(spatial, -2.0 * part, jnp.where(
            row == 7, 1.0, 0.0)))
        half_a[pl.ds(t, 1), :] = 0.5 * part[4:5, :]
        near[t] = target_terms(wanted)
        rows = loaded(part, press_ref[pl.ds(t, 1), :])
        left[t] = jnp.concatenate([rows, rows], axis=1)

    in_groups(own_tiles, 8, own)

    def ghost(g):
        rows = loaded(tile_rows(base_ref, own_tiles + g), press_far_ref[pl.ds(g, 1), :])
        moved = by_last(rows, ones_where(equal_rows(dest_ref[pl.ds(g, 1), :], LANES)))
        moved = moved.astype(jnp.bfloat16)
        none = jnp.zeros((16, LANES), jnp.bfloat16)
        for v in range(2):
            piece = moved[:, v * half:(v + 1) * half]
            two = jnp.concatenate([piece, piece], axis=1)
            left_half[v, 0, g] = jnp.concatenate([two, none], axis=1)
            left_half[v, 1, g] = jnp.concatenate([none, two], axis=1)

    in_groups(ghosts, 8, ghost)
    totals[...] = jnp.zeros_like(totals)

    def slopes(source, target, first, height):
        sq = jnp.dot(far[source, first:first + height], near[target],
                     preferred_element_type=jnp.float32)
        radius = half_b[source, first:first + height] + half_a[pl.ds(target, 1), :]
        sq = jnp.maximum(sq, TINY)
        dist = sq * lax.rsqrt(sq)
        inv = pl.reciprocal(radius, approx=True)
        wide = inv * inv
        fall = jnp.maximum(inv - dist * wide, 0.0)
        slope = fall * fall * (fall * wide)
        high = slope.astype(jnp.bfloat16)
        low = (slope - high.astype(jnp.float32)).astype(jnp.bfloat16)
        return [high, low]

    def add_one(picked):
        (target, source, place, weight), = picked
        terms = jnp.concatenate(slopes(source, target, 0, LANES), axis=0)
        totals[place] += weight * jnp.dot(left[source], terms, preferred_element_type=jnp.float32)

    def add_two(v):
        def body(both):
            terms, lhs = [], []
            for side, (target, source, place, weight) in enumerate(both):
                terms += slopes(source, target, v * half, half)
                lhs.append(left_half[v, side, jnp.maximum(source - own_tiles, 0)])
            moved = jnp.dot(jnp.concatenate(lhs, axis=0), jnp.concatenate(terms, axis=0),
                            preferred_element_type=jnp.float32)
            for side, (target, source, place, weight) in enumerate(both):
                totals[place] += weight * moved[side * 16:(side + 1) * 16]
        return body

    sweep(plan_ref, 0, tiles, own_tiles, (64, 16), 1, add_one)
    sweep(plan_ref, 1, tiles, own_tiles, (64, 32), 2, add_two(0))

    @pl.when(extra_ref[0] > 0)
    def _():
        sweep_extra(plan_ref, extra_ref, tiles, own_tiles, 8, 2, add_two(1))

    for t in range(own_tiles):
        both = totals[t, :8] + totals[t, 8:]
        mixed = jnp.where(row < 4, both * press_ref[t:t + 1, :], both)
        mixed = mixed + pltpu.roll(mixed, 4, 0)
        pulled = 20.0 * KERNEL_NORM * (base_ref[t * 8:(t + 1) * 8, :] * mixed[0:1, :] - mixed)
        out_ref[:, t * LANES:(t + 1) * LANES] = pulled[1:4, :]


SMEM = pl.BlockSpec(memory_space=pltpu.SMEM)
VMEM = pl.BlockSpec(memory_space=pltpu.VMEM)
HBM = pl.BlockSpec(memory_space=pltpu.HBM)
GRANT = 24 * 2 ** 20
WHOLE = 60 * 2 ** 20


def exchange_call(count, pairs, positions, mass, smoothing, energy, destination, rows, cols):
    tiles = mass.shape[0]
    pool_tiles = tiles + 4 * GT
    lists = 2 * pl.cdiv(tiles * max(tiles, 4 * GT), LANES)
    domains = rows * cols
    slots = tiles * LANES // domains
    edge = GT * LANES // slots
    dma = pltpu.SemaphoreType.DMA
    given = (pairs, positions, mass, smoothing, energy, destination)
    return pl.pallas_call(
        functools.partial(exchange_kernel, rows=rows, cols=cols),
        out_shape=(
            jax.ShapeDtypeStruct((domains + 4 * edge, 8, slots), jnp.float32),
            jax.ShapeDtypeStruct((2 * lists + 2, LANES), jnp.int32),
        ),
        in_specs=[SMEM] + [HBM] * 6,
        out_specs=[HBM, HBM],
        scratch_shapes=[pltpu.VMEM(x.shape, x.dtype) for x in given] + [
            pltpu.VMEM((domains, 8, slots), jnp.float32),
            pltpu.VMEM((tiles * domains, LANES), jnp.bfloat16),
            pltpu.VMEM((tiles * domains, 2 * LANES), jnp.float32),
            pltpu.VMEM((tiles, LANES), jnp.int32),
            pltpu.VMEM((tiles * 8, LANES), jnp.float32),
            pltpu.VMEM((2, tiles, LANES), jnp.int32),
            pltpu.VMEM((tiles, pool_tiles), jnp.int32),
            pltpu.VMEM((tiles, pool_tiles), jnp.int32),
            pltpu.VMEM((2 * lists + 2, LANES), jnp.int32),
            pltpu.VMEM((edge, 8, slots), jnp.float32),
            dma((6,)), dma, dma, dma((domains,)), dma((domains,)), dma((4,)), dma((4,)),
        ],
        compiler_params=pltpu.CompilerParams(
            collective_id=0, has_side_effects=True, vmem_limit_bytes=WHOLE),
        name="exchange",
    )(count, *given)


def press_call(press, rows, cols):
    dma = pltpu.SemaphoreType.DMA
    return pl.pallas_call(
        functools.partial(press_kernel, rows=rows, cols=cols),
        out_shape=jax.ShapeDtypeStruct((4,) + press.shape, jnp.float32),
        in_specs=[VMEM],
        out_specs=VMEM,
        scratch_shapes=[dma((4,)), dma((4,))],
        compiler_params=pltpu.CompilerParams(collective_id=1, has_side_effects=True, vmem_limit_bytes=GRANT),
        name="press",
    )(press)


def density_call(plan, pool, own_tiles):
    tiles = pool.shape[0] // 8
    ghosts = tiles - own_tiles
    lists = (plan.shape[0] // LANES - 2) // 4
    flat = jax.ShapeDtypeStruct((own_tiles, LANES), jnp.float32)
    return pl.pallas_call(
        density_kernel,
        out_shape=(
            flat,
            flat,
            jax.ShapeDtypeStruct((GT, LANES), jnp.float32),
            jax.ShapeDtypeStruct((tiles, LANES, DEPTH), jnp.bfloat16),
            jax.ShapeDtypeStruct((tiles * 8, LANES), jnp.float32),
            jax.ShapeDtypeStruct((tiles, LANES, LANES), jnp.float32),
            jax.ShapeDtypeStruct((ghosts, LANES), jnp.int32),
            jax.ShapeDtypeStruct((lists * LANES + LANES,), jnp.int32),
        ),
        in_specs=[SMEM, VMEM],
        out_specs=(VMEM,) * 7 + (SMEM,),
        scratch_shapes=[
            pltpu.VMEM((own_tiles, DEPTH, LANES), jnp.bfloat16),
            pltpu.VMEM((tiles, LANES, LANES), jnp.float32),
            pltpu.VMEM((own_tiles + 1, max(8, ghosts), LANES), jnp.float32),
            pltpu.VMEM((ghosts, LANES), jnp.int32),
            pltpu.SMEM((ghosts, LANES), jnp.int32),
            pltpu.SemaphoreType.DMA,
        ],
        compiler_params=pltpu.CompilerParams(vmem_limit_bytes=GRANT),
        name="density",
    )(plan, pool)


def accel_call(plan, extra, far, base, half, dest, press, press_far):
    own_tiles, ghosts = press.shape[0], dest.shape[0]
    return pl.pallas_call(
        accel_kernel,
        out_shape=jax.ShapeDtypeStruct((3, own_tiles * LANES), jnp.float32),
        in_specs=[SMEM] * 2 + [VMEM] * 6,
        out_specs=VMEM,
        scratch_shapes=[
            pltpu.VMEM((own_tiles, DEPTH, LANES), jnp.bfloat16),
            pltpu.VMEM((own_tiles, 16, 2 * LANES), jnp.bfloat16),
            pltpu.VMEM((2, 2, ghosts, 16, 2 * LANES), jnp.bfloat16),
            pltpu.VMEM((own_tiles + 1, 16, LANES), jnp.float32),
            pltpu.VMEM((own_tiles, LANES), jnp.float32),
        ],
        compiler_params=pltpu.CompilerParams(vmem_limit_bytes=GRANT),
        name="accel",
    )(plan, extra, far, base, half, dest, press, press_far)


def as_tiles(blocks):
    count, fields, slots = blocks.shape
    per = LANES // slots
    joined = blocks.reshape(count // per, per, fields, slots).transpose(0, 2, 1, 3)
    return joined.reshape(count // per * fields, LANES)


def local(positions, mass, smoothing, energy, destination, pairs, pair_count):
    rows = lax.axis_size("gx")
    cols = lax.axis_size("gy")
    own_tiles = mass.shape[0] // LANES
    flat = (own_tiles, LANES)
    pool, plan = exchange_call(
        pair_count, pairs, positions, mass.reshape(flat), smoothing.reshape(flat),
        energy.reshape(flat), destination.reshape(flat), rows, cols)
    plan = plan.reshape(-1)
    density, press, edge, far, base, half, dest, extra = density_call(
        plan, as_tiles(pool), own_tiles)
    press_far = press_call(edge, rows, cols).reshape(4 * GT, LANES)
    accel = accel_call(plan, extra, far, base, half, dest, press, press_far)
    return (density.reshape(-1), accel)


def solution(mesh):
    placed = (
        P(None, ("gx", "gy")),
        P(("gx", "gy")),
        P(("gx", "gy")),
        P(("gx", "gy")),
        P(("gx", "gy"), None),
        P(None, ("gx", "gy")),
        P(("gx", "gy")),
    )
    return jax.shard_map(
        local,
        mesh=mesh,
        in_specs=placed,
        out_specs=(P(("gx", "gy")), P(None, ("gx", "gy"))),
        check_vma=False,
    )
```

```python
import functools
import math

import jax
import jax.numpy as jnp
from jax import lax
from jax.experimental import pallas as pl
from jax.experimental.pallas import tpu as pltpu
from jax.sharding import PartitionSpec as P

GT = 8
LANES = 128
DEPTH = 48
TINY = 1e-12
MESH = pl.DeviceIdType.MESH

KERNEL_NORM = 21.0 / (2.0 * math.pi)
GAMMA_LESS = 2.0 / 3.0


def three(x):
    one = x.astype(jnp.bfloat16).astype(jnp.float32)
    rest = x - one
    two = rest.astype(jnp.bfloat16).astype(jnp.float32)
    return one, two, (rest - two).astype(jnp.bfloat16).astype(jnp.float32)


def source_terms(x):
    one, two, low = three(x)
    return jnp.concatenate([one, two, one, two, low, one], axis=0).astype(jnp.bfloat16)


def target_terms(x):
    one, two, low = three(x)
    return jnp.concatenate([one, one, two, two, one, low], axis=0).astype(jnp.bfloat16)


def put_rows(stage, rows, width, tiles, first=0):
    for k, row in enumerate(rows):
        stage[pl.ds(first + k, tiles, stride=width), :] = row


def equal_rows(row, height, base=0):
    at = lax.broadcasted_iota(jnp.int32, (height, row.shape[-1]), 0) + base
    return jnp.broadcast_to(row, at.shape) == at


def ones_where(mask):
    return jnp.where(mask, 1.0, 0.0).astype(jnp.bfloat16)


def earlier(size, width):
    row = lax.broadcasted_iota(jnp.int32, (size, width), 0)
    col = lax.broadcasted_iota(jnp.int32, (size, width), 1)
    return row, col


def list_pairs(count_ref, pairs_ref, plan_ref, rank_ref, hits_ref, own_tiles, tiles):
    slots = pairs_ref.shape[1]
    live = lax.broadcasted_iota(jnp.int32, (1, slots), 1) < count_ref[0]
    target = jnp.where(live, pairs_ref[0:1, :], -1)
    hits = by_last(ones_where(equal_rows(target, own_tiles)),
                   ones_where(equal_rows(pairs_ref[1:2, :], tiles)))
    fresh = jnp.where(hits > 0.0, 1.0, 0.0)
    row, col = earlier(tiles, tiles)
    far_row, far_col = row >= own_tiles, col >= own_tiles
    inside = jnp.dot(fresh.astype(jnp.bfloat16), ones_where((row < col) & (far_row == far_col)),
                     preferred_element_type=jnp.float32)
    total = jnp.dot(fresh.astype(jnp.bfloat16), ones_where(far_row == far_col),
                    preferred_element_type=jnp.float32)
    row, col = earlier(own_tiles, own_tiles)
    above = jnp.dot(ones_where(col < row), total.astype(jnp.bfloat16),
                    preferred_element_type=jnp.float32)
    all_rows = jnp.sum(total, axis=0, keepdims=True).astype(jnp.int32)
    column = lax.broadcasted_iota(jnp.int32, (own_tiles, tiles), 1)
    place = jnp.where(hits > 0.0, (inside + above).astype(jnp.int32), -1)
    lists = (plan_ref.shape[0] - 2) // 4
    place = jnp.where((column >= own_tiles) & (place >= 0), place + lists * LANES, place)
    rank_ref[...] = place
    hits_ref[...] = hits.astype(jnp.int32)
    source = lax.broadcasted_iota(jnp.int32, (1, tiles), 1).astype(jnp.float32)
    keys = jnp.zeros((2 * lists, LANES), jnp.float32)
    times = jnp.zeros((2 * lists, LANES), jnp.float32)
    for t in range(own_tiles):
        at = rank_ref[t:t + 1, :]
        high = at // LANES
        many = hits_ref[t:t + 1, :]
        upper = many // LANES
        mine = jnp.where(equal_rows(jnp.where(at < 0, -1, high), 2 * lists), 1.0, 0.0)
        parts = [mine * source, mine, mine * upper.astype(jnp.float32),
                 mine * (many - upper * LANES).astype(jnp.float32)]
        found = by_last(jnp.concatenate(parts, axis=0).astype(jnp.bfloat16),
                        ones_where(equal_rows(jnp.where(at < 0, -1, at - high * LANES), LANES)))
        size = 2 * lists
        keys = keys + found[:size] + float(t * tiles) * found[size:2 * size]
        times = times + float(LANES) * found[2 * size:3 * size] + found[3 * size:]
    plan_ref[:2 * lists] = keys.astype(jnp.int32)
    plan_ref[2 * lists:4 * lists] = times.astype(jnp.int32)
    plan_ref[4 * lists:4 * lists + 1] = jnp.broadcast_to(all_rows[:, :1], (1, LANES))
    plan_ref[4 * lists + 1:] = jnp.broadcast_to(all_rows[:, tiles - 1:], (1, LANES))


def order_rows(pos_ref, mass_ref, smooth_ref, energy_ref, dest_ref, sent_ref,
               flags, prefix, rank_ref, rows_ref, index_ref):
    tiles = mass_ref.shape[0]
    domains, width, slots = sent_ref.shape
    row, col = earlier(LANES, 2 * LANES)
    before = ones_where((row < col) | (col >= LANES))
    for t in range(tiles):
        flags[t * domains:(t + 1) * domains] = ones_where(
            equal_rows(dest_ref[t:t + 1, :], domains))
    prefix[...] = jnp.dot(flags[...], before, preferred_element_type=jnp.float32)
    seen = jnp.zeros((domains, LANES), jnp.float32)
    for t in range(tiles):
        part = slice(t * domains, (t + 1) * domains)
        mine = flags[part].astype(jnp.float32)
        rank = jnp.sum(mine * (prefix[part, :LANES] + seen), axis=0, keepdims=True)
        rank_ref[t:t + 1, :] = rank.astype(jnp.int32)
        seen = seen + prefix[part, LANES:]
    place = dest_ref[...] * slots + rank_ref[...]
    block = place // LANES
    rank_ref[...] = place - block * LANES
    lane = lax.broadcasted_iota(jnp.int32, (tiles, LANES), 1).astype(jnp.float32)
    from_lane = jnp.zeros((tiles, LANES), jnp.float32)
    from_tile = jnp.zeros((tiles, LANES), jnp.float32)
    for t in range(tiles):
        picked = equal_rows(block[t:t + 1, :], tiles)
        both = jnp.concatenate([jnp.where(picked, lane, 0.0), jnp.where(picked, 1.0, 0.0)], axis=0)
        found = by_last(both.astype(jnp.bfloat16),
                        ones_where(equal_rows(rank_ref[t:t + 1, :], LANES)))
        from_lane = from_lane + found[:tiles]
        from_tile = from_tile + float(t) * found[tiles:]
    ones = jnp.ones((tiles, LANES), jnp.float32)
    put_rows(rows_ref, [smooth_ref[...], mass_ref[...], energy_ref[...], 0.0 * ones], width, tiles, 4)
    put_rows(rows_ref, [ones], width, tiles, 0)
    for t in range(tiles):
        rows_ref[t * width + 1:t * width + 4, :] = pos_ref[:, t * LANES:(t + 1) * LANES]
    index_ref[0] = from_lane.astype(jnp.int32)
    index_ref[1] = from_tile.astype(jnp.int32)
    per = LANES // slots

    def gather(q, carry):
        at = jnp.broadcast_to(index_ref[0, pl.ds(q, 1), :], (width, LANES))
        tile = jnp.broadcast_to(index_ref[1, pl.ds(q, 1), :], (width, LANES))
        out = jnp.zeros((width, LANES), jnp.float32)
        for t in range(tiles):
            moved = jnp.take_along_axis(rows_ref[t * width:(t + 1) * width, :], at, axis=1)
            out = jnp.where(tile == t, moved, out)
        for p in range(per):
            sent_ref[q * per + p] = out[:, p * slots:(p + 1) * slots]
        return carry

    lax.fori_loop(0, tiles, gather, 0)


def beside(i, j, rows, cols):
    return [(i > 0, (i - 1, j), 1), (i < rows - 1, (i + 1, j), 0),
            (j > 0, (i, j - 1), 3), (j < cols - 1, (i, j + 1), 2)]


def exchange_kernel(count_ref, *refs, rows, cols):
    given, refs = refs[:6], refs[6:]
    pool_ref, listed_ref = refs[:2]
    held, refs = refs[2:8], refs[8:]
    (out_ref, flags, prefix, rank_ref, rows_ref, index_ref, place_ref, hits_ref, plan_ref,
     blank, load_sem, plan_sem, stay_sem, send_sem, recv_sem, edge_send, edge_recv) = refs
    pairs_ref, pos_ref, mass_ref, smooth_ref, energy_ref, dest_ref = held
    loads = [pltpu.make_async_copy(a, b, load_sem.at[k]) for k, (a, b) in enumerate(zip(given, held))]
    for load in loads:
        load.start()
    domains = rows * cols
    tiles = mass_ref.shape[0]
    edge = (pool_ref.shape[0] - domains) // 4
    i, j = lax.axis_index("gx"), lax.axis_index("gy")
    me = i * cols + j
    barrier = pltpu.get_barrier_semaphore()

    def greet(k, carry):
        peer = lax.rem(me + k, domains)
        pl.semaphore_signal(barrier, inc=1, device_id=(peer // cols, lax.rem(peer, cols)),
                            device_id_type=MESH)
        return carry

    lax.fori_loop(1, domains, greet, 0, unroll=domains <= 32)
    for load in loads:
        load.wait()
    order_rows(pos_ref, mass_ref, smooth_ref, energy_ref, dest_ref, out_ref,
               flags, prefix, rank_ref, rows_ref, index_ref)
    pl.semaphore_wait(barrier, domains - 1)

    def outgoing(peer):
        return pltpu.make_async_remote_copy(
            src_ref=out_ref.at[peer], dst_ref=pool_ref.at[me],
            send_sem=send_sem.at[peer], recv_sem=recv_sem.at[me],
            device_id=(peer // cols, lax.rem(peer, cols)), device_id_type=MESH)

    def incoming(source):
        return pltpu.make_async_remote_copy(
            src_ref=out_ref.at[source], dst_ref=pool_ref.at[source],
            send_sem=send_sem.at[source], recv_sem=recv_sem.at[source],
            device_id=(source // cols, lax.rem(source, cols)), device_id_type=MESH)

    def send(k, carry):
        outgoing(lax.rem(me + k, domains)).start()
        return carry

    lax.fori_loop(1, domains, send, 0, unroll=domains <= 32)
    stay = pltpu.make_async_copy(out_ref.at[me], pool_ref.at[me], stay_sem)
    stay.start()
    blank[...] = jnp.zeros_like(blank)
    list_pairs(count_ref, pairs_ref, plan_ref, place_ref, hits_ref, tiles, tiles + 4 * GT)
    listed = pltpu.make_async_copy(plan_ref, listed_ref, plan_sem)
    listed.start()

    def arrive(source, carry):
        @pl.when(source != me)
        def _():
            incoming(source).wait_recv()
        return carry

    stay.wait()
    lax.fori_loop(0, edge, arrive, 0)
    sides = beside(i, j, rows, cols)

    def across(side):
        there, peer, slot = sides[side]
        return pltpu.make_async_remote_copy(
            src_ref=pool_ref.at[pl.ds(0, edge)], dst_ref=pool_ref.at[pl.ds(domains + slot * edge, edge)],
            send_sem=edge_send.at[side], recv_sem=edge_recv.at[slot],
            device_id=peer, device_id_type=MESH)

    def clear(side):
        return pltpu.make_async_copy(
            blank, pool_ref.at[pl.ds(domains + side * edge, edge)], edge_recv.at[side])

    def back(side):
        there, peer, slot = sides[side]
        return pltpu.make_async_remote_copy(
            src_ref=pool_ref.at[pl.ds(0, edge)], dst_ref=pool_ref.at[pl.ds(domains + side * edge, edge)],
            send_sem=edge_send.at[side], recv_sem=edge_recv.at[side],
            device_id=peer, device_id_type=MESH)

    for side in range(4):
        @pl.when(sides[side][0])
        def _():
            across(side).start()

        @pl.when(jnp.logical_not(sides[side][0]))
        def _():
            clear(side).start()

    lax.fori_loop(edge, domains, arrive, 0)

    def left(k, carry):
        outgoing(lax.rem(me + k, domains)).wait_send()
        return carry

    lax.fori_loop(1, domains, left, 0)
    for side in range(4):
        @pl.when(sides[side][0])
        def _():
            across(side).wait_send()
            back(side).wait_recv()

        @pl.when(jnp.logical_not(sides[side][0]))
        def _():
            clear(side).wait()

    listed.wait()


def press_kernel(press_ref, ghost_ref, send_sem, recv_sem, rows, cols):
    i, j = lax.axis_index("gx"), lax.axis_index("gy")
    sides = beside(i, j, rows, cols)
    barrier = pltpu.get_barrier_semaphore()
    for there, peer, slot in sides:
        @pl.when(there)
        def _():
            pl.semaphore_signal(barrier, inc=1, device_id=peer, device_id_type=MESH)

    pl.semaphore_wait(barrier, sum(there.astype(jnp.int32) for there, peer, slot in sides))

    def across(side, slot):
        return pltpu.make_async_remote_copy(
            src_ref=press_ref, dst_ref=ghost_ref.at[slot],
            send_sem=send_sem.at[side], recv_sem=recv_sem.at[slot],
            device_id=sides[side][1], device_id_type=MESH)

    for side in range(4):
        @pl.when(sides[side][0])
        def _():
            across(side, sides[side][2]).start()

        @pl.when(jnp.logical_not(sides[side][0]))
        def _():
            ghost_ref[side] = jnp.zeros_like(ghost_ref[side])

    for side in range(4):
        @pl.when(sides[side][0])
        def _():
            across(side, sides[side][2]).wait_send()
            across(side, side).wait_recv()


def one_hot_rows(dest):
    rows = lax.broadcasted_iota(jnp.int32, (LANES, LANES), 0)
    wide = jnp.broadcast_to(dest, (LANES, LANES))
    return jnp.where(wide == rows, 1.0, 0.0).astype(jnp.bfloat16)


def by_last(a, b):
    return lax.dot_general(a, b, (((1,), (1,)), ((), ())), preferred_element_type=jnp.float32)


def sweep(plan_ref, which, tiles, dump, unrolls, together, body):
    length = (plan_ref.shape[0] - 2 * LANES) // 4
    size = plan_ref[4 * length + which * LANES]

    done = 0
    for unroll in unrolls:
        final = unroll == unrolls[-1]

        def advance(block, carry):
            for u in range(0, unroll, together):
                picked = []
                for v in range(together):
                    k = done + block * unroll + u + v
                    if final:
                        live = k < size
                        at = which * length + jnp.minimum(k, length - 1)
                        key = jnp.where(live, plan_ref[at], 0)
                    else:
                        at = which * length + k
                        key = plan_ref[at]
                    target = lax.div(key, tiles)
                    source = key - target * tiles
                    weight = plan_ref[2 * length + at].astype(jnp.float32)
                    place = jnp.where(live, target, dump) if final else target
                    picked.append((target, source, place, weight))
                body(picked)
            return carry

        blocks = lax.div(size - done + (unroll - 1 if final else 0), unroll)
        lax.fori_loop(0, blocks, advance, 0)
        done = done + blocks * unroll


def sweep_extra(plan_ref, extra_ref, tiles, dump, unroll, together, body):
    length = (plan_ref.shape[0] - 2 * LANES) // 4
    size = extra_ref[0]

    def advance(block, carry):
        for u in range(0, unroll, together):
            picked = []
            for v in range(together):
                k = block * unroll + u + v
                live = k < size
                at = length + jnp.where(live, extra_ref[1 + jnp.minimum(k, length - 1)], 0)
                key = jnp.where(live, plan_ref[at], 0)
                target = lax.div(key, tiles)
                source = key - target * tiles
                weight = plan_ref[2 * length + at].astype(jnp.float32)
                picked.append((target, source, jnp.where(live, target, dump), weight))
            body(picked)
        return carry

    lax.fori_loop(0, lax.div(size + unroll - 1, unroll), advance, 0)


def list_extra(plan_ref, rank_ref, extra_ref, own_tiles, tiles, height):
    length = (plan_ref.shape[0] - 2 * LANES) // 4
    size = plan_ref[4 * length + LANES]

    def look(block, found):
        for u in range(8):
            k = jnp.minimum(block * 8 + u, length - 1)
            key = plan_ref[length + k]
            ghost = jnp.maximum(key - lax.div(key, tiles) * tiles - own_tiles, 0)
            long = (block * 8 + u < size) & (rank_ref[ghost, LANES - 1] > height)
            extra_ref[1 + found] = k
            found = found + long.astype(jnp.int32)
        return found

    extra_ref[0] = lax.fori_loop(0, lax.div(size + 7, 8), look, 0)


def in_groups(count, group, body):
    def step(block, carry):
        for u in range(group):
            body(block * group + u)
        return carry

    lax.fori_loop(0, count // group, step, 0)


def tile_rows(ref, t, height=8):
    return ref[pl.ds(pl.multiple_of(t * height, height), height), :]


def put_tile(ref, t, value):
    ref[pl.ds(pl.multiple_of(t * 8, 8), 8), :] = value


def spread_rows(far, wides, first, tiles, height):
    row = lax.broadcasted_iota(jnp.int32, (DEPTH, LANES), 0)
    picks = [jnp.where((row == k) | (row == 8 + k) | (row == 32 + k), scale, 0.0)
             for k, scale, wide in wides]
    picks = jnp.concatenate(picks, axis=1).astype(jnp.bfloat16)

    def one(t):
        spread = jnp.dot(far[first + t, :height], picks, preferred_element_type=jnp.float32)
        for n, (k, scale, wide) in enumerate(wides):
            wide[first + t, :height] = spread[:, n * LANES:(n + 1) * LANES]

    in_groups(tiles, 8, one)


def density_kernel(plan_ref, pool_ref,
                   dens_ref, press_ref, edge_ref, far, base_ref, half_b, dest_ref, extra_ref,
                   near, mass_b, totals, whole, scalar_rank, rank_sem):
    own_tiles = dens_ref.shape[0]
    ghosts = dest_ref.shape[0]
    here_ref = pool_ref.at[pl.ds(0, own_tiles * 8)]
    there_ref = pool_ref.at[pl.ds(own_tiles * 8, ghosts * 8)]
    tiles = own_tiles + ghosts
    row = lax.broadcasted_iota(jnp.int32, (8, LANES), 0)
    spatial = (row >= 1) & (row <= 3)
    first = here_ref[0:8, :]
    low, high, most = first, first, there_ref[0:8, :]
    for t in range(1, own_tiles):
        part = here_ref[t * 8:(t + 1) * 8, :]
        low, high = jnp.minimum(low, part), jnp.maximum(high, part)
    for g in range(1, ghosts):
        most = jnp.maximum(most, there_ref[g * 8:(g + 1) * 8, :])
    low = jnp.min(low, axis=1, keepdims=True)
    high = jnp.max(high, axis=1, keepdims=True)
    most = jnp.maximum(jnp.max(most, axis=1, keepdims=True), high)
    reach = most[4:5, :] + 0.01
    reach = reach * reach
    centre = jnp.where(spatial, 0.5 * (low + high), 0.0)

    def shifted(part):
        moved = part - centre
        norm = jnp.sum(jnp.where(spatial, moved * moved, 0.0), axis=0, keepdims=True)
        return jnp.where(row == 7, norm, moved), norm

    def own(t):
        moved, norm = shifted(tile_rows(here_ref, t))
        put_tile(base_ref, t, moved)
        far[t] = by_last(ones_where(equal_rows(same, LANES)),
                         source_terms(moved)).astype(jnp.bfloat16)
        radius = moved[4:5, :]
        wanted = jnp.where(row == 0, norm, jnp.where(spatial, -2.0 * moved, jnp.where(
            row == 7, 1.0, 0.0)))
        near[t] = target_terms(wanted * (1.0 / (radius * radius)))

    same = lax.broadcasted_iota(jnp.int32, (1, LANES), 1)
    in_groups(own_tiles, 8, own)

    def ghost(g):
        part = tile_rows(there_ref, g)
        gap = jnp.maximum(jnp.maximum(low - part, part - high), 0.0)
        beyond = jnp.sum(jnp.where(spatial, gap * gap, 0.0), axis=0, keepdims=True)
        active = (beyond < reach) & (part[5:6, :] != 0.0)
        totals[0, pl.ds(g, 1), :] = jnp.where(active, 1.0, 0.0)
        moved, norm = shifted(part)
        put_tile(base_ref, own_tiles + g, moved)

    in_groups(ghosts, 8, ghost)
    flags = totals[0, :ghosts, :]
    at, upto = earlier(LANES, LANES)
    rank = jnp.dot(flags.astype(jnp.bfloat16), ones_where(at <= upto),
                   preferred_element_type=jnp.float32)
    dest_ref[...] = jnp.where(flags > 0.0, rank - 1.0, -1.0).astype(jnp.int32)
    totals[0, :ghosts, :] = rank
    slot = lax.broadcasted_iota(jnp.int32, (LANES // 2, DEPTH), 0).astype(jnp.float32)
    term = lax.broadcasted_iota(jnp.int32, (LANES // 2, DEPTH), 1)
    unit = (term == 0) | (term == 16) | (term == 40)
    half = LANES // 2
    more = (jnp.max(rank) > half + 0.5).astype(jnp.int32)
    extra_ref[0] = 0

    @pl.when(more > 0)
    def _():
        whole[...] = rank.astype(jnp.int32)
        copy = pltpu.make_async_copy(whole, scalar_rank, rank_sem)
        copy.start()
        copy.wait()
        list_extra(plan_ref, scalar_rank, extra_ref, own_tiles, tiles, half)


    def squeeze(first):
        def body(g):
            moved = by_last(ones_where(equal_rows(dest_ref[pl.ds(g, 1), :], half, first)),
                            source_terms(tile_rows(base_ref, own_tiles + g)))
            unused = slot >= totals[0, pl.ds(g, 1), LANES - 1:] - float(first)
            far[own_tiles + g, first:first + half] = jnp.where(
                unit & unused, 1.0, moved).astype(jnp.bfloat16)
        return body

    in_groups(ghosts, 8, squeeze(0))

    @pl.when(more > 0)
    def _():
        in_groups(ghosts, 8, squeeze(half))

    wides = [(5, 1.0, mass_b), (4, 0.5, half_b)]
    spread_rows(far, wides, 0, own_tiles, LANES)
    spread_rows(far, wides, own_tiles, ghosts, half)

    @pl.when(more > 0)
    def _():
        spread_rows(far, wides, own_tiles, ghosts, LANES)

    totals[...] = jnp.zeros_like(totals)

    def add(first, height):
        def body(picked):
            (target, source, place, weight), = picked
            sq = jnp.dot(far[source, first:first + height], near[target],
                         preferred_element_type=jnp.float32)
            sq = jnp.maximum(sq, TINY)
            ratio = sq * lax.rsqrt(sq)
            falloff = jnp.maximum(1.0 - ratio, 0.0)
            falloff = falloff * falloff
            term = falloff * falloff * ((ratio + 0.25) * mass_b[source, first:first + height])
            summed = jnp.sum(term.reshape(height // 8, 8, LANES), axis=0)
            totals[place, :8] += weight * summed
        return body

    sweep(plan_ref, 0, tiles, own_tiles, (64, 16), 1, add(0, LANES))
    sweep(plan_ref, 1, tiles, own_tiles, (96, 32), 1, add(0, half))

    @pl.when(more > 0)
    def _():
        sweep_extra(plan_ref, extra_ref, tiles, own_tiles, 8, 1, add(half, half))

    def field(k):
        return here_ref[pl.ds(k, own_tiles, stride=8), :]

    summed = jnp.sum(totals[:own_tiles, :8], axis=1)
    radius = field(4)
    density = KERNEL_NORM / (radius * radius * radius) * (4.0 * summed + field(5))
    dens_ref[...] = density
    press = GAMMA_LESS * field(6) / density
    press_ref[...] = press
    edge_ref[...] = press[:GT]


def accel_kernel(plan_ref, extra_ref, far, base_ref, half_b, dest_ref,
                 press_ref, press_far_ref, out_ref, near, left, left_half, totals, half_a):
    own_tiles = press_ref.shape[0]
    ghosts = dest_ref.shape[0]
    tiles = own_tiles + ghosts
    half = LANES // 2
    row = lax.broadcasted_iota(jnp.int32, (8, LANES), 0)
    spatial = (row >= 1) & (row <= 3)

    def loaded(part, press):
        twice = jnp.where(row < 4, part, pltpu.roll(part, 4, 0)) * part[5:6, :]
        one, two, low = three(jnp.where(row < 4, twice, twice * press))
        return jnp.concatenate([one, two], axis=0).astype(jnp.bfloat16)

    def own(t):
        part = tile_rows(base_ref, t)
        wanted = jnp.where(row == 0, part[7:8, :], jnp.where(spatial, -2.0 * part, jnp.where(
            row == 7, 1.0, 0.0)))
        half_a[pl.ds(t, 1), :] = 0.5 * part[4:5, :]
        near[t] = target_terms(wanted)
        rows = loaded(part, press_ref[pl.ds(t, 1), :])
        left[t] = jnp.concatenate([rows, rows], axis=1)

    in_groups(own_tiles, 8, own)

    def ghost(g):
        rows = loaded(tile_rows(base_ref, own_tiles + g), press_far_ref[pl.ds(g, 1), :])
        moved = by_last(rows, ones_where(equal_rows(dest_ref[pl.ds(g, 1), :], LANES)))
        moved = moved.astype(jnp.bfloat16)
        none = jnp.zeros((16, LANES), jnp.bfloat16)
        for v in range(2):
            piece = moved[:, v * half:(v + 1) * half]
            two = jnp.concatenate([piece, piece], axis=1)
            left_half[v, 0, g] = jnp.concatenate([two, none], axis=1)
            left_half[v, 1, g] = jnp.concatenate([none, two], axis=1)

    in_groups(ghosts, 8, ghost)
    totals[...] = jnp.zeros_like(totals)

    def slopes(source, target, first, height):
        sq = jnp.dot(far[source, first:first + height], near[target],
                     preferred_element_type=jnp.float32)
        radius = half_b[source, first:first + height] + half_a[pl.ds(target, 1), :]
        sq = jnp.maximum(sq, TINY)
        dist = sq * lax.rsqrt(sq)
        inv = pl.reciprocal(radius, approx=True)
        wide = inv * inv
        fall = jnp.maximum(inv - dist * wide, 0.0)
        slope = fall * fall * (fall * wide)
        high = slope.astype(jnp.bfloat16)
        low = (slope - high.astype(jnp.float32)).astype(jnp.bfloat16)
        return [high, low]

    def add_one(picked):
        (target, source, place, weight), = picked
        terms = jnp.concatenate(slopes(source, target, 0, LANES), axis=0)
        totals[place] += weight * jnp.dot(left[source], terms, preferred_element_type=jnp.float32)

    def add_two(v):
        def body(both):
            terms, lhs = [], []
            for side, (target, source, place, weight) in enumerate(both):
                terms += slopes(source, target, v * half, half)
                lhs.append(left_half[v, side, jnp.maximum(source - own_tiles, 0)])
            moved = jnp.dot(jnp.concatenate(lhs, axis=0), jnp.concatenate(terms, axis=0),
                            preferred_element_type=jnp.float32)
            for side, (target, source, place, weight) in enumerate(both):
                totals[place] += weight * moved[side * 16:(side + 1) * 16]
        return body

    sweep(plan_ref, 0, tiles, own_tiles, (64, 16), 1, add_one)
    sweep(plan_ref, 1, tiles, own_tiles, (64, 32), 2, add_two(0))

    @pl.when(extra_ref[0] > 0)
    def _():
        sweep_extra(plan_ref, extra_ref, tiles, own_tiles, 8, 2, add_two(1))

    for t in range(own_tiles):
        both = totals[t, :8] + totals[t, 8:]
        mixed = jnp.where(row < 4, both * press_ref[t:t + 1, :], both)
        mixed = mixed + pltpu.roll(mixed, 4, 0)
        pulled = 20.0 * KERNEL_NORM * (base_ref[t * 8:(t + 1) * 8, :] * mixed[0:1, :] - mixed)
        out_ref[:, t * LANES:(t + 1) * LANES] = pulled[1:4, :]


SMEM = pl.BlockSpec(memory_space=pltpu.SMEM)
VMEM = pl.BlockSpec(memory_space=pltpu.VMEM)
HBM = pl.BlockSpec(memory_space=pltpu.HBM)
GRANT = 24 * 2 ** 20
WHOLE = 60 * 2 ** 20


def exchange_call(count, pairs, positions, mass, smoothing, energy, destination, rows, cols):
    tiles = mass.shape[0]
    pool_tiles = tiles + 4 * GT
    lists = 2 * pl.cdiv(tiles * max(tiles, 4 * GT), LANES)
    domains = rows * cols
    slots = tiles * LANES // domains
    edge = GT * LANES // slots
    dma = pltpu.SemaphoreType.DMA
    given = (pairs, positions, mass, smoothing, energy, destination)
    return pl.pallas_call(
        functools.partial(exchange_kernel, rows=rows, cols=cols),
        out_shape=(
            jax.ShapeDtypeStruct((domains + 4 * edge, 8, slots), jnp.float32),
            jax.ShapeDtypeStruct((2 * lists + 2, LANES), jnp.int32),
        ),
        in_specs=[SMEM] + [HBM] * 6,
        out_specs=[HBM, HBM],
        scratch_shapes=[pltpu.VMEM(x.shape, x.dtype) for x in given] + [
            pltpu.VMEM((domains, 8, slots), jnp.float32),
            pltpu.VMEM((tiles * domains, LANES), jnp.bfloat16),
            pltpu.VMEM((tiles * domains, 2 * LANES), jnp.float32),
            pltpu.VMEM((tiles, LANES), jnp.int32),
            pltpu.VMEM((tiles * 8, LANES), jnp.float32),
            pltpu.VMEM((2, tiles, LANES), jnp.int32),
            pltpu.VMEM((tiles, pool_tiles), jnp.int32),
            pltpu.VMEM((tiles, pool_tiles), jnp.int32),
            pltpu.VMEM((2 * lists + 2, LANES), jnp.int32),
            pltpu.VMEM((edge, 8, slots), jnp.float32),
            dma((6,)), dma, dma, dma((domains,)), dma((domains,)), dma((4,)), dma((4,)),
        ],
        compiler_params=pltpu.CompilerParams(
            collective_id=0, has_side_effects=True, vmem_limit_bytes=WHOLE),
        name="exchange",
    )(count, *given)


def press_call(press, rows, cols):
    dma = pltpu.SemaphoreType.DMA
    return pl.pallas_call(
        functools.partial(press_kernel, rows=rows, cols=cols),
        out_shape=jax.ShapeDtypeStruct((4,) + press.shape, jnp.float32),
        in_specs=[VMEM],
        out_specs=VMEM,
        scratch_shapes=[dma((4,)), dma((4,))],
        compiler_params=pltpu.CompilerParams(collective_id=1, has_side_effects=True, vmem_limit_bytes=GRANT),
        name="press",
    )(press)


def density_call(plan, pool, own_tiles):
    tiles = pool.shape[0] // 8
    ghosts = tiles - own_tiles
    lists = (plan.shape[0] // LANES - 2) // 4
    flat = jax.ShapeDtypeStruct((own_tiles, LANES), jnp.float32)
    return pl.pallas_call(
        density_kernel,
        out_shape=(
            flat,
            flat,
            jax.ShapeDtypeStruct((GT, LANES), jnp.float32),
            jax.ShapeDtypeStruct((tiles, LANES, DEPTH), jnp.bfloat16),
            jax.ShapeDtypeStruct((tiles * 8, LANES), jnp.float32),
            jax.ShapeDtypeStruct((tiles, LANES, LANES), jnp.float32),
            jax.ShapeDtypeStruct((ghosts, LANES), jnp.int32),
            jax.ShapeDtypeStruct((lists * LANES + LANES,), jnp.int32),
        ),
        in_specs=[SMEM, VMEM],
        out_specs=(VMEM,) * 7 + (SMEM,),
        scratch_shapes=[
            pltpu.VMEM((own_tiles, DEPTH, LANES), jnp.bfloat16),
            pltpu.VMEM((tiles, LANES, LANES), jnp.float32),
            pltpu.VMEM((own_tiles + 1, max(8, ghosts), LANES), jnp.float32),
            pltpu.VMEM((ghosts, LANES), jnp.int32),
            pltpu.SMEM((ghosts, LANES), jnp.int32),
            pltpu.SemaphoreType.DMA,
        ],
        compiler_params=pltpu.CompilerParams(vmem_limit_bytes=GRANT),
        name="density",
    )(plan, pool)


def accel_call(plan, extra, far, base, half, dest, press, press_far):
    own_tiles, ghosts = press.shape[0], dest.shape[0]
    return pl.pallas_call(
        accel_kernel,
        out_shape=jax.ShapeDtypeStruct((3, own_tiles * LANES), jnp.float32),
        in_specs=[SMEM] * 2 + [VMEM] * 6,
        out_specs=VMEM,
        scratch_shapes=[
            pltpu.VMEM((own_tiles, DEPTH, LANES), jnp.bfloat16),
            pltpu.VMEM((own_tiles, 16, 2 * LANES), jnp.bfloat16),
            pltpu.VMEM((2, 2, ghosts, 16, 2 * LANES), jnp.bfloat16),
            pltpu.VMEM((own_tiles + 1, 16, LANES), jnp.float32),
            pltpu.VMEM((own_tiles, LANES), jnp.float32),
        ],
        compiler_params=pltpu.CompilerParams(vmem_limit_bytes=GRANT),
        name="accel",
    )(plan, extra, far, base, half, dest, press, press_far)


def as_tiles(blocks):
    count, fields, slots = blocks.shape
    per = LANES // slots
    joined = blocks.reshape(count // per, per, fields, slots).transpose(0, 2, 1, 3)
    return joined.reshape(count // per * fields, LANES)


def local(positions, mass, smoothing, energy, destination, pairs, pair_count):
    rows = lax.axis_size("gx")
    cols = lax.axis_size("gy")
    own_tiles = mass.shape[0] // LANES
    flat = (own_tiles, LANES)
    pool, plan = exchange_call(
        pair_count, pairs, positions, mass.reshape(flat), smoothing.reshape(flat),
        energy.reshape(flat), destination.reshape(flat), rows, cols)
    plan = plan.reshape(-1)
    density, press, edge, far, base, half, dest, extra = density_call(
        plan, as_tiles(pool), own_tiles)
    press_far = press_call(edge, rows, cols).reshape(4 * GT, LANES)
    accel = accel_call(plan, extra, far, base, half, dest, press, press_far)
    return (density.reshape(-1), accel)


def solution(mesh):
    placed = (
        P(None, ("gx", "gy")),
        P(("gx", "gy")),
        P(("gx", "gy")),
        P(("gx", "gy")),
        P(("gx", "gy"), None),
        P(None, ("gx", "gy")),
        P(("gx", "gy")),
    )
    return jax.shard_map(
        local,
        mesh=mesh,
        in_specs=placed,
        out_specs=(P(("gx", "gy")), P(None, ("gx", "gy"))),
        check_vma=False,
    )
```
